128 devices in a mesh: slab: 32 (over y, x, core), mp: 4 (over z).
Axes of the slice: x: 4, y: 4, z: 4, core: 2. Of those that a mesh axis runs over, the one named last changes fastest.
Arguments:
- velocity: float32 [3, 256, 512, 256], P(None, 'slab', 'mp'), may hold values from -6 to 6
- anchors: int32 [3, 32, 4, 256], P(None, 'slab', 'mp'), may hold values from 0 to 504, as said below
- dest: int32 [32, 4, 256, 1], P('slab', 'mp'), may hold values from 0 to 31; in each aligned block of 256 rows (0 to 255, 256 to 511, ..., all dimensions but the last counted through in order) at most 16 rows name the same one
- w_lift: bfloat16 [1536, 512], replicated, may hold values from -0.15625 to 0.15625
- w_query: bfloat16 [512, 512], P(None, 'mp'), may hold values from -0.25 to 0.25
- w_key: bfloat16 [512, 512], P(None, 'mp'), may hold values from -0.25 to 0.25
- w_value: bfloat16 [512, 512], P(None, 'mp'), may hold values from -0.25 to 0.25
- w_out: bfloat16 [512, 512], P('mp'), may hold values from -0.25 to 0.25
- w_proj: bfloat16 [512, 1536], replicated, may hold values from -0.25 to 0.25
Outputs:
- new_velocity: float32 [3, 256, 512, 256], P(None, 'slab', 'mp')
- loss: float32 [], replicated
- g_lift: float32 [1536, 512], P('slab')
- g_query: float32 [512, 512], P(None, 'mp')
- g_key: float32 [512, 512], P(None, 'mp')
- g_value: float32 [512, 512], P(None, 'mp')
- g_out: float32 [512, 512], P('mp')
- g_proj: float32 [512, 1536], P('slab')
The draws below stay inside these ranges and needn't reach their ends.
Inputs may be any that keep to these rules, and one draw needn't show every extreme that they name: Each device's 256 anchors are distinct, multiples of 8 in each coordinate (z, y, x along the first dimension), and name patches inside that device's own block of the grid. `dest`: among the 256 rows of one device no trainer shard is named more than 16 times, and in some device's rows some shard is named exactly 16 times; every shard is named by some row.
All inputs are finite; a program needn't handle non-finite values.
Results may differ from the reference program's by a relative error of at most 0.0035.
Values may be sent and summed in bfloat16 or wider, within the bound.
No kernel may reach another device: no remote copies, remote signals or barrier semaphores. Data moves between devices by JAX's collectives and lax.ppermute only.
A program may use at most 192 MiB of HBM per device.

```python
import math
import jax
import jax.numpy as jnp
import numpy as np
from jax import lax

D = 512
HEADS = 8
HEAD_DIM = 64
FEAT = 1536
NX = 256
CY = 128
CZ = 8
PICKS = 256
CAP = 16
NZ = 256
NY = 512
N_SLAB = 32
N_MP = 4


def draw_anchors(key, part):
    per_device = CZ // 8 * (CY // 8) * (NX // 8)
    key_list = jax.random.split(key, N_SLAB * N_MP)

    def choose(device_key):
        return jax.random.permutation(device_key, per_device)[:PICKS]
    chosen = jax.vmap(choose)(key_list).reshape(N_SLAB, N_MP, PICKS).astype(jnp.int32)
    cells_x = NX // 8
    cells_y = CY // 8
    local_x = chosen % cells_x
    local_y = chosen // cells_x % cells_y
    local_z = chosen // (cells_x * cells_y)
    slab_at = jnp.arange(N_SLAB, dtype=jnp.int32)[:, None, None]
    column_at = jnp.arange(N_MP, dtype=jnp.int32)[None, :, None]
    return jnp.stack([slab_at * CZ + 8 * local_z, column_at * CY + 8 * local_y, 8 * local_x]).astype(jnp.int32)


def block_scale(key, dims, pieces, least, top_value):
    gain, own = 1.0, jax.random.fold_in(key, 6)
    for axis_at, shards_of in pieces:
        steps = jnp.exp(jax.random.uniform(jax.random.fold_in(own, axis_at), (shards_of,), jnp.float32, least / len(pieces), top_value / len(pieces)))
        gain = gain * jnp.repeat(steps, dims[axis_at] // shards_of).reshape([-1 if axis == axis_at else 1 for axis in range(len(dims))])
    return gain


def assign_block(key, own, number, rows, number_of, top, most, skew):
    sequence = jax.random.permutation(key, number_of)
    heavy_load, common = load_shares(number_of, rows * top, most, skew, True), load_shares(number_of, rows * top, most, skew, False)
    places = jnp.arange(number_of)

    def named(tallies, offset_by):
        used = int((tallies > 0).sum())
        fixed = max(1, used // 4)
        moved = fixed + (places - fixed + offset_by * (used - fixed)) % max(1, number_of - fixed)
        return jnp.zeros((number_of,), jnp.int32).at[sequence[jnp.where(places < fixed, places, moved)]].set(jnp.asarray(tallies, jnp.int32))

    tallies = jnp.where(number % 4 == 0, named(heavy_load, number // 4), named(common, number - number // 4 - 1))
    mixed = jax.random.permutation(jax.random.fold_in(own, 3), number_of)
    donor, receiver = mixed[0:number_of // 2 * 2:2], mixed[1:number_of // 2 * 2:2]
    room = jnp.minimum(tallies[donor] - 1, most - tallies[receiver]) // 2
    room = jnp.where((donor == sequence[0]) | (receiver == sequence[0]) | (tallies[receiver] == 0), 0, jnp.maximum(room, 0))
    moved = jax.random.randint(jax.random.fold_in(own, 4), (number_of // 2,), 0, 1 << 20) % (room + 1)
    tallies = tallies.at[donor].add(-moved).at[receiver].add(moved)
    members = jnp.searchsorted(jnp.cumsum(tallies), jnp.arange(rows * top), side="right").astype(jnp.int32)
    listing = members.reshape(top, rows).T
    listing = listing[jax.random.permutation(jax.random.fold_in(own, 1), rows)]
    offset_by = jax.random.randint(jax.random.fold_in(own, 2), (rows, 1), 0, top)
    return jnp.take_along_axis(listing, (jnp.arange(top)[None, :] + offset_by) % top, axis=1)


def load_shares(number_of, total, bound, slope, full):
    weights = [(1 << 20) // math.isqrt(grade ** slope) + 1 for grade in range(1, number_of + 1)]
    largest = bound if full else min(bound, max(-(-total // number_of), total * weights[0] // sum(weights)))
    least = 1 if total - largest >= number_of - 1 else 0
    given, spare = [largest] + [least] * (number_of - 1), total - largest - least * (number_of - 1)
    while spare > 0:
        candidates = [i for i in range(1, number_of) if given[i] < largest] or [i for i in range(1, number_of) if given[i] < bound]
        whole, budget = sum([weights[i] for i in candidates]), spare
        for i in candidates:
            extra = min(bound - given[i], max(1, budget * weights[i] // whole), spare)
            given[i] = given[i] + extra
            spare = spare - extra
    return np.array(given)


def scatter_about(rng, dims, scale, most, pieces=(), held_as=jnp.bfloat16):
    entries = jax.random.normal(rng, dims, jnp.float32) * scale
    if len(pieces) > 0:
        entries = block_scale(rng, dims, pieces, -0.22, 0.18) * entries
    return jnp.clip(entries, min=-most, max=most).astype(held_as)


def setup_inputs(seed: int = 0) -> dict:
    seeds = jax.random.split(jax.random.key(seed), 10)
    velocity = scatter_about(seeds[0], (3, NZ, NY, NX), 1.0, 6.0, ((1, 32), (2, 4)), jnp.float32)
    anchors = draw_anchors(jax.random.fold_in(seeds[9], 71), 0)
    dest_keys = jax.random.split(jax.random.fold_in(seeds[2], 1), N_SLAB * N_MP * PICKS // PICKS)
    dest_turns = jax.random.permutation(jax.random.fold_in(seeds[2], 3), N_SLAB * N_MP * PICKS // PICKS)
    dest = jax.vmap(lambda own, number: assign_block(jax.random.fold_in(seeds[2], 2), own, number, PICKS, N_SLAB, 1, CAP, 2))(dest_keys, dest_turns).reshape((N_SLAB, N_MP, PICKS, 1))
    w_lift = scatter_about(seeds[3], (FEAT, D), FEAT ** -0.5, 0.15625)
    w_query = scatter_about(seeds[4], (D, D), D ** -0.5, 0.25, ((1, 4),))
    w_key = scatter_about(seeds[5], (D, D), D ** -0.5, 0.25, ((1, 4),))
    w_value = scatter_about(seeds[6], (D, D), D ** -0.5, 0.25, ((1, 4),))
    w_out = scatter_about(seeds[7], (D, D), D ** -0.5, 0.25, ((0, 4),))
    w_proj = scatter_about(seeds[8], (D, FEAT), D ** -0.5, 0.25)
    return {"velocity": velocity, "anchors": anchors, "dest": dest, "w_lift": w_lift, "w_query": w_query, "w_key": w_key, "w_value": w_value, "w_out": w_out, "w_proj": w_proj}


TIME_STEP = 0.1
VISCOSITY = 0.2
EPSILON = 1e-05
EXACT = lax.Precision.HIGHEST

def update(centre, z_next, z_prev, y_next, y_prev, x_next, x_prev):
    laplace = z_next + z_prev + y_next + y_prev + x_next + x_prev - 6.0 * centre
    transport = centre[0:1] * (0.5 * (x_next - x_prev)) + centre[1:2] * (0.5 * (y_next - y_prev)) + centre[2:3] * (0.5 * (z_next - z_prev))
    return centre - TIME_STEP * transport + VISCOSITY * TIME_STEP * laplace

def advance(velocity):
    return update(velocity, jnp.roll(velocity, -1, 1), jnp.roll(velocity, 1, 1), jnp.roll(velocity, -1, 2), jnp.roll(velocity, 1, 2), jnp.roll(velocity, -1, 3), jnp.roll(velocity, 1, 3))

def cut_patches(field):
    comps, size_z, size_y, size_x = field.shape
    blocks = field.reshape(comps, size_z // 8, 8, size_y // 8, 8, size_x // 8, 8)
    return blocks.transpose(1, 3, 5, 0, 2, 4, 6).reshape(-1, comps * 512)

def rounded(values):
    return lax.optimization_barrier(values.astype(jnp.bfloat16)).astype(jnp.float32)

def normalize(heads):
    centre = lax.optimization_barrier(jnp.mean(heads, axis=-1, keepdims=True))
    shifted = heads - centre
    spread = jnp.sqrt(lax.optimization_barrier(jnp.mean(shifted * shifted, axis=-1, keepdims=True)) + EPSILON)
    return (shifted / spread, spread)

def norm_back(grad, normed, spread):
    inner = lax.optimization_barrier(jnp.mean(grad, axis=-1, keepdims=True))
    cross = lax.optimization_barrier(jnp.mean(grad * normed, axis=-1, keepdims=True))
    return (grad - inner - normed * cross) / spread

def reference(velocity, anchors, dest, w_lift, w_query, w_key, w_value, w_out, w_proj):
    new_velocity = advance(velocity)
    flat = anchors.reshape(3, -1)
    index = ((flat[0] // 8 * (NY // 8) + flat[1] // 8) * (NX // 8) + flat[2] // 8).astype(jnp.int32)
    old = cut_patches(velocity.astype(jnp.bfloat16))[index]
    new = cut_patches(new_velocity.astype(jnp.bfloat16))[index]
    member = dest.reshape(-1).astype(jnp.int32)
    token_total = old.shape[0]
    counts = jax.ops.segment_sum(jnp.ones((token_total,), jnp.float32), member, num_segments=N_SLAB)

    def group_sum(left, right):

        def one_head(pair):
            return jax.ops.segment_sum(pair[0][:, :, None] * pair[1][:, None, :], member, num_segments=N_SLAB)
        return lax.map(one_head, (left.transpose(1, 0, 2), right.transpose(1, 0, 2))).transpose(1, 0, 2, 3)

    def apply_rows(left, table):

        def one_head(pair):
            return jnp.einsum('ti,tij->tj', pair[0], pair[1][member], precision=EXACT)
        return lax.map(one_head, (left.transpose(1, 0, 2), table.transpose(1, 0, 2, 3))).transpose(1, 0, 2)
    shape = (token_total, HEADS, HEAD_DIM)
    lifted = jnp.dot(old, w_lift, preferred_element_type=jnp.float32).astype(jnp.bfloat16)
    queries = rounded(jnp.dot(lifted, w_query, preferred_element_type=jnp.float32).reshape(shape))
    keys_hat, key_spread = normalize(jnp.dot(lifted, w_key, preferred_element_type=jnp.float32).reshape(shape))
    values_hat, value_spread = normalize(jnp.dot(lifted, w_value, preferred_element_type=jnp.float32).reshape(shape))
    keys_round = rounded(keys_hat)
    values_round = rounded(values_hat)
    summary = group_sum(keys_round, values_round) / counts[:, None, None, None]
    attended = apply_rows(queries, summary).astype(jnp.bfloat16).reshape(token_total, D)
    hidden = (lifted.astype(jnp.float32) + jnp.dot(attended, w_out, preferred_element_type=jnp.float32)).astype(jnp.bfloat16)
    guess = jnp.dot(hidden, w_proj, preferred_element_type=jnp.float32)
    error = guess - new.astype(jnp.float32)
    loss = jnp.sum(error * error) / (token_total * FEAT)
    d_guess = (error / token_total).astype(jnp.bfloat16)
    g_proj = jnp.dot(hidden.T, d_guess, preferred_element_type=jnp.float32)
    d_hidden = jnp.dot(d_guess, w_proj.T, preferred_element_type=jnp.float32)
    d_tokens = d_hidden.astype(jnp.bfloat16)
    g_out = jnp.dot(attended.T, d_tokens, preferred_element_type=jnp.float32)
    d_attended = jnp.dot(d_tokens, w_out.T, preferred_element_type=jnp.float32).reshape(shape)
    d_query = apply_rows(d_attended, summary.swapaxes(2, 3)).astype(jnp.bfloat16).reshape(token_total, D)
    d_summary = group_sum(queries, d_attended) / counts[:, None, None, None]
    d_keys = norm_back(apply_rows(values_round, d_summary.swapaxes(2, 3)), keys_hat, key_spread).astype(jnp.bfloat16).reshape(token_total, D)
    d_values = norm_back(apply_rows(keys_round, d_summary), values_hat, value_spread).astype(jnp.bfloat16).reshape(token_total, D)
    g_query = jnp.dot(lifted.T, d_query, preferred_element_type=jnp.float32)
    g_key = jnp.dot(lifted.T, d_keys, preferred_element_type=jnp.float32)
    g_value = jnp.dot(lifted.T, d_values, preferred_element_type=jnp.float32)
    d_lifted = d_hidden + jnp.dot(d_query, w_query.T, preferred_element_type=jnp.float32)
    d_lifted = d_lifted + jnp.dot(d_keys, w_key.T, preferred_element_type=jnp.float32)
    d_lifted = (d_lifted + jnp.dot(d_values, w_value.T, preferred_element_type=jnp.float32)).astype(jnp.bfloat16)
    g_lift = jnp.dot(old.T, d_lifted, preferred_element_type=jnp.float32)
    return (new_velocity, loss, g_lift, g_query, g_key, g_value, g_out, g_proj)
```

```python
import jax
import jax.numpy as jnp
from jax import lax
from jax.experimental import pallas as pl
from jax.experimental.pallas import tpu as pltpu
from jax.sharding import PartitionSpec as P

TIME_STEP = 0.1
VISCOSITY = 0.2
EPSILON = 1e-05
F32 = jnp.float32
BF16 = jnp.bfloat16
CHUNK = 128


def iota(shape, dim):
    return lax.broadcasted_iota(jnp.int32, shape, dim)


def dot(a, b, contract=(1, 0)):
    dims = (((contract[0],), (contract[1],)), ((), ()))
    return lax.dot_general(a, b, dims, preferred_element_type=F32)


def split(a):
    high = a.astype(BF16)
    return high, (a - high.astype(F32)).astype(BF16)


def head_mean(a, mix):
    high, low = split(a)
    halves = [
        dot(high[:, at : at + 256], mix) + dot(low[:, at : at + 256], mix) for at in (0, 256)
    ]
    return jnp.concatenate(halves, axis=1)


def mean_matrix():
    same = iota((256, 256), 0) // 64 == iota((256, 256), 1) // 64
    return jnp.where(same, 1.0 / 64, 0.0).astype(BF16)


def cut_patches(load, pick_ref, out_ref, whole_ref, rest_ref, once_ref, pair_ref, turn_ref):
    row, col = iota((256, 256), 0), iota((256, 256), 1)
    turn_ref[...] = jnp.where(col == (row & 31) * 8 + (row >> 5), 1.0, 0.0).astype(BF16)
    row, col = iota((128, 256), 0), iota((128, 256), 1)
    turn_pair = jnp.where(col == (row & 31) * 8 + 2 * (row >> 5), 1.0, 0.0).astype(BF16)

    def strip(by, carry):
        cells = load(by)
        first = cells[:128].astype(BF16)
        last = cells[128:]
        last = jnp.concatenate([last, pltpu.roll(last, 255, 1)], axis=0).astype(BF16)
        at = pl.ds(pl.multiple_of(by * 32, 32), 32)
        turned = dot(turn_ref[...], first, (1, 1)).astype(BF16)
        for x in range(8):
            whole_ref[at, x * 128 : (x + 1) * 128] = turned[x * 32 : (x + 1) * 32]
        turned = dot(turn_pair, last, (1, 1)).astype(BF16)
        for x in range(4):
            rest_ref[at, x * 128 : (x + 1) * 128] = turned[x * 32 : (x + 1) * 32]
        return carry

    lax.fori_loop(0, 16, strip, 0)

    def spread(i, carry):
        at = pl.ds(pl.multiple_of(i * 128, 128), 128)
        row, col = iota((128, 1024), 0), iota((128, 1024), 1)
        once_ref[at, :] = jnp.where(col == 8 * row + i, 1.0, 0.0).astype(BF16)
        return carry

    lax.fori_loop(0, 8, spread, 0)
    row, col = iota((512, 512), 0), iota((512, 512), 1)
    pair_ref[...] = jnp.where(col == 8 * (row & 63) + (row >> 6), 1.0, 0.0).astype(BF16)

    def place(i, carry):
        at = pl.ds(pl.multiple_of(i * CHUNK, CHUNK), CHUNK)
        pick = pick_ref[at, :]
        picked = dot(pick, whole_ref[...]).astype(BF16)
        out_ref[at, 0:1024] = dot(picked, once_ref[...]).astype(BF16)
        picked = dot(pick, rest_ref[...]).astype(BF16)
        out_ref[at, 1024:1536] = dot(picked, pair_ref[...]).astype(BF16)
        return carry

    lax.fori_loop(0, 512 // CHUNK, place, 0)


CUT_SCRATCH = [
    pltpu.VMEM((512, 1024), BF16),
    pltpu.VMEM((512, 512), BF16),
    pltpu.VMEM((1024, 1024), BF16),
    pltpu.VMEM((512, 512), BF16),
    pltpu.VMEM((256, 256), BF16),
]


def old_kernel(field_ref, anchor_ref, dest_ref, out_ref, pick_ref, *scratch):
    target = dest_ref[...].astype(F32)
    wide = jnp.broadcast_to(target, (256, 256))
    row, col = iota((256, 256), 0), iota((256, 256), 1)
    tall = jnp.sum(jnp.where(row == col, wide, 0.0), axis=1, keepdims=True)
    ahead = jnp.where((tall == wide) & (row < col), 1.0, 0.0)
    slot = target * 16.0 + jnp.sum(ahead, axis=0, keepdims=True)
    patch = ((anchor_ref[1:2, :] >> 3) & 15) * 32 + ((anchor_ref[2:3, :] >> 3) & 31)
    row = iota((512, 256), 0)
    sent = jnp.where(row == slot.astype(jnp.int32), 1.0, 0.0)
    taken = jnp.where(row == patch, 1.0, 0.0).astype(BF16)
    pick_ref[...] = dot(sent.astype(BF16), taken, (1, 1)).astype(BF16)
    tag = jnp.sum(sent, axis=1, keepdims=True)
    out_ref[:, 1536:1664] = jnp.broadcast_to(tag, (512, 128)).astype(BF16)

    def load(by):
        at = pl.ds(pl.multiple_of(by * 8, 8), 8)
        return field_ref[:, :, at, :].reshape(192, 256)

    cut_patches(load, pick_ref, out_ref, *scratch)


def new_kernel(
    field_ref, z_prev_ref, z_next_ref, y_prev_ref, y_next_ref, pick_ref, new_ref, out_ref, pad_ref, *scratch
):
    pad_ref[:, 1:9, 8:136, :] = field_ref[...]
    pad_ref[:, 0:1, 8:136, :] = z_prev_ref[...]
    pad_ref[:, 9:10, 8:136, :] = z_next_ref[...]
    pad_ref[:, 1:9, 7:8, :] = y_prev_ref[...]
    pad_ref[:, 1:9, 136:137, :] = y_next_ref[...]

    def layer(z, carry):
        for y in range(0, 128, 32):
            along = [pad_ref[c, z + 1, 8 + y : 40 + y, :] for c in range(3)]
            for c in range(3):
                centre = along[c]
                z_next = pad_ref[c, z + 2, 8 + y : 40 + y, :]
                z_prev = pad_ref[c, z, 8 + y : 40 + y, :]
                y_next = pad_ref[c, z + 1, 9 + y : 41 + y, :]
                y_prev = pad_ref[c, z + 1, 7 + y : 39 + y, :]
                x_next = pltpu.roll(centre, 255, 1)
                x_prev = pltpu.roll(centre, 1, 1)
                laplace = z_next + z_prev + y_next + y_prev + x_next + x_prev - 6.0 * centre
                transport = (
                    along[0] * (0.5 * (x_next - x_prev))
                    + along[1] * (0.5 * (y_next - y_prev))
                    + along[2] * (0.5 * (z_next - z_prev))
                )
                new_ref[c, z, y : y + 32, :] = (
                    centre - TIME_STEP * transport + VISCOSITY * TIME_STEP * laplace
                )
        return carry

    lax.fori_loop(0, 8, layer, 0)

    def load(by):
        at = pl.ds(pl.multiple_of(by * 8, 8), 8)
        return new_ref[:, :, at, :].reshape(192, 256)

    cut_patches(load, pick_ref, out_ref, *scratch)


def pack(blocks):
    row, col = iota((128, 128), 0), iota((128, 128), 1)
    return jnp.where(row // 64 == col // 64, blocks[0], pltpu.roll(blocks[1], 64, 1))


def unpack(packed):
    row, col = iota((128, 128), 0), iota((128, 128), 1)
    own = row // 64 == col // 64
    return jnp.where(own, packed, 0.0), jnp.where(own, pltpu.roll(packed, 64, 1), 0.0)


def absolute(m, j):
    return pl.multiple_of(((m - j) & 3) * 128, 128)


def forward_kernel(
    m_ref, old_ref, lift_w_ref, w0_ref, w1_ref, w2_ref, w3_ref,
    lifted_ref, query_ref, key_ref, key_spread_ref, value_ref, value_spread_ref,
    query_w_ref, key_w_ref, value_w_ref, sums_ref, acc_ref,
):
    m = m_ref[0]
    for j, block in enumerate((w0_ref, w1_ref, w2_ref, w3_ref)):
        at = pl.ds(absolute(m, j), 128)
        query_w_ref[:, at] = block[0]
        key_w_ref[:, at] = block[1]
        value_w_ref[:, at] = block[2]
    acc_ref[...] = jnp.zeros_like(acc_ref)
    mix = mean_matrix()

    def rows(i, carry):
        at = pl.ds(pl.multiple_of(i * CHUNK, CHUNK), CHUNK)
        lifted = dot(old_ref[at, 0:1536], lift_w_ref[...]).astype(BF16)
        lifted_ref[at, :] = lifted
        query_ref[at, :] = dot(lifted, query_w_ref[...]).astype(BF16)
        normed = []
        for w_ref, hat_ref, spread_ref in (
            (key_w_ref, key_ref, key_spread_ref),
            (value_w_ref, value_ref, value_spread_ref),
        ):
            heads = dot(lifted, w_ref[...])
            shifted = heads - head_mean(heads, mix)
            spread = jnp.sqrt(head_mean(shifted * shifted, mix) + EPSILON)
            hat = shifted / spread
            hat_ref[at, :] = hat
            spread_ref[at, :] = spread
            normed.append(hat.astype(BF16))
        for p in range(4):
            part = slice(p * 128, (p + 1) * 128)
            acc_ref[p] += dot(normed[0][:, part], normed[1][:, part], (0, 0))
        return carry

    lax.fori_loop(0, 512 // CHUNK, rows, 0)
    sums_ref[0:128, :] = pack((acc_ref[0], acc_ref[1]))
    sums_ref[128:256, :] = pack((acc_ref[2], acc_ref[3]))
    count = jnp.sum(old_ref[:, 1536:1664].astype(F32), axis=0, keepdims=True)
    sums_ref[256:264, :] = jnp.broadcast_to(count, (8, 128))


def middle_kernel(
    m_ref, s0_ref, s1_ref, s2_ref, s3_ref, lifted_ref, query_ref, new_ref,
    o0_ref, o1_ref, o2_ref, o3_ref, proj_w_ref,
    send_ref, d_query_ref, d_hidden_ref, sums_ref, count_ref,
    out_w_ref, hidden_ref, d_guess_ref, attended_ref, d_tokens_ref, acc_ref, high_ref, low_ref, loss_ref,
):
    m = m_ref[0]
    for j, block in enumerate((o0_ref, o1_ref, o2_ref, o3_ref)):
        out_w_ref[pl.ds(absolute(m, j), 128), :] = block[...]
    total = (s0_ref[...] + s1_ref[...]) + (s2_ref[...] + s3_ref[...])
    count = total[256:264, :]
    count_ref[...] = count
    for p in range(2):
        blocks = unpack(total[p * 128 : (p + 1) * 128] / count[0:1, :])
        for q in range(2):
            high_ref[2 * p + q], low_ref[2 * p + q] = split(blocks[q])
    acc_ref[...] = jnp.zeros_like(acc_ref)
    loss_ref[...] = jnp.zeros_like(loss_ref)

    def rows(i, carry):
        at = pl.ds(pl.multiple_of(i * CHUNK, CHUNK), CHUNK)
        query = query_ref[at, :]
        parts = []
        for p in range(4):
            part = query[:, p * 128 : (p + 1) * 128]
            parts.append(dot(part, high_ref[p]) + dot(part, low_ref[p]))
        attended = jnp.concatenate(parts, axis=1).astype(BF16)
        attended_ref[at, :] = attended
        mixed = dot(attended, out_w_ref[...])
        hidden = (lifted_ref[at, :].astype(F32) + mixed).astype(BF16)
        hidden_ref[at, :] = hidden
        error = dot(hidden, proj_w_ref[...]) - new_ref[at, :].astype(F32)
        loss_ref[...] += jnp.sum((error * error).reshape(CHUNK // 8, 8, 1536), axis=0)
        d_guess = (error * (1.0 / 32768)).astype(BF16)
        d_guess_ref[at, :] = d_guess
        d_hidden = dot(d_guess, proj_w_ref[...], (1, 1))
        d_hidden_ref[at, :] = d_hidden
        d_tokens = d_hidden.astype(BF16)
        d_tokens_ref[at, :] = d_tokens
        high, low = split(dot(d_tokens, out_w_ref[...], (1, 1)))
        for p in range(4):
            part = slice(p * 128, (p + 1) * 128)
            back = (
                dot(high[:, part], high_ref[p], (1, 1))
                + dot(high[:, part], low_ref[p], (1, 1))
                + dot(low[:, part], high_ref[p], (1, 1))
            )
            d_query_ref[at, part] = back.astype(BF16)
            acc_ref[p] += dot(query[:, part], high[:, part], (0, 0)) + dot(
                query[:, part], low[:, part], (0, 0)
            )
        return carry

    lax.fori_loop(0, 512 // CHUNK, rows, 0)
    sums_ref[0:128, :] = pack((acc_ref[0], acc_ref[1]))
    sums_ref[128:256, :] = pack((acc_ref[2], acc_ref[3]))
    loss = jnp.sum(loss_ref[...], axis=(0, 1), keepdims=True) * (1.0 / 50331648)
    sums_ref[256:264, :] = jnp.broadcast_to(loss, (8, 128))
    for n in range(4):
        for j in range(3):
            at = n * 384 + j * 128
            grad = dot(hidden_ref[...], d_guess_ref[:, at : at + 128], (0, 0)).astype(BF16)
            send_ref[:, n, 16 * j : 16 * j + 16, :] = grad.reshape(32, 16, 128)
        at = n * 128
        grad = dot(d_tokens_ref[...], attended_ref[:, at : at + 128], (0, 0)).astype(BF16)
        send_ref[:, n, 48:64, :] = grad.reshape(32, 16, 128)


def backward_kernel(
    s0_ref, s1_ref, s2_ref, s3_ref, count_ref, old_ref, lifted_ref, key_ref, key_spread_ref,
    value_ref, value_spread_ref, d_query_ref, d_hidden_ref, query_w_ref, key_w_ref, value_w_ref,
    send_ref, loss_ref, high_ref, low_ref, d_key_ref, d_value_ref, d_lifted_ref,
):
    total = (s0_ref[...] + s1_ref[...]) + (s2_ref[...] + s3_ref[...])
    loss_ref[...] = total[256:264, :]
    for p in range(2):
        blocks = unpack(total[p * 128 : (p + 1) * 128] / count_ref[0:1, :])
        for q in range(2):
            high_ref[2 * p + q], low_ref[2 * p + q] = split(blocks[q])
    mix = mean_matrix()

    def rows(i, carry):
        at = pl.ds(pl.multiple_of(i * CHUNK, CHUNK), CHUNK)
        d_lifted = d_hidden_ref[at, :] + dot(d_query_ref[at, :], query_w_ref[...], (1, 1))
        for hat_ref, spread_ref, other_ref, across, grad_ref, w_ref in (
            (key_ref, key_spread_ref, value_ref, (1, 1), d_key_ref, key_w_ref),
            (value_ref, value_spread_ref, key_ref, (1, 0), d_value_ref, value_w_ref),
        ):
            other = other_ref[at, :].astype(BF16)
            parts = []
            for p in range(4):
                part = other[:, p * 128 : (p + 1) * 128]
                parts.append(dot(part, high_ref[p], across) + dot(part, low_ref[p], across))
            grad = jnp.concatenate(parts, axis=1)
            hat = hat_ref[at, :]
            inner = head_mean(grad, mix)
            cross = head_mean(grad * hat, mix)
            grad = ((grad - inner - hat * cross) / spread_ref[at, :]).astype(BF16)
            grad_ref[at, :] = grad
            d_lifted = d_lifted + dot(grad, w_ref[...], (1, 1))
        d_lifted_ref[at, :] = d_lifted.astype(BF16)
        return carry

    lax.fori_loop(0, 512 // CHUNK, rows, 0)
    for n in range(4):
        at = slice(n * 128, (n + 1) * 128)
        grad = dot(old_ref[:, 0:1536], d_lifted_ref[:, at], (0, 0)).astype(BF16)
        send_ref[:, n, 0:48, :] = grad.reshape(32, 48, 128)
        for j, grad_ref in enumerate((d_query_ref, d_key_ref, d_value_ref)):
            grad = dot(lifted_ref[...], grad_ref[:, at], (0, 0)).astype(BF16)
            send_ref[:, n, 48 + 16 * j : 64 + 16 * j, :] = grad.reshape(32, 16, 128)


def last_kernel(
    m_ref, r0_ref, r1_ref, r2_ref, r3_ref, heads_ref,
    lift_ref, query_ref, key_ref, value_ref, out_ref, proj_ref, loss_ref,
):
    m = m_ref[0]
    for j, block in enumerate((r0_ref, r1_ref, r2_ref, r3_ref)):
        lift_ref[:, pl.ds(absolute(m, j), 128)] = block[0:48, :]
        for k in range(3):
            at = pl.multiple_of(((m - j) & 3) * 384 + k * 128, 128)
            proj_ref[:, pl.ds(at, 128)] = block[48 + 16 * k : 64 + 16 * k, :]
    query_ref[...] = heads_ref[:, 0:16, :].astype(F32).reshape(512, 128)
    key_ref[...] = heads_ref[:, 16:32, :].astype(F32).reshape(512, 128)
    value_ref[...] = heads_ref[:, 32:48, :].astype(F32).reshape(512, 128)
    out_ref[...] = heads_ref[:, 48:64, :].astype(F32).reshape(512, 128).T
    loss = jnp.sum(heads_ref[:, 64:80, :].astype(F32), axis=0)
    loss_ref[...] = jnp.broadcast_to(loss[0:1] + loss[1:2], (8, 128))


def call(body, outs, scratch=(), scalars=0, ins=0):
    shapes = [jax.ShapeDtypeStruct(shape, kind) for shape, kind in outs]
    memory = [pl.BlockSpec(memory_space=pltpu.SMEM)] * scalars
    memory += [pl.BlockSpec(memory_space=pltpu.VMEM)] * ins
    return pl.pallas_call(
        body,
        out_shape=shapes,
        in_specs=memory,
        out_specs=[pl.BlockSpec(memory_space=pltpu.VMEM)] * len(outs),
        scratch_shapes=list(scratch),
        compiler_params=pltpu.CompilerParams(vmem_limit_bytes=60 << 20),
    )


def around(value):
    return [value] + [lax.ppermute(value, "mp", [(i, (i + d) % 4) for i in range(4)]) for d in (1, 2, 3)]


def shards(velocity, anchors, dest, w_lift, w_query, w_key, w_value, w_out, w_proj):
    slabs = lax.axis_size("slab")
    m = lax.axis_index("mp").reshape(1)
    up = [(i, (i + 1) % slabs) for i in range(slabs)]
    z_prev = lax.ppermute(velocity[:, 7:8], "slab", up)
    z_next = lax.ppermute(velocity[:, 0:1], "slab", [(j, i) for i, j in up])
    up = [(i, (i + 1) % 4) for i in range(4)]
    y_prev = lax.ppermute(velocity[:, :, 127:128], "mp", up)
    y_next = lax.ppermute(velocity[:, :, 0:1], "mp", [(j, i) for i, j in up])
    heads_w = around(jnp.stack([w_query, w_key, w_value]))
    outs_w = around(w_out)

    send_old, pick = call(
        old_kernel, [((512, 1664), BF16), ((512, 512), BF16)], CUT_SCRATCH, 0, 3
    )(velocity, anchors.reshape(3, 256), dest.reshape(1, 256))
    old = lax.all_to_all(send_old, "slab", split_axis=0, concat_axis=0, tiled=True)
    new_velocity, send_new = call(
        new_kernel,
        [((3, 8, 128, 256), F32), ((512, 1536), BF16)],
        [pltpu.VMEM((3, 10, 144, 256), F32)] + CUT_SCRATCH,
        0,
        6,
    )(velocity, z_prev, z_next, y_prev, y_next, pick)
    new = lax.all_to_all(send_new, "slab", split_axis=0, concat_axis=0, tiled=True)

    wide, wide_f = ((512, 512), BF16), ((512, 512), F32)
    lifted, query, key, key_spread, value, value_spread, wq, wk, wv, sums = call(
        forward_kernel,
        [wide, wide, wide_f, wide_f, wide_f, wide_f, wide, wide, wide, ((264, 128), F32)],
        [pltpu.VMEM((4, 128, 128), F32)],
        1,
        6,
    )(m, old, w_lift, *heads_w)
    send_out, d_query, d_hidden, d_sums, count = call(
        middle_kernel,
        [((32, 4, 64, 128), BF16), wide, wide_f, ((264, 128), F32), ((8, 128), F32)],
        [
            pltpu.VMEM((512, 512), BF16),
            pltpu.VMEM((512, 512), BF16),
            pltpu.VMEM((512, 1536), BF16),
            pltpu.VMEM((512, 512), BF16),
            pltpu.VMEM((512, 512), BF16),
            pltpu.VMEM((4, 128, 128), F32),
            pltpu.VMEM((4, 128, 128), BF16),
            pltpu.VMEM((4, 128, 128), BF16),
            pltpu.VMEM((8, 1536), F32),
        ],
        1,
        12,
    )(m, *around(sums), lifted, query, new, *outs_w, w_proj)
    send_in, loss_part = call(
        backward_kernel,
        [((32, 4, 96, 128), BF16), ((8, 128), F32)],
        [
            pltpu.VMEM((4, 128, 128), BF16),
            pltpu.VMEM((4, 128, 128), BF16),
            pltpu.VMEM((512, 512), BF16),
            pltpu.VMEM((512, 512), BF16),
            pltpu.VMEM((512, 512), BF16),
        ],
        0,
        16,
    )(*around(d_sums), count, old, lifted, key, key_spread, value, value_spread, d_query, d_hidden, wq, wk, wv)

    everyone = ("slab", "mp")
    got_out = lax.all_to_all(send_out.reshape(128, 64, 128), everyone, split_axis=0, concat_axis=0, tiled=True)
    got_in = lax.all_to_all(send_in.reshape(128, 96, 128), everyone, split_axis=0, concat_axis=0, tiled=True)
    total_out = jnp.sum(got_out.astype(F32), axis=0)
    total_in = jnp.sum(got_in.astype(F32), axis=0)
    blocks = jnp.concatenate([total_in[0:48], total_out[0:48]], axis=0)
    loss_high = loss_part.astype(BF16)
    loss_low = (loss_part - loss_high.astype(F32)).astype(BF16)
    heads = jnp.concatenate([total_in[48:96], total_out[48:64]], axis=0).astype(BF16)
    heads = jnp.concatenate([heads, loss_high[0:1], loss_low[0:1], jnp.zeros((14, 128), BF16)], axis=0)
    heads = lax.all_to_all(
        jnp.broadcast_to(heads[None], (32, 80, 128)), "slab", split_axis=0, concat_axis=0, tiled=True
    )
    lift, g_query, g_key, g_value, g_out, proj, loss = call(
        last_kernel,
        [
            ((48, 512), F32),
            ((512, 128), F32),
            ((512, 128), F32),
            ((512, 128), F32),
            ((128, 512), F32),
            ((16, 1536), F32),
            ((8, 128), F32),
        ],
        (),
        1,
        5,
    )(m, *around(blocks), heads)
    return (new_velocity, loss[0, 0], lift, g_query, g_key, g_value, g_out, proj)


def solution(mesh):
    return jax.shard_map(
        shards,
        mesh=mesh,
        in_specs=(
            P(None, "slab", "mp", None),
            P(None, "slab", "mp", None),
            P("slab", "mp", None, None),
            P(),
            P(None, "mp"),
            P(None, "mp"),
            P(None, "mp"),
            P("mp", None),
            P(),
        ),
        out_specs=(
            P(None, "slab", "mp", None),
            P(),
            P("slab", None),
            P(None, "mp"),
            P(None, "mp"),
            P(None, "mp"),
            P("mp", None),
            P("slab", None),
        ),
        check_vma=False,
    )
```

```python
import jax
import jax.numpy as jnp
from jax import lax
from jax.experimental import pallas as pl
from jax.experimental.pallas import tpu as pltpu
from jax.sharding import PartitionSpec as P


TIME_STEP = 0.1
VISCOSITY = 0.2
EPSILON = 1e-05
F32 = jnp.float32
BF16 = jnp.bfloat16
CHUNK = 256


def iota(shape, dim):
    return lax.broadcasted_iota(jnp.int32, shape, dim)


def dot(a, b, contract=(1, 0)):
    dims = (((contract[0],), (contract[1],)), ((), ()))
    return lax.dot_general(a, b, dims, preferred_element_type=F32)


def split(a):
    high = a.astype(BF16)
    return high, (a - high.astype(F32)).astype(BF16)


def head_mean(a, mix):
    high, low = split(a)
    halves = [
        dot(high[:, at : at + 256], mix) + dot(low[:, at : at + 256], mix) for at in (0, 256)
    ]
    return jnp.concatenate(halves, axis=1)


def mean_matrix():
    same = iota((256, 256), 0) // 64 == iota((256, 256), 1) // 64
    return jnp.where(same, 1.0 / 64, 0.0).astype(BF16)


def selections(once_ref, pair_ref, turn_ref):
    row, col = iota((256, 256), 0), iota((256, 256), 1)
    turn_ref[...] = jnp.where(col == (row & 31) * 8 + (row >> 5), 1.0, 0.0).astype(BF16)

    def spread(i, carry):
        at = pl.ds(pl.multiple_of(i * 128, 128), 128)
        row, col = iota((128, 1024), 0), iota((128, 1024), 1)
        once_ref[at, :] = jnp.where(col == 8 * row + i, 1.0, 0.0).astype(BF16)
        return carry

    lax.fori_loop(0, 8, spread, 0)
    row, col = iota((512, 512), 0), iota((512, 512), 1)
    pair_ref[...] = jnp.where(col == 8 * (row & 63) + (row >> 6), 1.0, 0.0).astype(BF16)


def cut_patches(load, pick_ref, out_ref, once_ref, pair_ref, turn_ref, whole_ref, rest_ref):
    row, col = iota((128, 256), 0), iota((128, 256), 1)
    turn_pair = jnp.where(col == (row & 31) * 8 + 2 * (row >> 5), 1.0, 0.0).astype(BF16)

    def strips(i, carry):
        cells = [load(2 * i), load(2 * i + 1)]
        first = jnp.concatenate([c[:128] for c in cells], axis=0).astype(BF16)
        last = [c[128:] for c in cells]
        last = [jnp.concatenate([c, pltpu.roll(c, 255, 1)], axis=0) for c in last]
        last = jnp.concatenate(last, axis=0).astype(BF16)
        whole = dot(turn_ref[...], first, (1, 1)).astype(BF16)
        rest = dot(turn_pair, last, (1, 1)).astype(BF16)
        for k in range(2):
            at = pl.ds(pl.multiple_of(i * 64 + k * 32, 32), 32)
            lanes = slice(k * 128, (k + 1) * 128)
            for x in range(8):
                whole_ref[at, x * 128 : (x + 1) * 128] = whole[x * 32 : (x + 1) * 32, lanes]
            for x in range(4):
                rest_ref[at, x * 128 : (x + 1) * 128] = rest[x * 32 : (x + 1) * 32, lanes]
        return carry

    lax.fori_loop(0, 8, strips, 0)

    def place(i, carry):
        at = pl.ds(pl.multiple_of(i * CHUNK, CHUNK), CHUNK)
        pick = pick_ref[at, :]
        picked = dot(pick, whole_ref[...]).astype(BF16)
        out_ref[at, 0:1024] = dot(picked, once_ref[...]).astype(BF16)
        picked = dot(pick, rest_ref[...]).astype(BF16)
        out_ref[at, 1024:1536] = dot(picked, pair_ref[...]).astype(BF16)
        return carry

    lax.fori_loop(0, 512 // CHUNK, place, 0)


CUT_SCRATCH = [
    pltpu.VMEM((1024, 1024), BF16),
    pltpu.VMEM((512, 512), BF16),
    pltpu.VMEM((256, 256), BF16),
    pltpu.VMEM((512, 1024), BF16),
    pltpu.VMEM((512, 512), BF16),
]


def old_kernel(field_hbm, anchor_ref, dest_ref, out_ref, pick_ref, field_ref, sem, *scratch):
    fetch = pltpu.make_async_copy(field_hbm, field_ref, sem)
    fetch.start()
    selections(*scratch[:3])
    target = dest_ref[...].astype(F32)
    wide = jnp.broadcast_to(target, (256, 256))
    row, col = iota((256, 256), 0), iota((256, 256), 1)
    tall = jnp.sum(jnp.where(row == col, wide, 0.0), axis=1, keepdims=True)
    ahead = jnp.where((tall == wide) & (row < col), 1.0, 0.0)
    slot = target * 16.0 + jnp.sum(ahead, axis=0, keepdims=True)
    patch = ((anchor_ref[1] >> 3) & 15) * 32 + ((anchor_ref[2] >> 3) & 31)
    row = iota((512, 256), 0)
    sent = jnp.where(row == slot.astype(jnp.int32), 1.0, 0.0)
    taken = jnp.where(row == patch, 1.0, 0.0).astype(BF16)
    pick_ref[...] = dot(sent.astype(BF16), taken, (1, 1)).astype(BF16)
    tag = jnp.sum(sent, axis=1, keepdims=True)
    out_ref[:, 1536:1664] = jnp.broadcast_to(tag, (512, 128)).astype(BF16)
    fetch.wait()

    def load(by):
        at = pl.ds(pl.multiple_of(by * 8, 8), 8)
        return field_ref[:, :, at, :].reshape(192, 256)

    cut_patches(load, pick_ref, out_ref, *scratch)


def new_kernel(
    field_hbm, z_prev_ref, z_next_ref, y_prev_ref, y_next_ref, pick_ref,
    new_hbm, out_ref, pad_ref, new_ref, sem, *scratch,
):
    fetch = pltpu.make_async_copy(field_hbm, pad_ref.at[:, 1:9, 8:136, :], sem.at[0])
    fetch.start()
    selections(*scratch[:3])
    pad_ref[:, 0:1, 8:136, :] = z_prev_ref[...]
    pad_ref[:, 9:10, 8:136, :] = z_next_ref[...]
    pad_ref[:, 1:9, 7:8, :] = y_prev_ref[...]
    pad_ref[:, 1:9, 136:137, :] = y_next_ref[...]
    fetch.wait()
    near = VISCOSITY * TIME_STEP

    def layer(z, carry):
        for y in range(0, 128, 32):
            along = [pad_ref[c, z + 1, 8 + y : 40 + y, :] for c in range(3)]
            drift = [(0.5 * TIME_STEP) * v for v in along]
            ahead = [near - v for v in drift]
            behind = [near + v for v in drift]
            for c in range(3):
                centre = along[c]
                z_next = pad_ref[c, z + 2, 8 + y : 40 + y, :]
                z_prev = pad_ref[c, z, 8 + y : 40 + y, :]
                y_next = pad_ref[c, z + 1, 9 + y : 41 + y, :]
                y_prev = pad_ref[c, z + 1, 7 + y : 39 + y, :]
                x_next = pltpu.roll(centre, 255, 1)
                x_prev = pltpu.roll(centre, 1, 1)
                new_ref[c, z, y : y + 32, :] = (
                    (1.0 - 6.0 * near) * centre
                    + (ahead[0] * x_next + behind[0] * x_prev)
                    + (ahead[1] * y_next + behind[1] * y_prev)
                    + (ahead[2] * z_next + behind[2] * z_prev)
                )
        return carry

    lax.fori_loop(0, 8, layer, 0)
    store = pltpu.make_async_copy(new_ref, new_hbm, sem.at[1])
    store.start()

    def load(by):
        at = pl.ds(pl.multiple_of(by * 8, 8), 8)
        return new_ref[:, :, at, :].reshape(192, 256)

    cut_patches(load, pick_ref, out_ref, *scratch)
    store.wait()


def pack(blocks):
    row, col = iota((128, 128), 0), iota((128, 128), 1)
    return jnp.where(row // 64 == col // 64, blocks[0], pltpu.roll(blocks[1], 64, 1))


def unpack(packed):
    row, col = iota((128, 128), 0), iota((128, 128), 1)
    own = row // 64 == col // 64
    return jnp.where(own, packed, 0.0), jnp.where(own, pltpu.roll(packed, 64, 1), 0.0)


def absolute(m, j):
    return pl.multiple_of(((m - j) & 3) * 128, 128)


def forward_kernel(
    m_ref, old_ref, lift_w_ref, w0_ref, w1_ref, w2_ref, w3_ref,
    lifted_ref, query_ref, key_ref, key_spread_ref, value_ref, value_spread_ref,
    query_w_ref, key_w_ref, value_w_ref, out_w_ref, sums_ref, acc_ref,
):
    m = m_ref[0]
    for j, block in enumerate((w0_ref, w1_ref, w2_ref, w3_ref)):
        at = pl.ds(absolute(m, j), 128)
        query_w_ref[:, at] = block[0]
        key_w_ref[:, at] = block[1]
        value_w_ref[:, at] = block[2]
        for k in range(4):
            out_w_ref[at, k * 128 : (k + 1) * 128] = block[3, k * 128 : (k + 1) * 128, :]
    acc_ref[...] = jnp.zeros_like(acc_ref)
    mix = mean_matrix()

    def rows(i, carry):
        at = pl.ds(pl.multiple_of(i * CHUNK, CHUNK), CHUNK)
        lifted = dot(old_ref[at, 0:1536], lift_w_ref[...]).astype(BF16)
        lifted_ref[at, :] = lifted
        query_ref[at, :] = dot(lifted, query_w_ref[...]).astype(BF16)
        normed = []
        for w_ref, hat_ref, spread_ref in (
            (key_w_ref, key_ref, key_spread_ref),
            (value_w_ref, value_ref, value_spread_ref),
        ):
            heads = dot(lifted, w_ref[...])
            shifted = heads - head_mean(heads, mix)
            spread = jnp.sqrt(head_mean(shifted * shifted, mix) + EPSILON)
            hat = shifted / spread
            normed.append(hat.astype(BF16))
            hat_ref[at, :] = normed[-1]
            spread_ref[at, :] = spread
        for p in range(4):
            part = slice(p * 128, (p + 1) * 128)
            acc_ref[p] += dot(normed[0][:, part], normed[1][:, part], (0, 0))
        return carry

    lax.fori_loop(0, 512 // CHUNK, rows, 0)
    sums_ref[0:128, :] = pack((acc_ref[0], acc_ref[1]))
    sums_ref[128:256, :] = pack((acc_ref[2], acc_ref[3]))
    count = jnp.sum(old_ref[:, 1536:1664].astype(F32), axis=0, keepdims=True)
    sums_ref[256:264, :] = jnp.broadcast_to(count, (8, 128))


def middle_kernel(
    s0_ref, s1_ref, s2_ref, s3_ref, lifted_ref, query_ref, new_ref,
    out_w_ref, proj_w_ref,
    send_ref, d_query_ref, d_hidden_ref, sums_ref, count_ref,
    hidden_ref, d_guess_ref, attended_ref, d_tokens_ref, acc_ref, high_ref, low_ref, loss_ref,
):
    total = (s0_ref[...] + s1_ref[...]) + (s2_ref[...] + s3_ref[...])
    count = total[256:264, :]
    count_ref[...] = count
    for p in range(2):
        blocks = unpack(total[p * 128 : (p + 1) * 128] / count[0:1, :])
        for q in range(2):
            high_ref[2 * p + q], low_ref[2 * p + q] = split(blocks[q])
    acc_ref[...] = jnp.zeros_like(acc_ref)
    loss_ref[...] = jnp.zeros_like(loss_ref)

    def rows(i, carry):
        at = pl.ds(pl.multiple_of(i * CHUNK, CHUNK), CHUNK)
        query = query_ref[at, :]
        parts = []
        for p in range(4):
            part = query[:, p * 128 : (p + 1) * 128]
            parts.append(dot(part, high_ref[p]) + dot(part, low_ref[p]))
        attended = jnp.concatenate(parts, axis=1).astype(BF16)
        attended_ref[at, :] = attended
        mixed = dot(attended, out_w_ref[...])
        hidden = (lifted_ref[at, :].astype(F32) + mixed).astype(BF16)
        hidden_ref[at, :] = hidden
        error = dot(hidden, proj_w_ref[...]) - new_ref[at, :].astype(F32)
        loss_ref[...] += jnp.sum((error * error).reshape(CHUNK // 8, 8, 1536), axis=0)
        d_guess = (error * (1.0 / 32768)).astype(BF16)
        d_guess_ref[at, :] = d_guess
        d_hidden = dot(d_guess, proj_w_ref[...], (1, 1))
        d_hidden_ref[at, :] = d_hidden
        d_tokens = d_hidden.astype(BF16)
        d_tokens_ref[at, :] = d_tokens
        high, low = split(dot(d_tokens, out_w_ref[...], (1, 1)))
        for p in range(4):
            part = slice(p * 128, (p + 1) * 128)
            back = (
                dot(high[:, part], high_ref[p], (1, 1))
                + dot(high[:, part], low_ref[p], (1, 1))
                + dot(low[:, part], high_ref[p], (1, 1))
            )
            d_query_ref[at, part] = back.astype(BF16)
            acc_ref[p] += dot(query[:, part], high[:, part], (0, 0)) + dot(
                query[:, part], low[:, part], (0, 0)
            )
        return carry

    lax.fori_loop(0, 512 // CHUNK, rows, 0)
    sums_ref[0:128, :] = pack((acc_ref[0], acc_ref[1]))
    sums_ref[128:256, :] = pack((acc_ref[2], acc_ref[3]))
    loss = jnp.sum(loss_ref[...], axis=(0, 1), keepdims=True) * (1.0 / 50331648)
    sums_ref[256:264, :] = jnp.broadcast_to(loss, (8, 128))
    grad = dot(hidden_ref[...], d_guess_ref[...], (0, 0)).astype(BF16)
    for n in range(4):
        for j in range(3):
            at = n * 384 + j * 128
            send_ref[:, n, 16 * j : 16 * j + 16, :] = grad[:, at : at + 128].reshape(32, 16, 128)
    grad = dot(d_tokens_ref[...], attended_ref[...], (0, 0)).astype(BF16)
    for n in range(4):
        send_ref[:, n, 48:64, :] = grad[:, n * 128 : (n + 1) * 128].reshape(32, 16, 128)


def backward_kernel(
    s0_ref, s1_ref, s2_ref, s3_ref, count_ref, old_hbm, lifted_ref, key_ref, key_spread_ref,
    value_ref, value_spread_ref, d_query_ref, d_hidden_ref, query_w_ref, key_w_ref, value_w_ref,
    send_ref, loss_ref, high_ref, low_ref, d_heads_ref, d_lifted_ref, old_ref, sem,
):
    fetch = pltpu.make_async_copy(old_hbm.at[:, 0:1536], old_ref, sem)
    fetch.start()
    total = (s0_ref[...] + s1_ref[...]) + (s2_ref[...] + s3_ref[...])
    loss_ref[...] = total[256:264, :]
    for p in range(2):
        blocks = unpack(total[p * 128 : (p + 1) * 128] / count_ref[0:1, :])
        for q in range(2):
            high_ref[2 * p + q], low_ref[2 * p + q] = split(blocks[q])
    mix = mean_matrix()

    def rows(i, carry):
        at = pl.ds(pl.multiple_of(i * CHUNK, CHUNK), CHUNK)
        d_query = d_query_ref[at, :]
        d_heads_ref[at, 0:512] = d_query
        d_lifted = d_hidden_ref[at, :] + dot(d_query, query_w_ref[...], (1, 1))
        for hat_ref, spread_ref, other_ref, across, lanes, w_ref in (
            (key_ref, key_spread_ref, value_ref, (1, 1), 512, key_w_ref),
            (value_ref, value_spread_ref, key_ref, (1, 0), 1024, value_w_ref),
        ):
            other = other_ref[at, :]
            parts = []
            for p in range(4):
                part = other[:, p * 128 : (p + 1) * 128]
                parts.append(dot(part, high_ref[p], across) + dot(part, low_ref[p], across))
            grad = jnp.concatenate(parts, axis=1)
            hat = hat_ref[at, :].astype(F32)
            inner = head_mean(grad, mix)
            cross = head_mean(grad * hat, mix)
            grad = ((grad - inner - hat * cross) / spread_ref[at, :]).astype(BF16)
            d_heads_ref[at, lanes : lanes + 512] = grad
            d_lifted = d_lifted + dot(grad, w_ref[...], (1, 1))
        d_lifted_ref[at, :] = d_lifted.astype(BF16)
        return carry

    lax.fori_loop(0, 512 // CHUNK, rows, 0)
    grad = dot(lifted_ref[...], d_heads_ref[...], (0, 0)).astype(BF16)
    for n in range(4):
        for j in range(3):
            at = 512 * j + 128 * n
            send_ref[:, n, 48 + 16 * j : 64 + 16 * j, :] = grad[:, at : at + 128].reshape(32, 16, 128)
    fetch.wait()
    grad = dot(old_ref[...], d_lifted_ref[...], (0, 0)).astype(BF16)
    for n in range(4):
        send_ref[:, n, 0:48, :] = grad[:, n * 128 : (n + 1) * 128].reshape(32, 48, 128)


def last_kernel(
    m_ref, r0_ref, r1_ref, r2_ref, r3_ref, heads_ref,
    lift_ref, query_ref, key_ref, value_ref, out_ref, proj_ref, loss_ref,
):
    m = m_ref[0]
    for j, block in enumerate((r0_ref, r1_ref, r2_ref, r3_ref)):
        lift_ref[:, pl.ds(absolute(m, j), 128)] = block[0:48, :]
        for k in range(3):
            at = pl.multiple_of(((m - j) & 3) * 384 + k * 128, 128)
            proj_ref[:, pl.ds(at, 128)] = block[48 + 16 * k : 64 + 16 * k, :]
    query_ref[...] = heads_ref[:, 0:16, :].astype(F32).reshape(512, 128)
    key_ref[...] = heads_ref[:, 16:32, :].astype(F32).reshape(512, 128)
    value_ref[...] = heads_ref[:, 32:48, :].astype(F32).reshape(512, 128)
    out_ref[...] = heads_ref[:, 48:64, :].astype(F32).reshape(512, 128).T
    loss = jnp.sum(heads_ref[:, 64:80, :].astype(F32), axis=0)
    loss_ref[...] = jnp.broadcast_to(loss[0:1] + loss[1:2], (8, 128))


def call(body, outs, scratch=(), ins="", results=None):
    spaces = {"s": pltpu.SMEM, "h": pl.ANY, "v": pltpu.VMEM}
    return pl.pallas_call(
        body,
        out_shape=[jax.ShapeDtypeStruct(shape, kind) for shape, kind in outs],
        in_specs=[pl.BlockSpec(memory_space=spaces[k]) for k in ins],
        out_specs=[pl.BlockSpec(memory_space=spaces[k]) for k in results or "v" * len(outs)],
        scratch_shapes=list(scratch),
        compiler_params=pltpu.CompilerParams(vmem_limit_bytes=60 << 20),
    )


def around(value):
    got = [value]
    for d in (1, 2, 3):
        got.append(lax.ppermute(value, "mp", [(i, (i + d) % 4) for i in range(4)]))
    return got


def exchange(value, axes):
    return lax.all_to_all(value, axes, split_axis=0, concat_axis=0, tiled=True)


def step(velocity, anchors, dest, w_lift, w_query, w_key, w_value, w_out, w_proj):
    slabs = lax.axis_size("slab")
    m = lax.axis_index("mp").reshape(1)
    up = [(i, (i + 1) % slabs) for i in range(slabs)]
    z_prev = lax.ppermute(velocity[:, 7:8], "slab", up)
    z_next = lax.ppermute(velocity[:, 0:1], "slab", [(j, i) for i, j in up])
    up = [(i, (i + 1) % 4) for i in range(4)]
    y_prev = lax.ppermute(velocity[:, :, 127:128], "mp", up)
    y_next = lax.ppermute(velocity[:, :, 0:1], "mp", [(j, i) for i, j in up])
    tall = jnp.concatenate([w_out[:, k * 128 : (k + 1) * 128] for k in range(4)], axis=0)
    heads_w = around(jnp.stack([w_query, w_key, w_value, tall]))

    send_old, pick = call(
        old_kernel,
        [((512, 1664), BF16), ((512, 512), BF16)],
        [pltpu.VMEM((3, 8, 128, 256), F32), pltpu.SemaphoreType.DMA] + CUT_SCRATCH,
        "hvv",
    )(velocity, anchors.reshape(3, 1, 256), dest.reshape(1, 256))
    old = exchange(send_old, "slab")
    new_velocity, send_new = call(
        new_kernel,
        [((3, 8, 128, 256), F32), ((512, 1536), BF16)],
        [
            pltpu.VMEM((3, 10, 144, 256), F32),
            pltpu.VMEM((3, 8, 128, 256), F32),
            pltpu.SemaphoreType.DMA((2,)),
        ]
        + CUT_SCRATCH,
        "hvvvvv",
        "hv",
    )(velocity, z_prev, z_next, y_prev, y_next, pick)
    new = exchange(send_new, "slab")

    wide, wide_f = ((512, 512), BF16), ((512, 512), F32)
    lifted, query, key, key_spread, value, value_spread, wq, wk, wv, wo, sums = call(
        forward_kernel,
        [wide, wide, wide, wide_f, wide, wide_f, wide, wide, wide, wide, ((264, 128), F32)],
        [pltpu.VMEM((4, 128, 128), F32)],
        "svvvvvv",
    )(m, old, w_lift, *heads_w)
    sums = around(sums)
    send_out, d_query, d_hidden, d_sums, count = call(
        middle_kernel,
        [((32, 4, 64, 128), BF16), wide, wide_f, ((264, 128), F32), ((8, 128), F32)],
        [
            pltpu.VMEM((512, 512), BF16),
            pltpu.VMEM((512, 1536), BF16),
            pltpu.VMEM((512, 512), BF16),
            pltpu.VMEM((512, 512), BF16),
            pltpu.VMEM((4, 128, 128), F32),
            pltpu.VMEM((4, 128, 128), BF16),
            pltpu.VMEM((4, 128, 128), BF16),
            pltpu.VMEM((8, 1536), F32),
        ],
        "vvvvvvvvv",
    )(*sums, lifted, query, new, wo, w_proj)
    d_sums = around(d_sums)
    everyone = ("slab", "mp")
    got_out = exchange(send_out.reshape(128, 64, 128), everyone)
    send_in, loss_part = call(
        backward_kernel,
        [((32, 4, 96, 128), BF16), ((8, 128), F32)],
        [
            pltpu.VMEM((4, 128, 128), BF16),
            pltpu.VMEM((4, 128, 128), BF16),
            pltpu.VMEM((512, 1536), BF16),
            pltpu.VMEM((512, 512), BF16),
            pltpu.VMEM((512, 1536), BF16),
            pltpu.SemaphoreType.DMA,
        ],
        "vvvvvhvvvvvvvvvv",
    )(*d_sums, count, old, lifted, key, key_spread, value, value_spread, d_query, d_hidden, wq, wk, wv)
    got_in = exchange(send_in.reshape(128, 96, 128), everyone)

    total_out = jnp.sum(got_out.astype(F32), axis=0)
    total_in = jnp.sum(got_in.astype(F32), axis=0)
    blocks = jnp.concatenate([total_in[0:48], total_out[0:48]], axis=0)
    loss_high = loss_part.astype(BF16)
    loss_low = (loss_part - loss_high.astype(F32)).astype(BF16)
    heads = jnp.concatenate([total_in[48:96], total_out[48:64]], axis=0).astype(BF16)
    heads = jnp.concatenate([heads, loss_high[0:1], loss_low[0:1], jnp.zeros((14, 128), BF16)], axis=0)
    heads = exchange(jnp.broadcast_to(heads[None], (32, 80, 128)), "slab")
    lift, g_query, g_key, g_value, g_out, proj, loss = call(
        last_kernel,
        [
            ((48, 512), F32),
            ((512, 128), F32),
            ((512, 128), F32),
            ((512, 128), F32),
            ((128, 512), F32),
            ((16, 1536), F32),
            ((8, 128), F32),
        ],
        (),
        "svvvvv",
    )(m, *around(blocks), heads)
    return (new_velocity, loss[0, 0], lift, g_query, g_key, g_value, g_out, proj)


def solution(mesh):
    return jax.shard_map(
        step,
        mesh=mesh,
        in_specs=(
            P(None, "slab", "mp", None),
            P(None, "slab", "mp", None),
            P("slab", "mp", None, None),
            P(),
            P(None, "mp"),
            P(None, "mp"),
            P(None, "mp"),
            P("mp", None),
            P(),
        ),
        out_specs=(
            P(None, "slab", "mp", None),
            P(),
            P("slab", None),
            P(None, "mp"),
            P(None, "mp"),
            P(None, "mp"),
            P("mp", None),
            P("slab", None),
        ),
        check_vma=False,
    )
```

```python
import jax
import jax.numpy as jnp
from jax import lax
from jax.experimental import pallas as pl
from jax.experimental.pallas import tpu as pltpu
from jax.sharding import PartitionSpec as P


TIME_STEP = 0.1
VISCOSITY = 0.2
EPSILON = 1e-05
F32 = jnp.float32
BF16 = jnp.bfloat16
CHUNK = 256


def iota(shape, dim):
    return lax.broadcasted_iota(jnp.int32, shape, dim)


def dot(a, b, contract=(1, 0)):
    dims = (((contract[0],), (contract[1],)), ((), ()))
    return lax.dot_general(a, b, dims, preferred_element_type=F32)


def split(a):
    high = a.astype(BF16)
    return high, (a - high.astype(F32)).astype(BF16)


def head_mean(a, mix):
    high, low = split(a)
    halves = [
        dot(high[:, at : at + 256], mix) + dot(low[:, at : at + 256], mix) for at in (0, 256)
    ]
    return jnp.concatenate(halves, axis=1)


def mean_matrix():
    same = iota((256, 256), 0) // 64 == iota((256, 256), 1) // 64
    return jnp.where(same, 1.0 / 64, 0.0).astype(BF16)


def selections(once_ref, pair_ref, turn_ref):
    row, col = iota((256, 256), 0), iota((256, 256), 1)
    turn_ref[...] = jnp.where(col == (row & 31) * 8 + (row >> 5), 1.0, 0.0).astype(BF16)

    def spread(i, carry):
        at = pl.ds(pl.multiple_of(i * 128, 128), 128)
        row, col = iota((128, 1024), 0), iota((128, 1024), 1)
        once_ref[at, :] = jnp.where(col == 8 * row + i, 1.0, 0.0).astype(BF16)
        return carry

    lax.fori_loop(0, 8, spread, 0)
    row, col = iota((512, 512), 0), iota((512, 512), 1)
    pair_ref[...] = jnp.where(col == 8 * (row & 63) + (row >> 6), 1.0, 0.0).astype(BF16)


def cut_patches(load, pick_ref, out_ref, once_ref, pair_ref, turn_ref, whole_ref, rest_ref):
    row, col = iota((128, 256), 0), iota((128, 256), 1)
    turn_pair = jnp.where(col == (row & 31) * 8 + 2 * (row >> 5), 1.0, 0.0).astype(BF16)

    def strips(i, carry):
        cells = [load(2 * i), load(2 * i + 1)]
        first = jnp.concatenate([c[:128] for c in cells], axis=0).astype(BF16)
        last = [c[128:] for c in cells]
        last = [jnp.concatenate([c, pltpu.roll(c, 255, 1)], axis=0) for c in last]
        last = jnp.concatenate(last, axis=0).astype(BF16)
        whole = dot(turn_ref[...], first, (1, 1)).astype(BF16)
        rest = dot(turn_pair, last, (1, 1)).astype(BF16)
        for k in range(2):
            at = pl.ds(pl.multiple_of(i * 64 + k * 32, 32), 32)
            lanes = slice(k * 128, (k + 1) * 128)
            for x in range(8):
                whole_ref[at, x * 128 : (x + 1) * 128] = whole[x * 32 : (x + 1) * 32, lanes]
            for x in range(4):
                rest_ref[at, x * 128 : (x + 1) * 128] = rest[x * 32 : (x + 1) * 32, lanes]
        return carry

    lax.fori_loop(0, 8, strips, 0)

    def place(i, carry):
        at = pl.ds(pl.multiple_of(i * CHUNK, CHUNK), CHUNK)
        pick = pick_ref[at, :]
        picked = dot(pick, whole_ref[...]).astype(BF16)
        out_ref[at, 0:1024] = dot(picked, once_ref[...]).astype(BF16)
        picked = dot(pick, rest_ref[...]).astype(BF16)
        out_ref[at, 1024:1536] = dot(picked, pair_ref[...]).astype(BF16)
        return carry

    lax.fori_loop(0, 512 // CHUNK, place, 0)


CUT_SCRATCH = [
    pltpu.VMEM((1024, 1024), BF16),
    pltpu.VMEM((512, 512), BF16),
    pltpu.VMEM((256, 256), BF16),
    pltpu.VMEM((512, 1024), BF16),
    pltpu.VMEM((512, 512), BF16),
]


def old_kernel(field_hbm, anchor_ref, dest_ref, out_ref, pick_ref, field_ref, sem, *scratch):
    fetch = pltpu.make_async_copy(field_hbm, field_ref, sem)
    fetch.start()
    selections(*scratch[:3])
    target = dest_ref[...].astype(F32)
    wide = jnp.broadcast_to(target, (256, 256))
    row, col = iota((256, 256), 0), iota((256, 256), 1)
    tall = jnp.sum(jnp.where(row == col, wide, 0.0), axis=1, keepdims=True)
    ahead = jnp.where((tall == wide) & (row < col), 1.0, 0.0)
    slot = target * 16.0 + jnp.sum(ahead, axis=0, keepdims=True)
    patch = ((anchor_ref[1] >> 3) & 15) * 32 + ((anchor_ref[2] >> 3) & 31)
    row = iota((512, 256), 0)
    sent = jnp.where(row == slot.astype(jnp.int32), 1.0, 0.0)
    taken = jnp.where(row == patch, 1.0, 0.0).astype(BF16)
    pick_ref[...] = dot(sent.astype(BF16), taken, (1, 1)).astype(BF16)
    tag = jnp.sum(sent, axis=1, keepdims=True)
    out_ref[:, 1536:1664] = jnp.broadcast_to(tag, (512, 128)).astype(BF16)
    fetch.wait()

    def load(by):
        at = pl.ds(pl.multiple_of(by * 8, 8), 8)
        return field_ref[:, :, at, :].reshape(192, 256)

    cut_patches(load, pick_ref, out_ref, *scratch)


def new_kernel(
    field_hbm, z_prev_ref, z_next_ref, y_prev_ref, y_next_ref, pick_ref,
    new_hbm, out_ref, pad_ref, new_ref, sem, *scratch,
):
    fetch = pltpu.make_async_copy(field_hbm, pad_ref.at[:, 1:9, 8:136, :], sem.at[0])
    fetch.start()
    selections(*scratch[:3])
    pad_ref[:, 0:1, 8:136, :] = z_prev_ref[...]
    pad_ref[:, 9:10, 8:136, :] = z_next_ref[...]
    pad_ref[:, 1:9, 7:8, :] = y_prev_ref[...]
    pad_ref[:, 1:9, 136:137, :] = y_next_ref[...]
    fetch.wait()
    near = VISCOSITY * TIME_STEP

    def layer(z, carry):
        for y in range(0, 128, 32):
            along = [pad_ref[c, z + 1, 8 + y : 40 + y, :] for c in range(3)]
            drift = [(0.5 * TIME_STEP) * v for v in along]
            ahead = [near - v for v in drift]
            behind = [near + v for v in drift]
            for c in range(3):
                centre = along[c]
                z_next = pad_ref[c, z + 2, 8 + y : 40 + y, :]
                z_prev = pad_ref[c, z, 8 + y : 40 + y, :]
                y_next = pad_ref[c, z + 1, 9 + y : 41 + y, :]
                y_prev = pad_ref[c, z + 1, 7 + y : 39 + y, :]
                x_next = pltpu.roll(centre, 255, 1)
                x_prev = pltpu.roll(centre, 1, 1)
                new_ref[c, z, y : y + 32, :] = (
                    (1.0 - 6.0 * near) * centre
                    + (ahead[0] * x_next + behind[0] * x_prev)
                    + (ahead[1] * y_next + behind[1] * y_prev)
                    + (ahead[2] * z_next + behind[2] * z_prev)
                )
        return carry

    lax.fori_loop(0, 8, layer, 0)
    store = pltpu.make_async_copy(new_ref, new_hbm, sem.at[1])
    store.start()

    def load(by):
        at = pl.ds(pl.multiple_of(by * 8, 8), 8)
        return new_ref[:, :, at, :].reshape(192, 256)

    cut_patches(load, pick_ref, out_ref, *scratch)
    store.wait()


def pack(blocks):
    row, col = iota((128, 128), 0), iota((128, 128), 1)
    return jnp.where(row // 64 == col // 64, blocks[0], pltpu.roll(blocks[1], 64, 1))


def unpack(packed):
    row, col = iota((128, 128), 0), iota((128, 128), 1)
    own = row // 64 == col // 64
    return jnp.where(own, packed, 0.0), jnp.where(own, pltpu.roll(packed, 64, 1), 0.0)


def absolute(m, j):
    return pl.multiple_of(((m - j) & 3) * 128, 128)


def forward_kernel(
    place_ref, old_ref, lift_w_ref, w0_ref, w1_ref, w2_ref, w3_ref,
    lifted_ref, query_ref, key_ref, key_spread_ref, value_ref, value_spread_ref,
    query_w_ref, key_w_ref, value_w_ref, out_w_ref, sums_ref, acc_ref,
):
    m = place_ref[0]
    for j, block in enumerate((w0_ref, w1_ref, w2_ref, w3_ref)):
        at = pl.ds(absolute(m, j), 128)
        query_w_ref[:, at] = block[0]
        key_w_ref[:, at] = block[1]
        value_w_ref[:, at] = block[2]
        for k in range(4):
            out_w_ref[at, k * 128 : (k + 1) * 128] = block[3, k * 128 : (k + 1) * 128, :]
    acc_ref[...] = jnp.zeros_like(acc_ref)
    mix = mean_matrix()

    def rows(i, carry):
        at = pl.ds(pl.multiple_of(i * CHUNK, CHUNK), CHUNK)
        lifted = dot(old_ref[at, 0:1536], lift_w_ref[...]).astype(BF16)
        lifted_ref[at, :] = lifted
        query_ref[at, :] = dot(lifted, query_w_ref[...]).astype(BF16)
        normed = []
        for w_ref, hat_ref, spread_ref in (
            (key_w_ref, key_ref, key_spread_ref),
            (value_w_ref, value_ref, value_spread_ref),
        ):
            heads = dot(lifted, w_ref[...])
            shifted = heads - head_mean(heads, mix)
            spread = jnp.sqrt(head_mean(shifted * shifted, mix) + EPSILON)
            hat = shifted / spread
            normed.append(hat.astype(BF16))
            hat_ref[at, :] = normed[-1]
            spread_ref[at, :] = spread
        for p in range(4):
            part = slice(p * 128, (p + 1) * 128)
            acc_ref[p] += dot(normed[0][:, part], normed[1][:, part], (0, 0))
        return carry

    lax.fori_loop(0, 512 // CHUNK, rows, 0)
    sums_ref[0:128, :] = pack((acc_ref[0], acc_ref[1]))
    sums_ref[128:256, :] = pack((acc_ref[2], acc_ref[3]))
    count = jnp.sum(old_ref[:, 1536:1664].astype(F32), axis=0, keepdims=True)
    sums_ref[256:264, :] = jnp.broadcast_to(count, (8, 128))


def dealer(place_ref, mine_ref, theirs_ref):
    first = place_ref[1] == 0

    def deal(grad, rows, n, at):
        grad = grad.reshape(16, 2, rows, 128)
        even, odd = grad[:, 0], grad[:, 1]
        mine_ref[:, n, at : at + rows, :] = jnp.where(first, even, odd).astype(BF16)
        theirs_ref[:, n, at : at + rows, :] = jnp.where(first, odd, even).astype(BF16)

    return deal


def middle_kernel(
    place_ref, s0_ref, s1_ref, s2_ref, s3_ref, lifted_ref, query_ref, new_ref, out_w_ref, proj_w_ref,
    mine_ref, theirs_ref, d_query_ref, d_hidden_ref, sums_ref, count_ref,
    hidden_ref, d_guess_ref, attended_ref, d_tokens_ref, acc_ref, high_ref, low_ref, loss_ref,
):
    total = (s0_ref[...] + s1_ref[...]) + (s2_ref[...] + s3_ref[...])
    count = total[256:264, :]
    count_ref[...] = count
    for p in range(2):
        blocks = unpack(total[p * 128 : (p + 1) * 128] / count[0:1, :])
        for q in range(2):
            high_ref[2 * p + q], low_ref[2 * p + q] = split(blocks[q])
    acc_ref[...] = jnp.zeros_like(acc_ref)
    loss_ref[...] = jnp.zeros_like(loss_ref)

    def rows(i, carry):
        at = pl.ds(pl.multiple_of(i * CHUNK, CHUNK), CHUNK)
        query = query_ref[at, :]
        parts = []
        for p in range(4):
            part = query[:, p * 128 : (p + 1) * 128]
            parts.append(dot(part, high_ref[p]) + dot(part, low_ref[p]))
        attended = jnp.concatenate(parts, axis=1).astype(BF16)
        attended_ref[at, :] = attended
        mixed = dot(attended, out_w_ref[...])
        hidden = (lifted_ref[at, :].astype(F32) + mixed).astype(BF16)
        hidden_ref[at, :] = hidden
        error = dot(hidden, proj_w_ref[...]) - new_ref[at, :].astype(F32)
        loss_ref[...] += jnp.sum((error * error).reshape(CHUNK // 8, 8, 1536), axis=0)
        d_guess = (error * (1.0 / 32768)).astype(BF16)
        d_guess_ref[at, :] = d_guess
        d_hidden = dot(d_guess, proj_w_ref[...], (1, 1))
        d_hidden_ref[at, :] = d_hidden
        d_tokens = d_hidden.astype(BF16)
        d_tokens_ref[at, :] = d_tokens
        high, low = split(dot(d_tokens, out_w_ref[...], (1, 1)))
        for p in range(4):
            part = slice(p * 128, (p + 1) * 128)
            back = (
                dot(high[:, part], high_ref[p], (1, 1))
                + dot(high[:, part], low_ref[p], (1, 1))
                + dot(low[:, part], high_ref[p], (1, 1))
            )
            d_query_ref[at, part] = back.astype(BF16)
            acc_ref[p] += dot(query[:, part], high[:, part], (0, 0)) + dot(
                query[:, part], low[:, part], (0, 0)
            )
        return carry

    lax.fori_loop(0, 512 // CHUNK, rows, 0)
    sums_ref[0:128, :] = pack((acc_ref[0], acc_ref[1]))
    sums_ref[128:256, :] = pack((acc_ref[2], acc_ref[3]))
    loss = jnp.sum(loss_ref[...], axis=(0, 1), keepdims=True) * (1.0 / 50331648)
    sums_ref[256:264, :] = jnp.broadcast_to(loss, (8, 128))
    deal = dealer(place_ref, mine_ref, theirs_ref)
    grad = dot(hidden_ref[...], d_guess_ref[...], (0, 0))
    for n in range(4):
        for j in range(3):
            at = n * 384 + j * 128
            deal(grad[:, at : at + 128], 16, n, 16 * j)
    grad = dot(d_tokens_ref[...], attended_ref[...], (0, 0))
    for n in range(4):
        deal(grad[:, n * 128 : (n + 1) * 128], 16, n, 48)


def backward_kernel(
    place_ref, s0_ref, s1_ref, s2_ref, s3_ref, count_ref, old_hbm, lifted_ref, key_ref, key_spread_ref,
    value_ref, value_spread_ref, d_query_ref, d_hidden_ref, query_w_ref, key_w_ref, value_w_ref,
    mine_ref, theirs_ref, loss_ref, high_ref, low_ref, d_heads_ref, d_lifted_ref, old_ref, sem,
):
    fetch = pltpu.make_async_copy(old_hbm.at[:, 0:1536], old_ref, sem)
    fetch.start()
    total = (s0_ref[...] + s1_ref[...]) + (s2_ref[...] + s3_ref[...])
    loss_ref[...] = total[256:264, :]
    for p in range(2):
        blocks = unpack(total[p * 128 : (p + 1) * 128] / count_ref[0:1, :])
        for q in range(2):
            high_ref[2 * p + q], low_ref[2 * p + q] = split(blocks[q])
    mix = mean_matrix()

    def rows(i, carry):
        at = pl.ds(pl.multiple_of(i * CHUNK, CHUNK), CHUNK)
        d_query = d_query_ref[at, :]
        d_heads_ref[at, 0:512] = d_query
        d_lifted = d_hidden_ref[at, :] + dot(d_query, query_w_ref[...], (1, 1))
        for hat_ref, spread_ref, other_ref, across, lanes, w_ref in (
            (key_ref, key_spread_ref, value_ref, (1, 1), 512, key_w_ref),
            (value_ref, value_spread_ref, key_ref, (1, 0), 1024, value_w_ref),
        ):
            other = other_ref[at, :]
            parts = []
            for p in range(4):
                part = other[:, p * 128 : (p + 1) * 128]
                parts.append(dot(part, high_ref[p], across) + dot(part, low_ref[p], across))
            grad = jnp.concatenate(parts, axis=1)
            hat = hat_ref[at, :].astype(F32)
            inner = head_mean(grad, mix)
            cross = head_mean(grad * hat, mix)
            grad = ((grad - inner - hat * cross) / spread_ref[at, :]).astype(BF16)
            d_heads_ref[at, lanes : lanes + 512] = grad
            d_lifted = d_lifted + dot(grad, w_ref[...], (1, 1))
        d_lifted_ref[at, :] = d_lifted.astype(BF16)
        return carry

    lax.fori_loop(0, 512 // CHUNK, rows, 0)
    deal = dealer(place_ref, mine_ref, theirs_ref)
    grad = dot(lifted_ref[...], d_heads_ref[...], (0, 0))
    for n in range(4):
        for j in range(3):
            at = 512 * j + 128 * n
            deal(grad[:, at : at + 128], 16, n, 48 + 16 * j)
    fetch.wait()
    grad = dot(old_ref[...], d_lifted_ref[...], (0, 0))
    for n in range(4):
        deal(grad[:, n * 128 : (n + 1) * 128], 48, n, 0)


def last_kernel(
    place_ref, r0_ref, r1_ref, r2_ref, r3_ref, heads_ref,
    lift_ref, query_ref, key_ref, value_ref, out_ref, proj_ref, loss_ref,
):
    m = place_ref[0]
    for j, block in enumerate((r0_ref, r1_ref, r2_ref, r3_ref)):
        lift_ref[:, pl.ds(absolute(m, j), 128)] = block[0:48, :]
        for k in range(3):
            at = pl.multiple_of(((m - j) & 3) * 384 + k * 128, 128)
            proj_ref[:, pl.ds(at, 128)] = block[48 + 16 * k : 64 + 16 * k, :]
    query_ref[...] = heads_ref[:, 0:16, :].astype(F32).reshape(512, 128)
    key_ref[...] = heads_ref[:, 16:32, :].astype(F32).reshape(512, 128)
    value_ref[...] = heads_ref[:, 32:48, :].astype(F32).reshape(512, 128)
    out_ref[...] = heads_ref[:, 48:64, :].astype(F32).reshape(512, 128).T
    loss = jnp.sum(heads_ref[:, 64:80, :].astype(F32), axis=0)
    loss_ref[...] = loss[0:1, 0:1] + loss[1:2, 0:1]


def call(body, outs, scratch=(), ins="", results=None):
    spaces = {"s": pltpu.SMEM, "h": pl.ANY, "v": pltpu.VMEM}
    return pl.pallas_call(
        body,
        out_shape=[jax.ShapeDtypeStruct(shape, kind) for shape, kind in outs],
        in_specs=[pl.BlockSpec(memory_space=spaces[k]) for k in ins],
        out_specs=[pl.BlockSpec(memory_space=spaces[k]) for k in results or "v" * len(outs)],
        scratch_shapes=list(scratch),
        compiler_params=pltpu.CompilerParams(vmem_limit_bytes=60 << 20),
    )


def around(value):
    got = [value]
    for d in (1, 2, 3):
        got.append(lax.ppermute(value, "mp", [(i, (i + d) % 4) for i in range(4)]))
    return got


def exchange(value, axes):
    return lax.all_to_all(value, axes, split_axis=0, concat_axis=0, tiled=True)


def pair_sum(mine, theirs):
    got = lax.ppermute(theirs, "slab", [(i, i ^ 1) for i in range(32)])
    return (mine.astype(F32) + got.astype(F32)).astype(BF16)


def total(partial):
    groups = [[(2 * q + c) * 4 + n for q in range(16) for n in range(4)] for c in range(2)]
    got = lax.all_to_all(
        partial.reshape(64, -1, 128),
        ("slab", "mp"),
        split_axis=0,
        concat_axis=0,
        axis_index_groups=groups,
        tiled=True,
    )
    return jnp.sum(got.astype(F32), axis=0)


def step(velocity, anchors, dest, w_lift, w_query, w_key, w_value, w_out, w_proj):
    slabs = lax.axis_size("slab")
    place = jnp.stack([lax.axis_index("mp"), lax.axis_index("slab") & 1])
    up = [(i, (i + 1) % slabs) for i in range(slabs)]
    z_prev = lax.ppermute(velocity[:, 7:8], "slab", up)
    z_next = lax.ppermute(velocity[:, 0:1], "slab", [(j, i) for i, j in up])
    up = [(i, (i + 1) % 4) for i in range(4)]
    y_prev = lax.ppermute(velocity[:, :, 127:128], "mp", up)
    y_next = lax.ppermute(velocity[:, :, 0:1], "mp", [(j, i) for i, j in up])
    tall = jnp.concatenate([w_out[:, k * 128 : (k + 1) * 128] for k in range(4)], axis=0)
    heads_w = around(jnp.stack([w_query, w_key, w_value, tall]))

    send_old, pick = call(
        old_kernel,
        [((512, 1664), BF16), ((512, 512), BF16)],
        [pltpu.VMEM((3, 8, 128, 256), F32), pltpu.SemaphoreType.DMA] + CUT_SCRATCH,
        "hvv",
    )(velocity, anchors.reshape(3, 1, 256), dest.reshape(1, 256))
    old = exchange(send_old, "slab")
    new_velocity, send_new = call(
        new_kernel,
        [((3, 8, 128, 256), F32), ((512, 1536), BF16)],
        [
            pltpu.VMEM((3, 10, 144, 256), F32),
            pltpu.VMEM((3, 8, 128, 256), F32),
            pltpu.SemaphoreType.DMA((2,)),
        ]
        + CUT_SCRATCH,
        "hvvvvv",
        "hv",
    )(velocity, z_prev, z_next, y_prev, y_next, pick)
    new = exchange(send_new, "slab")

    wide, wide_f = ((512, 512), BF16), ((512, 512), F32)
    lifted, query, key, key_spread, value, value_spread, wq, wk, wv, wo, sums = call(
        forward_kernel,
        [wide, wide, wide, wide_f, wide, wide_f, wide, wide, wide, wide, ((264, 128), F32)],
        [pltpu.VMEM((4, 128, 128), F32)],
        "svvvvvv",
    )(place, old, w_lift, *heads_w)
    sums = around(sums)
    mine, theirs, d_query, d_hidden, d_sums, count = call(
        middle_kernel,
        [((16, 4, 64, 128), BF16), ((16, 4, 64, 128), BF16), wide, wide_f, ((264, 128), F32), ((8, 128), F32)],
        [
            pltpu.VMEM((512, 512), BF16),
            pltpu.VMEM((512, 1536), BF16),
            pltpu.VMEM((512, 512), BF16),
            pltpu.VMEM((512, 512), BF16),
            pltpu.VMEM((4, 128, 128), F32),
            pltpu.VMEM((4, 128, 128), BF16),
            pltpu.VMEM((4, 128, 128), BF16),
            pltpu.VMEM((8, 1536), F32),
        ],
        "svvvvvvvvv",
    )(place, *sums, lifted, query, new, wo, w_proj)
    d_sums = around(d_sums)
    total_out = total(pair_sum(mine, theirs))
    mine, theirs, loss_part = call(
        backward_kernel,
        [((16, 4, 96, 128), BF16), ((16, 4, 96, 128), BF16), ((8, 128), F32)],
        [
            pltpu.VMEM((4, 128, 128), BF16),
            pltpu.VMEM((4, 128, 128), BF16),
            pltpu.VMEM((512, 1536), BF16),
            pltpu.VMEM((512, 512), BF16),
            pltpu.VMEM((512, 1536), BF16),
            pltpu.SemaphoreType.DMA,
        ],
        "svvvvvhvvvvvvvvvv",
    )(place, *d_sums, count, old, lifted, key, key_spread, value, value_spread, d_query, d_hidden, wq, wk, wv)
    total_in = total(pair_sum(mine, theirs))
    blocks = jnp.concatenate([total_in[0:48], total_out[0:48]], axis=0)
    loss_high = loss_part.astype(BF16)
    loss_low = (loss_part - loss_high.astype(F32)).astype(BF16)
    heads = jnp.concatenate([total_in[48:96], total_out[48:64]], axis=0).astype(BF16)
    heads = jnp.concatenate([heads, loss_high[0:1], loss_low[0:1], jnp.zeros((14, 128), BF16)], axis=0)
    heads = exchange(jnp.broadcast_to(heads[None], (32, 80, 128)), "slab")
    lift, g_query, g_key, g_value, g_out, proj, loss = call(
        last_kernel,
        [
            ((48, 512), F32),
            ((512, 128), F32),
            ((512, 128), F32),
            ((512, 128), F32),
            ((128, 512), F32),
            ((16, 1536), F32),
            ((1, 1), F32),
        ],
        (),
        "svvvvv",
    )(place, *around(blocks), heads)
    return (new_velocity, loss.reshape(()), lift, g_query, g_key, g_value, g_out, proj)


def solution(mesh):
    return jax.shard_map(
        step,
        mesh=mesh,
        in_specs=(
            P(None, "slab", "mp", None),
            P(None, "slab", "mp", None),
            P("slab", "mp", None, None),
            P(),
            P(None, "mp"),
            P(None, "mp"),
            P(None, "mp"),
            P("mp", None),
            P(),
        ),
        out_specs=(
            P(None, "slab", "mp", None),
            P(),
            P("slab", None),
            P(None, "mp"),
            P(None, "mp"),
            P(None, "mp"),
            P("mp", None),
            P("slab", None),
        ),
        check_vma=False,
    )
```

```python
import jax
import jax.numpy as jnp
from jax import lax
from jax.experimental import pallas as pl
from jax.experimental.pallas import tpu as pltpu
from jax.sharding import PartitionSpec as P


TIME_STEP = 0.1
VISCOSITY = 0.2
EPSILON = 1e-05
F32 = jnp.float32
BF16 = jnp.bfloat16
CHUNK = 256
UNROLL = 2


def iota(shape, dim):
    return lax.broadcasted_iota(jnp.int32, shape, dim)


def dot(a, b, contract=(1, 0)):
    dims = (((contract[0],), (contract[1],)), ((), ()))
    return lax.dot_general(a, b, dims, preferred_element_type=F32)


def split(a):
    high = a.astype(BF16)
    return high, (a - high.astype(F32)).astype(BF16)


def head_mean(a, mix):
    high, low = split(a)
    halves = [
        dot(high[:, at : at + 256], mix) + dot(low[:, at : at + 256], mix) for at in (0, 256)
    ]
    return jnp.concatenate(halves, axis=1)


def mean_matrix():
    same = iota((256, 256), 0) // 64 == iota((256, 256), 1) // 64
    return jnp.where(same, 1.0 / 64, 0.0).astype(BF16)


def selections(once_ref, pair_ref, turn_ref):
    row, col = iota((256, 256), 0), iota((256, 256), 1)
    turn_ref[...] = jnp.where(col == (row & 31) * 8 + (row >> 5), 1.0, 0.0).astype(BF16)

    def spread(i, carry):
        at = pl.ds(pl.multiple_of(i * 128, 128), 128)
        row, col = iota((128, 1024), 0), iota((128, 1024), 1)
        once_ref[at, :] = jnp.where(col == 8 * row + i, 1.0, 0.0).astype(BF16)
        return carry

    lax.fori_loop(0, 8, spread, 0)
    row, col = iota((512, 512), 0), iota((512, 512), 1)
    pair_ref[...] = jnp.where(col == 8 * (row & 63) + (row >> 6), 1.0, 0.0).astype(BF16)


def cut_patches(load, pick_ref, slot_ref, out_ref, once_ref, pair_ref, turn_ref, whole_ref, rest_ref):
    row, col = iota((128, 256), 0), iota((128, 256), 1)
    turn_pair = jnp.where(col == (row & 31) * 8 + 2 * (row >> 5), 1.0, 0.0).astype(BF16)

    def strips(i, carry):
        cells = [load(2 * i), load(2 * i + 1)]
        first = jnp.concatenate([c[:128] for c in cells], axis=0).astype(BF16)
        last = [c[128:] for c in cells]
        last = [jnp.concatenate([c, pltpu.roll(c, 255, 1)], axis=0) for c in last]
        last = jnp.concatenate(last, axis=0).astype(BF16)
        whole = dot(turn_ref[...], first, (1, 1)).astype(BF16)
        rest = dot(turn_pair, last, (1, 1)).astype(BF16)
        for k in range(2):
            at = pl.ds(pl.multiple_of(i * 64 + k * 32, 32), 32)
            lanes = slice(k * 128, (k + 1) * 128)
            for x in range(8):
                whole_ref[at, x * 128 : (x + 1) * 128] = whole[x * 32 : (x + 1) * 32, lanes]
            for x in range(4):
                rest_ref[at, x * 128 : (x + 1) * 128] = rest[x * 32 : (x + 1) * 32, lanes]
        return carry

    lax.fori_loop(0, 8, strips, 0, unroll=UNROLL)

    for part_ref, turn_back_ref, lanes in (
        (whole_ref, once_ref, slice(0, 1024)),
        (rest_ref, pair_ref, slice(1024, 1536)),
    ):
        picked = dot(pick_ref[...], part_ref[...]).astype(BF16)
        picked = dot(picked, turn_back_ref[...]).astype(BF16)
        out_ref[:, lanes] = dot(slot_ref[...], picked).astype(BF16)


CUT_SCRATCH = [
    pltpu.VMEM((1024, 1024), BF16),
    pltpu.VMEM((512, 512), BF16),
    pltpu.VMEM((256, 256), BF16),
    pltpu.VMEM((512, 1024), BF16),
    pltpu.VMEM((512, 512), BF16),
]


def old_kernel(field_hbm, anchor_ref, dest_ref, out_ref, pick_ref, slot_ref, field_ref, sem, *scratch):
    fetch = pltpu.make_async_copy(field_hbm, field_ref, sem)
    fetch.start()
    selections(*scratch[:3])
    target = dest_ref[...].astype(F32)
    row, col = iota((256, 256), 0), iota((256, 256), 1)

    def upright(line):
        return jnp.sum(jnp.where(row == col, jnp.broadcast_to(line, (256, 256)), 0.0), axis=1, keepdims=True)

    ahead = jnp.where((upright(target) == target) & (row < col), 1.0, 0.0)
    slot = target * 16.0 + jnp.sum(ahead, axis=0, keepdims=True)
    patch = ((anchor_ref[1] >> 3) & 15) * 32 + ((anchor_ref[2] >> 3) & 31)
    patch = upright(patch.astype(F32)).astype(jnp.int32)
    pick_ref[...] = jnp.where(iota((256, 512), 1) == patch, 1.0, 0.0).astype(BF16)
    sent = jnp.where(iota((512, 256), 0) == slot.astype(jnp.int32), 1.0, 0.0)
    slot_ref[...] = sent.astype(BF16)
    tag = jnp.sum(sent, axis=1, keepdims=True)
    out_ref[:, 1536:1664] = jnp.broadcast_to(tag, (512, 128)).astype(BF16)
    fetch.wait()

    def load(by):
        at = pl.ds(pl.multiple_of(by * 8, 8), 8)
        return field_ref[:, :, at, :].reshape(192, 256)

    cut_patches(load, pick_ref, slot_ref, out_ref, *scratch)


def new_kernel(
    field_hbm, z_prev_ref, z_next_ref, y_prev_ref, y_next_ref, pick_ref, slot_ref,
    new_hbm, out_ref, pad_ref, new_ref, sem, *scratch,
):
    fetch = pltpu.make_async_copy(field_hbm, pad_ref.at[:, 1:9, 8:136, :], sem.at[0])
    fetch.start()
    selections(*scratch[:3])
    pad_ref[:, 0:1, 8:136, :] = z_prev_ref[...]
    pad_ref[:, 9:10, 8:136, :] = z_next_ref[...]
    pad_ref[:, 1:9, 7:8, :] = y_prev_ref[...]
    pad_ref[:, 1:9, 136:137, :] = y_next_ref[...]
    fetch.wait()
    near = VISCOSITY * TIME_STEP

    def layer(z, carry):
        for y in range(0, 128, 32):
            along = [pad_ref[c, z + 1, 8 + y : 40 + y, :] for c in range(3)]
            drift = [(0.5 * TIME_STEP) * v for v in along]
            ahead = [near - v for v in drift]
            behind = [near + v for v in drift]
            for c in range(3):
                centre = along[c]
                z_next = pad_ref[c, z + 2, 8 + y : 40 + y, :]
                z_prev = pad_ref[c, z, 8 + y : 40 + y, :]
                y_next = pad_ref[c, z + 1, 9 + y : 41 + y, :]
                y_prev = pad_ref[c, z + 1, 7 + y : 39 + y, :]
                x_next = pltpu.roll(centre, 255, 1)
                x_prev = pltpu.roll(centre, 1, 1)
                new_ref[c, z, y : y + 32, :] = (
                    (1.0 - 6.0 * near) * centre
                    + (ahead[0] * x_next + behind[0] * x_prev)
                    + (ahead[1] * y_next + behind[1] * y_prev)
                    + (ahead[2] * z_next + behind[2] * z_prev)
                )
        return carry

    lax.fori_loop(0, 8, layer, 0)
    store = pltpu.make_async_copy(new_ref, new_hbm, sem.at[1])
    store.start()

    def load(by):
        at = pl.ds(pl.multiple_of(by * 8, 8), 8)
        return new_ref[:, :, at, :].reshape(192, 256)

    cut_patches(load, pick_ref, slot_ref, out_ref, *scratch)
    store.wait()


def pack(blocks):
    row, col = iota((128, 128), 0), iota((128, 128), 1)
    return jnp.where(row // 64 == col // 64, blocks[0], pltpu.roll(blocks[1], 64, 1))


def unpack(packed):
    row, col = iota((128, 128), 0), iota((128, 128), 1)
    own = row // 64 == col // 64
    return jnp.where(own, packed, 0.0), jnp.where(own, pltpu.roll(packed, 64, 1), 0.0)


def absolute(m, j):
    return pl.multiple_of(((m - j) & 3) * 128, 128)


def forward_kernel(
    place_ref, old_ref, lift_w_ref, w0_ref, w1_ref, w2_ref, w3_ref,
    lifted_ref, query_ref, key_ref, key_spread_ref, value_ref, value_spread_ref,
    query_w_ref, key_w_ref, value_w_ref, out_w_ref, sums_ref, acc_ref,
):
    m = place_ref[0]
    for j, block in enumerate((w0_ref, w1_ref, w2_ref, w3_ref)):
        at = pl.ds(absolute(m, j), 128)
        query_w_ref[:, at] = block[0]
        key_w_ref[:, at] = block[1]
        value_w_ref[:, at] = block[2]
        for k in range(4):
            out_w_ref[at, k * 128 : (k + 1) * 128] = block[3, k * 128 : (k + 1) * 128, :]
    acc_ref[...] = jnp.zeros_like(acc_ref)
    mix = mean_matrix()

    def rows(i, carry):
        at = pl.ds(pl.multiple_of(i * CHUNK, CHUNK), CHUNK)
        lifted = dot(old_ref[at, 0:1536], lift_w_ref[...]).astype(BF16)
        lifted_ref[at, :] = lifted
        query_ref[at, :] = dot(lifted, query_w_ref[...]).astype(BF16)
        normed = []
        for w_ref, hat_ref, spread_ref in (
            (key_w_ref, key_ref, key_spread_ref),
            (value_w_ref, value_ref, value_spread_ref),
        ):
            heads = dot(lifted, w_ref[...])
            shifted = heads - head_mean(heads, mix)
            spread = jnp.sqrt(head_mean(shifted * shifted, mix) + EPSILON)
            hat = shifted / spread
            normed.append(hat.astype(BF16))
            hat_ref[at, :] = normed[-1]
            spread_ref[at, :] = spread
        for p in range(4):
            part = slice(p * 128, (p + 1) * 128)
            acc_ref[p] += dot(normed[0][:, part], normed[1][:, part], (0, 0))
        return carry

    lax.fori_loop(0, 512 // CHUNK, rows, 0)
    sums_ref[0:128, :] = pack((acc_ref[0], acc_ref[1]))
    sums_ref[128:256, :] = pack((acc_ref[2], acc_ref[3]))
    count = jnp.sum(old_ref[:, 1536:1664].astype(F32), axis=0, keepdims=True)
    sums_ref[256:264, :] = jnp.broadcast_to(count, (8, 128))


def dealer(place_ref, mine_ref, theirs_ref):
    first = place_ref[1] == 0

    def deal(grad, rows, n, at):
        grad = grad.reshape(16, 2, rows, 128)
        even, odd = grad[:, 0], grad[:, 1]
        mine_ref[:, n, at : at + rows, :] = jnp.where(first, even, odd).astype(BF16)
        theirs_ref[:, n, at : at + rows, :] = jnp.where(first, odd, even).astype(BF16)

    return deal


def middle_kernel(
    s0_ref, s1_ref, s2_ref, s3_ref, lifted_ref, query_ref, new_ref, out_w_ref, proj_w_ref,
    hidden_ref, d_guess_ref, attended_ref, d_tokens_ref, d_query_ref, d_hidden_ref, sums_ref, count_ref,
    acc_ref, high_ref, low_ref, loss_ref,
):
    total = (s0_ref[...] + s1_ref[...]) + (s2_ref[...] + s3_ref[...])
    count = total[256:264, :]
    count_ref[...] = count
    for p in range(2):
        blocks = unpack(total[p * 128 : (p + 1) * 128] / count[0:1, :])
        for q in range(2):
            high_ref[2 * p + q], low_ref[2 * p + q] = split(blocks[q])
    acc_ref[...] = jnp.zeros_like(acc_ref)
    loss_ref[...] = jnp.zeros_like(loss_ref)

    def rows(i, carry):
        at = pl.ds(pl.multiple_of(i * CHUNK, CHUNK), CHUNK)
        query = query_ref[at, :]
        parts = []
        for p in range(4):
            part = query[:, p * 128 : (p + 1) * 128]
            parts.append(dot(part, high_ref[p]) + dot(part, low_ref[p]))
        attended = jnp.concatenate(parts, axis=1).astype(BF16)
        attended_ref[at, :] = attended
        mixed = dot(attended, out_w_ref[...])
        hidden = (lifted_ref[at, :].astype(F32) + mixed).astype(BF16)
        hidden_ref[at, :] = hidden
        error = dot(hidden, proj_w_ref[...]) - new_ref[at, :].astype(F32)
        loss_ref[...] += jnp.sum((error * error).reshape(CHUNK // 8, 8, 1536), axis=0)
        d_guess = (error * (1.0 / 32768)).astype(BF16)
        d_guess_ref[at, :] = d_guess
        d_hidden = dot(d_guess, proj_w_ref[...], (1, 1))
        d_hidden_ref[at, :] = d_hidden
        d_tokens = d_hidden.astype(BF16)
        d_tokens_ref[at, :] = d_tokens
        high, low = split(dot(d_tokens, out_w_ref[...], (1, 1)))
        for p in range(4):
            part = slice(p * 128, (p + 1) * 128)
            back = (
                dot(high[:, part], high_ref[p], (1, 1))
                + dot(high[:, part], low_ref[p], (1, 1))
                + dot(low[:, part], high_ref[p], (1, 1))
            )
            d_query_ref[at, part] = back.astype(BF16)
            acc_ref[p] += dot(query[:, part], high[:, part], (0, 0)) + dot(
                query[:, part], low[:, part], (0, 0)
            )
        return carry

    lax.fori_loop(0, 512 // CHUNK, rows, 0)
    sums_ref[0:128, :] = pack((acc_ref[0], acc_ref[1]))
    sums_ref[128:256, :] = pack((acc_ref[2], acc_ref[3]))
    loss = jnp.sum(loss_ref[...], axis=(0, 1), keepdims=True) * (1.0 / 50331648)
    sums_ref[256:264, :] = jnp.broadcast_to(loss, (8, 128))


def product_kernel(place_ref, hidden_ref, d_guess_ref, attended_ref, d_tokens_ref, mine_ref, theirs_ref):
    deal = dealer(place_ref, mine_ref, theirs_ref)
    grad = dot(hidden_ref[...], d_guess_ref[...], (0, 0))
    for n in range(4):
        for j in range(3):
            at = n * 384 + j * 128
            deal(grad[:, at : at + 128], 16, n, 16 * j)
    grad = dot(d_tokens_ref[...], attended_ref[...], (0, 0))
    for n in range(4):
        deal(grad[:, n * 128 : (n + 1) * 128], 16, n, 48)


def backward_kernel(
    place_ref, s0_ref, s1_ref, s2_ref, s3_ref, count_ref, old_hbm, lifted_ref, key_ref, key_spread_ref,
    value_ref, value_spread_ref, d_query_ref, d_hidden_ref, query_w_ref, key_w_ref, value_w_ref,
    mine_ref, theirs_ref, loss_ref, high_ref, low_ref, d_heads_ref, d_lifted_ref, old_ref, sem,
):
    fetch = pltpu.make_async_copy(old_hbm.at[:, 0:1536], old_ref, sem)
    fetch.start()
    total = (s0_ref[...] + s1_ref[...]) + (s2_ref[...] + s3_ref[...])
    loss_ref[...] = total[256:264, :]
    for p in range(2):
        blocks = unpack(total[p * 128 : (p + 1) * 128] / count_ref[0:1, :])
        for q in range(2):
            high_ref[2 * p + q], low_ref[2 * p + q] = split(blocks[q])
    mix = mean_matrix()

    def rows(i, carry):
        at = pl.ds(pl.multiple_of(i * CHUNK, CHUNK), CHUNK)
        d_query = d_query_ref[at, :]
        d_heads_ref[at, 0:512] = d_query
        d_lifted = d_hidden_ref[at, :] + dot(d_query, query_w_ref[...], (1, 1))
        for hat_ref, spread_ref, other_ref, across, lanes, w_ref in (
            (key_ref, key_spread_ref, value_ref, (1, 1), 512, key_w_ref),
            (value_ref, value_spread_ref, key_ref, (1, 0), 1024, value_w_ref),
        ):
            other = other_ref[at, :]
            parts = []
            for p in range(4):
                part = other[:, p * 128 : (p + 1) * 128]
                parts.append(dot(part, high_ref[p], across) + dot(part, low_ref[p], across))
            grad = jnp.concatenate(parts, axis=1)
            hat = hat_ref[at, :].astype(F32)
            inner = head_mean(grad, mix)
            cross = head_mean(grad * hat, mix)
            grad = ((grad - inner - hat * cross) / spread_ref[at, :]).astype(BF16)
            d_heads_ref[at, lanes : lanes + 512] = grad
            d_lifted = d_lifted + dot(grad, w_ref[...], (1, 1))
        d_lifted_ref[at, :] = d_lifted.astype(BF16)
        return carry

    lax.fori_loop(0, 512 // CHUNK, rows, 0)
    deal = dealer(place_ref, mine_ref, theirs_ref)
    grad = dot(lifted_ref[...], d_heads_ref[...], (0, 0))
    for n in range(4):
        for j in range(3):
            at = 512 * j + 128 * n
            deal(grad[:, at : at + 128], 16, n, 48 + 16 * j)
    fetch.wait()
    grad = dot(old_ref[...], d_lifted_ref[...], (0, 0))
    for n in range(4):
        deal(grad[:, n * 128 : (n + 1) * 128], 48, n, 0)


def merge_kernel(in_ref, in_got_ref, out_ref, out_got_ref, send_ref):
    send_ref[:, 0:96, :] = (in_ref[...].astype(F32) + in_got_ref[...].astype(F32)).astype(BF16)
    send_ref[:, 96:160, :] = (out_ref[...].astype(F32) + out_got_ref[...].astype(F32)).astype(BF16)


def merge(*parts):
    def block(rows):
        return pl.BlockSpec((16, rows, 128), lambda i: (i, 0, 0))

    return pl.pallas_call(
        merge_kernel,
        grid=(4,),
        out_shape=jax.ShapeDtypeStruct((64, 160, 128), BF16),
        in_specs=[block(96), block(96), block(64), block(64)],
        out_specs=block(160),
    )(*[part.reshape(64, -1, 128) for part in parts])


def last_kernel(
    place_ref, r0_ref, r1_ref, r2_ref, r3_ref, heads_ref,
    lift_ref, query_ref, key_ref, value_ref, out_ref, proj_ref, loss_ref,
):
    m = place_ref[0]
    for j, block in enumerate((r0_ref, r1_ref, r2_ref, r3_ref)):
        lift_ref[:, pl.ds(absolute(m, j), 128)] = block[0:48, :]
        for k in range(3):
            at = pl.multiple_of(((m - j) & 3) * 384 + k * 128, 128)
            proj_ref[:, pl.ds(at, 128)] = block[48 + 16 * k : 64 + 16 * k, :]
    query_ref[...] = heads_ref[:, 0:16, :].astype(F32).reshape(512, 128)
    key_ref[...] = heads_ref[:, 16:32, :].astype(F32).reshape(512, 128)
    value_ref[...] = heads_ref[:, 32:48, :].astype(F32).reshape(512, 128)
    out_ref[...] = heads_ref[:, 48:64, :].astype(F32).reshape(512, 128).T
    loss = jnp.sum(heads_ref[:, 64:80, :].astype(F32), axis=0)
    loss_ref[...] = loss[0:1, 0:1] + loss[1:2, 0:1]


def call(body, outs, scratch=(), ins="", results=None):
    spaces = {"s": pltpu.SMEM, "h": pl.ANY, "v": pltpu.VMEM}
    return pl.pallas_call(
        body,
        out_shape=[jax.ShapeDtypeStruct(shape, kind) for shape, kind in outs],
        in_specs=[pl.BlockSpec(memory_space=spaces[k]) for k in ins],
        out_specs=[pl.BlockSpec(memory_space=spaces[k]) for k in results or "v" * len(outs)],
        scratch_shapes=list(scratch),
        compiler_params=pltpu.CompilerParams(vmem_limit_bytes=60 << 20),
    )


def around(value):
    got = [value]
    for d in (1, 2, 3):
        got.append(lax.ppermute(value, "mp", [(i, (i + d) % 4) for i in range(4)]))
    return got


def exchange(value, axes):
    return lax.all_to_all(value, axes, split_axis=0, concat_axis=0, tiled=True)


def swap(theirs):
    return lax.ppermute(theirs, "slab", [(i, i ^ 1) for i in range(32)])


def total(partial):
    groups = [[(2 * q + c) * 4 + n for q in range(16) for n in range(4)] for c in range(2)]
    got = lax.all_to_all(
        partial, ("slab", "mp"), split_axis=0, concat_axis=0, axis_index_groups=groups, tiled=True
    )
    return jnp.sum(got.astype(F32), axis=0)


def step(velocity, anchors, dest, w_lift, w_query, w_key, w_value, w_out, w_proj):
    slabs = lax.axis_size("slab")
    place = jnp.stack([lax.axis_index("mp"), lax.axis_index("slab") & 1])
    up = [(i, (i + 1) % slabs) for i in range(slabs)]
    z_prev = lax.ppermute(velocity[:, 7:8], "slab", up)
    z_next = lax.ppermute(velocity[:, 0:1], "slab", [(j, i) for i, j in up])
    up = [(i, (i + 1) % 4) for i in range(4)]
    y_prev = lax.ppermute(velocity[:, :, 127:128], "mp", up)
    y_next = lax.ppermute(velocity[:, :, 0:1], "mp", [(j, i) for i, j in up])
    tall = jnp.concatenate([w_out[:, k * 128 : (k + 1) * 128] for k in range(4)], axis=0)
    heads_w = around(jnp.stack([w_query, w_key, w_value, tall]))

    send_old, pick, slot = call(
        old_kernel,
        [((512, 1664), BF16), ((256, 512), BF16), ((512, 256), BF16)],
        [pltpu.VMEM((3, 8, 128, 256), F32), pltpu.SemaphoreType.DMA] + CUT_SCRATCH,
        "hvv",
    )(velocity, anchors.reshape(3, 1, 256), dest.reshape(1, 256))
    old = exchange(send_old, "slab")
    new_velocity, send_new = call(
        new_kernel,
        [((3, 8, 128, 256), F32), ((512, 1536), BF16)],
        [
            pltpu.VMEM((3, 10, 144, 256), F32),
            pltpu.VMEM((3, 8, 128, 256), F32),
            pltpu.SemaphoreType.DMA((2,)),
        ]
        + CUT_SCRATCH,
        "hvvvvvv",
        "hv",
    )(velocity, z_prev, z_next, y_prev, y_next, pick, slot)
    new = exchange(send_new, "slab")

    wide, wide_f = ((512, 512), BF16), ((512, 512), F32)
    lifted, query, key, key_spread, value, value_spread, wq, wk, wv, wo, sums = call(
        forward_kernel,
        [wide, wide, wide, wide_f, wide, wide_f, wide, wide, wide, wide, ((264, 128), F32)],
        [pltpu.VMEM((4, 128, 128), F32)],
        "svvvvvv",
    )(place, old, w_lift, *heads_w)
    sums = around(sums)
    hidden, d_guess, attended, d_tokens, d_query, d_hidden, d_sums, count = call(
        middle_kernel,
        [wide, ((512, 1536), BF16), wide, wide, wide, wide_f, ((264, 128), F32), ((8, 128), F32)],
        [
            pltpu.VMEM((4, 128, 128), F32),
            pltpu.VMEM((4, 128, 128), BF16),
            pltpu.VMEM((4, 128, 128), BF16),
            pltpu.VMEM((8, 1536), F32),
        ],
        "vvvvvvvvv",
    )(*sums, lifted, query, new, wo, w_proj)
    d_sums = around(d_sums)
    mine_out, theirs_out = call(
        product_kernel, [((16, 4, 64, 128), BF16), ((16, 4, 64, 128), BF16)], (), "svvvv"
    )(place, hidden, d_guess, attended, d_tokens)
    got_out = swap(theirs_out)
    mine, theirs, loss_part = call(
        backward_kernel,
        [((16, 4, 96, 128), BF16), ((16, 4, 96, 128), BF16), ((8, 128), F32)],
        [
            pltpu.VMEM((4, 128, 128), BF16),
            pltpu.VMEM((4, 128, 128), BF16),
            pltpu.VMEM((512, 1536), BF16),
            pltpu.VMEM((512, 512), BF16),
            pltpu.VMEM((512, 1536), BF16),
            pltpu.SemaphoreType.DMA,
        ],
        "svvvvvhvvvvvvvvvv",
    )(place, *d_sums, count, old, lifted, key, key_spread, value, value_spread, d_query, d_hidden, wq, wk, wv)
    got = swap(theirs)
    partial = merge(mine, got, mine_out, got_out)
    sums = total(partial)
    blocks = jnp.concatenate([sums[0:48], sums[96:144]], axis=0)
    loss_high = loss_part.astype(BF16)
    loss_low = (loss_part - loss_high.astype(F32)).astype(BF16)
    heads = jnp.concatenate([sums[48:96], sums[144:160]], axis=0).astype(BF16)
    heads = jnp.concatenate([heads, loss_high[0:1], loss_low[0:1], jnp.zeros((14, 128), BF16)], axis=0)
    heads = exchange(jnp.broadcast_to(heads[None], (32, 80, 128)), "slab")
    lift, g_query, g_key, g_value, g_out, proj, loss = call(
        last_kernel,
        [
            ((48, 512), F32),
            ((512, 128), F32),
            ((512, 128), F32),
            ((512, 128), F32),
            ((128, 512), F32),
            ((16, 1536), F32),
            ((1, 1), F32),
        ],
        (),
        "svvvvv",
    )(place, *around(blocks), heads)
    return (new_velocity, loss.reshape(()), lift, g_query, g_key, g_value, g_out, proj)


def solution(mesh):
    return jax.shard_map(
        step,
        mesh=mesh,
        in_specs=(
            P(None, "slab", "mp", None),
            P(None, "slab", "mp", None),
            P("slab", "mp", None, None),
            P(),
            P(None, "mp"),
            P(None, "mp"),
            P(None, "mp"),
            P("mp", None),
            P(),
        ),
        out_specs=(
            P(None, "slab", "mp", None),
            P(),
            P("slab", None),
            P(None, "mp"),
            P(None, "mp"),
            P(None, "mp"),
            P("mp", None),
            P("slab", None),
        ),
        check_vma=False,
    )
```

```python
import jax
import jax.numpy as jnp
from jax import lax
from jax.experimental import pallas as pl
from jax.experimental.pallas import tpu as pltpu
from jax.sharding import PartitionSpec as P


TIME_STEP = 0.1
VISCOSITY = 0.2
EPSILON = 1e-05
F32 = jnp.float32
BF16 = jnp.bfloat16
CHUNK = 256
UNROLL = 2


def iota(shape, dim):
    return lax.broadcasted_iota(jnp.int32, shape, dim)


def dot(a, b, contract=(1, 0)):
    dims = (((contract[0],), (contract[1],)), ((), ()))
    return lax.dot_general(a, b, dims, preferred_element_type=F32)


def split(a):
    high = a.astype(BF16)
    return high, (a - high.astype(F32)).astype(BF16)


def head_mean(a, mix, terms=2):
    halves = []
    for at in (0, 256):
        parts = split(a[:, at : at + 256])[:terms]
        halves.append(sum(dot(part, mix) for part in parts))
    return jnp.concatenate(halves, axis=1)


def mean_matrix():
    same = iota((256, 256), 0) // 64 == iota((256, 256), 1) // 64
    return jnp.where(same, 1.0 / 64, 0.0).astype(BF16)


def selections(once_ref, pair_ref, turn_ref):
    row, col = iota((256, 256), 0), iota((256, 256), 1)
    turn_ref[...] = jnp.where(col == (row & 31) * 8 + (row >> 5), 1.0, 0.0).astype(BF16)

    def spread(i, carry):
        at = pl.ds(pl.multiple_of(i * 128, 128), 128)
        row, col = iota((128, 1024), 0), iota((128, 1024), 1)
        once_ref[at, :] = jnp.where(col == 8 * row + i, 1.0, 0.0).astype(BF16)
        return carry

    lax.fori_loop(0, 8, spread, 0)
    row, col = iota((512, 512), 0), iota((512, 512), 1)
    pair_ref[...] = jnp.where(col == 8 * (row & 63) + (row >> 6), 1.0, 0.0).astype(BF16)


def cut_patches(load, pick_ref, slot_ref, out_ref, once_ref, pair_ref, turn_ref, whole_ref, rest_ref):
    row, col = iota((128, 256), 0), iota((128, 256), 1)
    turn_pair = jnp.where(col == (row & 31) * 8 + 2 * (row >> 5), 1.0, 0.0).astype(BF16)

    def strips(i, carry):
        cells = [load(2 * i), load(2 * i + 1)]
        first = jnp.concatenate([c[:128] for c in cells], axis=0).astype(BF16)
        last = [c[128:] for c in cells]
        last = [jnp.concatenate([c, pltpu.roll(c, 255, 1)], axis=0) for c in last]
        last = jnp.concatenate(last, axis=0).astype(BF16)
        whole = dot(turn_ref[...], first, (1, 1)).astype(BF16)
        rest = dot(turn_pair, last, (1, 1)).astype(BF16)
        for k in range(2):
            at = pl.ds(pl.multiple_of(i * 64 + k * 32, 32), 32)
            lanes = slice(k * 128, (k + 1) * 128)
            for x in range(8):
                whole_ref[at, x * 128 : (x + 1) * 128] = whole[x * 32 : (x + 1) * 32, lanes]
            for x in range(4):
                rest_ref[at, x * 128 : (x + 1) * 128] = rest[x * 32 : (x + 1) * 32, lanes]
        return carry

    lax.fori_loop(0, 8, strips, 0, unroll=UNROLL)

    for part_ref, turn_back_ref, lanes in (
        (whole_ref, once_ref, slice(0, 1024)),
        (rest_ref, pair_ref, slice(1024, 1536)),
    ):
        picked = dot(pick_ref[...], part_ref[...]).astype(BF16)
        picked = dot(picked, turn_back_ref[...]).astype(BF16)
        out_ref[:, lanes] = dot(slot_ref[...], picked).astype(BF16)


CUT_SCRATCH = [
    pltpu.VMEM((1024, 1024), BF16),
    pltpu.VMEM((512, 512), BF16),
    pltpu.VMEM((256, 256), BF16),
    pltpu.VMEM((512, 1024), BF16),
    pltpu.VMEM((512, 512), BF16),
]


def old_kernel(field_hbm, anchor_ref, dest_ref, out_ref, pick_ref, slot_ref, field_ref, sem, *scratch):
    fetch = pltpu.make_async_copy(field_hbm, field_ref, sem)
    fetch.start()
    selections(*scratch[:3])
    target = dest_ref[...].astype(F32)
    row, col = iota((256, 256), 0), iota((256, 256), 1)

    def upright(line):
        return jnp.sum(jnp.where(row == col, jnp.broadcast_to(line, (256, 256)), 0.0), axis=1, keepdims=True)

    ahead = jnp.where((upright(target) == target) & (row < col), 1.0, 0.0)
    slot = target * 16.0 + jnp.sum(ahead, axis=0, keepdims=True)
    patch = ((anchor_ref[1] >> 3) & 15) * 32 + ((anchor_ref[2] >> 3) & 31)
    patch = upright(patch.astype(F32)).astype(jnp.int32)
    pick_ref[...] = jnp.where(iota((256, 512), 1) == patch, 1.0, 0.0).astype(BF16)
    sent = jnp.where(iota((512, 256), 0) == slot.astype(jnp.int32), 1.0, 0.0)
    slot_ref[...] = sent.astype(BF16)
    tag = jnp.sum(sent, axis=1, keepdims=True)
    out_ref[:, 1536:1664] = jnp.broadcast_to(tag, (512, 128)).astype(BF16)
    fetch.wait()

    def load(by):
        at = pl.ds(pl.multiple_of(by * 8, 8), 8)
        return field_ref[:, :, at, :].reshape(192, 256)

    cut_patches(load, pick_ref, slot_ref, out_ref, *scratch)


def new_kernel(
    field_hbm, z_prev_ref, z_next_ref, y_prev_ref, y_next_ref, pick_ref, slot_ref,
    new_hbm, out_ref, pad_ref, new_ref, sem, *scratch,
):
    fetch = pltpu.make_async_copy(field_hbm, pad_ref.at[:, 1:9, 8:136, :], sem.at[0])
    fetch.start()
    selections(*scratch[:3])
    pad_ref[:, 0:1, 8:136, :] = z_prev_ref[...]
    pad_ref[:, 9:10, 8:136, :] = z_next_ref[...]
    pad_ref[:, 1:9, 7:8, :] = y_prev_ref[...]
    pad_ref[:, 1:9, 136:137, :] = y_next_ref[...]
    fetch.wait()
    near = VISCOSITY * TIME_STEP

    def layer(z, carry):
        for y in range(0, 128, 32):
            along = [pad_ref[c, z + 1, 8 + y : 40 + y, :] for c in range(3)]
            drift = [(0.5 * TIME_STEP) * v for v in along]
            ahead = [near - v for v in drift]
            behind = [near + v for v in drift]
            for c in range(3):
                centre = along[c]
                z_next = pad_ref[c, z + 2, 8 + y : 40 + y, :]
                z_prev = pad_ref[c, z, 8 + y : 40 + y, :]
                y_next = pad_ref[c, z + 1, 9 + y : 41 + y, :]
                y_prev = pad_ref[c, z + 1, 7 + y : 39 + y, :]
                x_next = pltpu.roll(centre, 255, 1)
                x_prev = pltpu.roll(centre, 1, 1)
                new_ref[c, z, y : y + 32, :] = (
                    (1.0 - 6.0 * near) * centre
                    + (ahead[0] * x_next + behind[0] * x_prev)
                    + (ahead[1] * y_next + behind[1] * y_prev)
                    + (ahead[2] * z_next + behind[2] * z_prev)
                )
        return carry

    lax.fori_loop(0, 8, layer, 0)
    store = pltpu.make_async_copy(new_ref, new_hbm, sem.at[1])
    store.start()

    def load(by):
        at = pl.ds(pl.multiple_of(by * 8, 8), 8)
        return new_ref[:, :, at, :].reshape(192, 256)

    cut_patches(load, pick_ref, slot_ref, out_ref, *scratch)
    store.wait()


def pack(blocks):
    row, col = iota((128, 128), 0), iota((128, 128), 1)
    return jnp.where(row // 64 == col // 64, blocks[0], pltpu.roll(blocks[1], 64, 1))


def unpack(packed):
    row, col = iota((128, 128), 0), iota((128, 128), 1)
    own = row // 64 == col // 64
    return jnp.where(own, packed, 0.0), jnp.where(own, pltpu.roll(packed, 64, 1), 0.0)


def quartets(packed, high_ref, low_ref):
    blank = jnp.zeros((128, 128), F32)
    for p in range(2):
        one, two = unpack(packed[p * 128 : (p + 1) * 128])
        whole = jnp.concatenate(
            [jnp.concatenate([one, blank], axis=1), jnp.concatenate([blank, two], axis=1)], axis=0
        )
        high_ref[p], low_ref[p] = split(whole)


def absolute(m, j):
    return pl.multiple_of(((m - j) & 3) * 128, 128)


def forward_kernel(
    place_ref, old_ref, lift_w_ref, w0_ref, w1_ref, w2_ref, w3_ref,
    lifted_ref, query_ref, key_ref, key_spread_ref, value_ref, value_spread_ref,
    query_w_ref, key_w_ref, value_w_ref, out_w_ref, sums_ref, acc_ref,
):
    m = place_ref[0]
    for j, block in enumerate((w0_ref, w1_ref, w2_ref, w3_ref)):
        at = pl.ds(absolute(m, j), 128)
        query_w_ref[:, at] = block[0]
        key_w_ref[:, at] = block[1]
        value_w_ref[:, at] = block[2]
        for k in range(4):
            out_w_ref[at, k * 128 : (k + 1) * 128] = block[3, k * 128 : (k + 1) * 128, :]
    acc_ref[...] = jnp.zeros_like(acc_ref)
    mix = mean_matrix()

    def rows(i, carry):
        at = pl.ds(pl.multiple_of(i * CHUNK, CHUNK), CHUNK)
        lifted = dot(old_ref[at, 0:1536], lift_w_ref[...]).astype(BF16)
        lifted_ref[at, :] = lifted
        query_ref[at, :] = dot(lifted, query_w_ref[...]).astype(BF16)
        normed = []
        for w_ref, hat_ref, spread_ref in (
            (key_w_ref, key_ref, key_spread_ref),
            (value_w_ref, value_ref, value_spread_ref),
        ):
            heads = dot(lifted, w_ref[...])
            shifted = heads - head_mean(heads, mix)
            spread = jnp.sqrt(head_mean(shifted * shifted, mix, 1) + EPSILON)
            hat = shifted / spread
            normed.append(hat.astype(BF16))
            hat_ref[at, :] = normed[-1]
            spread_ref[at, :] = spread
        for p in range(4):
            part = slice(p * 128, (p + 1) * 128)
            acc_ref[p] += dot(normed[0][:, part], normed[1][:, part], (0, 0))
        return carry

    lax.fori_loop(0, 512 // CHUNK, rows, 0)
    sums_ref[0:128, :] = pack((acc_ref[0], acc_ref[1]))
    sums_ref[128:256, :] = pack((acc_ref[2], acc_ref[3]))
    count = jnp.sum(old_ref[:, 1536:1664].astype(F32), axis=0, keepdims=True)
    sums_ref[256:264, :] = jnp.broadcast_to(count, (8, 128))


def dealer(place_ref, mine_ref, theirs_ref):
    first = place_ref[1] == 0

    def deal(grad, rows, n, at):
        grad = grad.reshape(16, 2, rows, 128)
        even, odd = grad[:, 0], grad[:, 1]
        mine_ref[:, n, at : at + rows, :] = jnp.where(first, even, odd).astype(BF16)
        theirs_ref[:, n, at : at + rows, :] = jnp.where(first, odd, even).astype(BF16)

    return deal


def middle_kernel(
    place_ref, s0_ref, s1_ref, s2_ref, s3_ref, lifted_ref, query_ref, new_ref, out_w_ref, proj_w_ref,
    mine_ref, theirs_ref, d_query_ref, d_hidden_ref, sums_ref, count_ref,
    hidden_ref, d_guess_ref, attended_ref, d_tokens_ref, acc_ref, high_ref, low_ref, loss_ref,
):
    total = (s0_ref[...] + s1_ref[...]) + (s2_ref[...] + s3_ref[...])
    count = total[256:264, :]
    count_ref[...] = count
    quartets(total[0:256] / count[0:1, :], high_ref, low_ref)
    acc_ref[...] = jnp.zeros_like(acc_ref)
    loss_ref[...] = jnp.zeros_like(loss_ref)

    def rows(i, carry):
        at = pl.ds(pl.multiple_of(i * CHUNK, CHUNK), CHUNK)
        query = query_ref[at, :]
        parts = []
        for p in range(2):
            part = query[:, p * 256 : (p + 1) * 256]
            parts.append(dot(part, high_ref[p]) + dot(part, low_ref[p]))
        attended = jnp.concatenate(parts, axis=1).astype(BF16)
        attended_ref[at, :] = attended
        mixed = dot(attended, out_w_ref[...])
        hidden = (lifted_ref[at, :].astype(F32) + mixed).astype(BF16)
        hidden_ref[at, :] = hidden
        error = dot(hidden, proj_w_ref[...]) - new_ref[at, :].astype(F32)
        loss_ref[...] += jnp.sum((error * error).reshape(CHUNK // 8, 8, 1536), axis=0)
        d_guess = (error * (1.0 / 32768)).astype(BF16)
        d_guess_ref[at, :] = d_guess
        d_hidden = dot(d_guess, proj_w_ref[...], (1, 1))
        d_hidden_ref[at, :] = d_hidden
        d_tokens = d_hidden.astype(BF16)
        d_tokens_ref[at, :] = d_tokens
        high, low = split(dot(d_tokens, out_w_ref[...], (1, 1)))
        for p in range(2):
            part = slice(p * 256, (p + 1) * 256)
            back = (
                dot(high[:, part], high_ref[p], (1, 1))
                + dot(high[:, part], low_ref[p], (1, 1))
                + dot(low[:, part], high_ref[p], (1, 1))
            )
            d_query_ref[at, part] = back.astype(BF16)
        for p in range(4):
            part = slice(p * 128, (p + 1) * 128)
            acc_ref[p] += dot(query[:, part], high[:, part], (0, 0)) + dot(
                query[:, part], low[:, part], (0, 0)
            )
        return carry

    lax.fori_loop(0, 512 // CHUNK, rows, 0)
    sums_ref[0:128, :] = pack((acc_ref[0], acc_ref[1]))
    sums_ref[128:256, :] = pack((acc_ref[2], acc_ref[3]))
    loss = jnp.sum(loss_ref[...], axis=(0, 1), keepdims=True) * (1.0 / 50331648)
    sums_ref[256:264, :] = jnp.broadcast_to(loss, (8, 128))
    deal = dealer(place_ref, mine_ref, theirs_ref)
    grad = dot(hidden_ref[...], d_guess_ref[...], (0, 0))
    for n in range(4):
        for j in range(3):
            at = n * 384 + j * 128
            deal(grad[:, at : at + 128], 16, n, 16 * j)
    grad = dot(d_tokens_ref[...], attended_ref[...], (0, 0))
    for n in range(4):
        deal(grad[:, n * 128 : (n + 1) * 128], 16, n, 48)


def backward_kernel(
    place_ref, s0_ref, s1_ref, s2_ref, s3_ref, count_ref, old_hbm, lifted_ref, key_ref, key_spread_ref,
    value_ref, value_spread_ref, d_query_ref, d_hidden_ref, query_w_ref, key_w_ref, value_w_ref,
    mine_ref, theirs_ref, loss_ref, high_ref, low_ref, d_heads_ref, d_lifted_ref, old_ref, sem,
):
    fetch = pltpu.make_async_copy(old_hbm.at[:, 0:1536], old_ref, sem)
    fetch.start()
    total = (s0_ref[...] + s1_ref[...]) + (s2_ref[...] + s3_ref[...])
    loss_ref[...] = total[256:264, :]
    quartets(total[0:256] / count_ref[0:1, :], high_ref, low_ref)
    mix = mean_matrix()

    def rows(i, carry):
        at = pl.ds(pl.multiple_of(i * CHUNK, CHUNK), CHUNK)
        d_query = d_query_ref[at, :]
        d_heads_ref[at, 0:512] = d_query
        d_lifted = d_hidden_ref[at, :] + dot(d_query, query_w_ref[...], (1, 1))
        for hat_ref, spread_ref, other_ref, across, lanes, w_ref in (
            (key_ref, key_spread_ref, value_ref, (1, 1), 512, key_w_ref),
            (value_ref, value_spread_ref, key_ref, (1, 0), 1024, value_w_ref),
        ):
            other = other_ref[at, :]
            parts = []
            for p in range(2):
                part = other[:, p * 256 : (p + 1) * 256]
                parts.append(dot(part, high_ref[p], across) + dot(part, low_ref[p], across))
            grad = jnp.concatenate(parts, axis=1)
            hat = hat_ref[at, :].astype(F32)
            inner = head_mean(grad, mix)
            cross = head_mean(grad * hat, mix)
            grad = ((grad - inner - hat * cross) / spread_ref[at, :]).astype(BF16)
            d_heads_ref[at, lanes : lanes + 512] = grad
            d_lifted = d_lifted + dot(grad, w_ref[...], (1, 1))
        d_lifted_ref[at, :] = d_lifted.astype(BF16)
        return carry

    lax.fori_loop(0, 512 // CHUNK, rows, 0)
    deal = dealer(place_ref, mine_ref, theirs_ref)
    grad = dot(lifted_ref[...], d_heads_ref[...], (0, 0))
    for n in range(4):
        for j in range(3):
            at = 512 * j + 128 * n
            deal(grad[:, at : at + 128], 16, n, 48 + 16 * j)
    fetch.wait()
    grad = dot(old_ref[...], d_lifted_ref[...], (0, 0))
    for n in range(4):
        deal(grad[:, n * 128 : (n + 1) * 128], 48, n, 0)


def last_kernel(
    place_ref, r0_ref, r1_ref, r2_ref, r3_ref, heads_ref,
    lift_ref, query_ref, key_ref, value_ref, out_ref, proj_ref, loss_ref,
):
    m = place_ref[0]
    for j, block in enumerate((r0_ref, r1_ref, r2_ref, r3_ref)):
        lift_ref[:, pl.ds(absolute(m, j), 128)] = block[0:48, :]
        for k in range(3):
            at = pl.multiple_of(((m - j) & 3) * 384 + k * 128, 128)
            proj_ref[:, pl.ds(at, 128)] = block[48 + 16 * k : 64 + 16 * k, :]
    query_ref[...] = heads_ref[:, 0:16, :].astype(F32).reshape(512, 128)
    key_ref[...] = heads_ref[:, 16:32, :].astype(F32).reshape(512, 128)
    value_ref[...] = heads_ref[:, 32:48, :].astype(F32).reshape(512, 128)
    out_ref[...] = heads_ref[:, 48:64, :].astype(F32).reshape(512, 128).T
    loss = jnp.sum(heads_ref[:, 64:80, :].astype(F32), axis=0)
    loss_ref[...] = loss[0:1, 0:1] + loss[1:2, 0:1]


def call(body, outs, scratch=(), ins="", results=None):
    spaces = {"s": pltpu.SMEM, "h": pl.ANY, "v": pltpu.VMEM}
    return pl.pallas_call(
        body,
        out_shape=[jax.ShapeDtypeStruct(shape, kind) for shape, kind in outs],
        in_specs=[pl.BlockSpec(memory_space=spaces[k]) for k in ins],
        out_specs=[pl.BlockSpec(memory_space=spaces[k]) for k in results or "v" * len(outs)],
        scratch_shapes=list(scratch),
        compiler_params=pltpu.CompilerParams(vmem_limit_bytes=60 << 20),
    )


def around(value):
    got = [value]
    for d in (1, 2, 3):
        got.append(lax.ppermute(value, "mp", [(i, (i + d) % 4) for i in range(4)]))
    return got


def exchange(value, axes):
    return lax.all_to_all(value, axes, split_axis=0, concat_axis=0, tiled=True)


def pair_sum(mine, theirs):
    got = lax.ppermute(theirs, "slab", [(i, i ^ 1) for i in range(32)])
    return (mine.astype(F32) + got.astype(F32)).astype(BF16)


def total(partial):
    groups = [[(2 * q + c) * 4 + n for q in range(16) for n in range(4)] for c in range(2)]
    got = lax.all_to_all(
        partial.reshape(64, -1, 128),
        ("slab", "mp"),
        split_axis=0,
        concat_axis=0,
        axis_index_groups=groups,
        tiled=True,
    )
    return jnp.sum(got.astype(F32), axis=0)


def step(velocity, anchors, dest, w_lift, w_query, w_key, w_value, w_out, w_proj):
    slabs = lax.axis_size("slab")
    place = jnp.stack([lax.axis_index("mp"), lax.axis_index("slab") & 1])
    up = [(i, (i + 1) % slabs) for i in range(slabs)]
    z_prev = lax.ppermute(velocity[:, 7:8], "slab", up)
    z_next = lax.ppermute(velocity[:, 0:1], "slab", [(j, i) for i, j in up])
    up = [(i, (i + 1) % 4) for i in range(4)]
    y_prev = lax.ppermute(velocity[:, :, 127:128], "mp", up)
    y_next = lax.ppermute(velocity[:, :, 0:1], "mp", [(j, i) for i, j in up])
    tall = jnp.concatenate([w_out[:, k * 128 : (k + 1) * 128] for k in range(4)], axis=0)
    heads_w = around(jnp.stack([w_query, w_key, w_value, tall]))

    send_old, pick, slot = call(
        old_kernel,
        [((512, 1664), BF16), ((256, 512), BF16), ((512, 256), BF16)],
        [pltpu.VMEM((3, 8, 128, 256), F32), pltpu.SemaphoreType.DMA] + CUT_SCRATCH,
        "hvv",
    )(velocity, anchors.reshape(3, 1, 256), dest.reshape(1, 256))
    old = exchange(send_old, "slab")
    new_velocity, send_new = call(
        new_kernel,
        [((3, 8, 128, 256), F32), ((512, 1536), BF16)],
        [
            pltpu.VMEM((3, 10, 144, 256), F32),
            pltpu.VMEM((3, 8, 128, 256), F32),
            pltpu.SemaphoreType.DMA((2,)),
        ]
        + CUT_SCRATCH,
        "hvvvvvv",
        "hv",
    )(velocity, z_prev, z_next, y_prev, y_next, pick, slot)
    new = exchange(send_new, "slab")

    wide, wide_f = ((512, 512), BF16), ((512, 512), F32)
    lifted, query, key, key_spread, value, value_spread, wq, wk, wv, wo, sums = call(
        forward_kernel,
        [wide, wide, wide, wide_f, wide, wide_f, wide, wide, wide, wide, ((264, 128), F32)],
        [pltpu.VMEM((4, 128, 128), F32)],
        "svvvvvv",
    )(place, old, w_lift, *heads_w)
    sums = around(sums)
    mine, theirs, d_query, d_hidden, d_sums, count = call(
        middle_kernel,
        [((16, 4, 64, 128), BF16), ((16, 4, 64, 128), BF16), wide, wide_f, ((264, 128), F32), ((8, 128), F32)],
        [
            pltpu.VMEM((512, 512), BF16),
            pltpu.VMEM((512, 1536), BF16),
            pltpu.VMEM((512, 512), BF16),
            pltpu.VMEM((512, 512), BF16),
            pltpu.VMEM((4, 128, 128), F32),
            pltpu.VMEM((2, 256, 256), BF16),
            pltpu.VMEM((2, 256, 256), BF16),
            pltpu.VMEM((8, 1536), F32),
        ],
        "svvvvvvvvv",
    )(place, *sums, lifted, query, new, wo, w_proj)
    d_sums = around(d_sums)
    total_out = total(pair_sum(mine, theirs))
    mine, theirs, loss_part = call(
        backward_kernel,
        [((16, 4, 96, 128), BF16), ((16, 4, 96, 128), BF16), ((8, 128), F32)],
        [
            pltpu.VMEM((2, 256, 256), BF16),
            pltpu.VMEM((2, 256, 256), BF16),
            pltpu.VMEM((512, 1536), BF16),
            pltpu.VMEM((512, 512), BF16),
            pltpu.VMEM((512, 1536), BF16),
            pltpu.SemaphoreType.DMA,
        ],
        "svvvvvhvvvvvvvvvv",
    )(place, *d_sums, count, old, lifted, key, key_spread, value, value_spread, d_query, d_hidden, wq, wk, wv)
    total_in = total(pair_sum(mine, theirs))
    blocks = jnp.concatenate([total_in[0:48], total_out[0:48]], axis=0)
    loss_high = loss_part.astype(BF16)
    loss_low = (loss_part - loss_high.astype(F32)).astype(BF16)
    heads = jnp.concatenate([total_in[48:96], total_out[48:64]], axis=0).astype(BF16)
    heads = jnp.concatenate([heads, loss_high[0:1], loss_low[0:1], jnp.zeros((14, 128), BF16)], axis=0)
    heads = exchange(jnp.broadcast_to(heads[None], (32, 80, 128)), "slab")
    lift, g_query, g_key, g_value, g_out, proj, loss = call(
        last_kernel,
        [
            ((48, 512), F32),
            ((512, 128), F32),
            ((512, 128), F32),
            ((512, 128), F32),
            ((128, 512), F32),
            ((16, 1536), F32),
            ((1, 1), F32),
        ],
        (),
        "svvvvv",
    )(place, *around(blocks), heads)
    return (new_velocity, loss.reshape(()), lift, g_query, g_key, g_value, g_out, proj)


def solution(mesh):
    return jax.shard_map(
        step,
        mesh=mesh,
        in_specs=(
            P(None, "slab", "mp", None),
            P(None, "slab", "mp", None),
            P("slab", "mp", None, None),
            P(),
            P(None, "mp"),
            P(None, "mp"),
            P(None, "mp"),
            P("mp", None),
            P(),
        ),
        out_specs=(
            P(None, "slab", "mp", None),
            P(),
            P("slab", None),
            P(None, "mp"),
            P(None, "mp"),
            P(None, "mp"),
            P("mp", None),
            P("slab", None),
        ),
        check_vma=False,
    )
```

```python
import jax
import jax.numpy as jnp
from jax import lax
from jax.experimental import pallas as pl
from jax.experimental.pallas import tpu as pltpu
from jax.sharding import PartitionSpec as P


TIME_STEP = 0.1
VISCOSITY = 0.2
EPSILON = 1e-05
F32 = jnp.float32
BF16 = jnp.bfloat16
CHUNK = 512
UNROLL = 2


def iota(shape, dim):
    return lax.broadcasted_iota(jnp.int32, shape, dim)


def dot(a, b, contract=(1, 0)):
    dims = (((contract[0],), (contract[1],)), ((), ()))
    return lax.dot_general(a, b, dims, preferred_element_type=F32)


def split(a):
    high = a.astype(BF16)
    return high, (a - high.astype(F32)).astype(BF16)


def head_mean(a, mix, terms=2):
    halves = []
    for at in (0, 256):
        parts = split(a[:, at : at + 256])[:terms]
        halves.append(sum(dot(part, mix) for part in parts))
    return jnp.concatenate(halves, axis=1)


def mean_matrix():
    same = iota((256, 256), 0) // 64 == iota((256, 256), 1) // 64
    return jnp.where(same, 1.0 / 64, 0.0).astype(BF16)


def selections(once_ref, pair_ref, turn_ref):
    row, col = iota((256, 256), 0), iota((256, 256), 1)
    turn_ref[...] = jnp.where(col == (row & 31) * 8 + (row >> 5), 1.0, 0.0).astype(BF16)

    def spread(i, carry):
        at = pl.ds(pl.multiple_of(i * 128, 128), 128)
        row, col = iota((128, 1024), 0), iota((128, 1024), 1)
        once_ref[at, :] = jnp.where(col == 8 * row + i, 1.0, 0.0).astype(BF16)
        return carry

    lax.fori_loop(0, 8, spread, 0)
    row, col = iota((512, 512), 0), iota((512, 512), 1)
    pair_ref[...] = jnp.where(col == 8 * (row & 63) + (row >> 6), 1.0, 0.0).astype(BF16)


def cut_patches(load, pick_ref, slot_ref, out_ref, once_ref, pair_ref, turn_ref, whole_ref, rest_ref):
    row, col = iota((128, 256), 0), iota((128, 256), 1)
    turn_pair = jnp.where(col == (row & 31) * 8 + 2 * (row >> 5), 1.0, 0.0).astype(BF16)

    def strips(i, carry):
        cells = [load(2 * i), load(2 * i + 1)]
        first = jnp.concatenate([c[:128] for c in cells], axis=0).astype(BF16)
        last = [c[128:] for c in cells]
        last = [jnp.concatenate([c, pltpu.roll(c, 255, 1)], axis=0) for c in last]
        last = jnp.concatenate(last, axis=0).astype(BF16)
        whole = dot(turn_ref[...], first, (1, 1)).astype(BF16)
        rest = dot(turn_pair, last, (1, 1)).astype(BF16)
        for k in range(2):
            at = pl.ds(pl.multiple_of(i * 64 + k * 32, 32), 32)
            lanes = slice(k * 128, (k + 1) * 128)
            for x in range(8):
                whole_ref[at, x * 128 : (x + 1) * 128] = whole[x * 32 : (x + 1) * 32, lanes]
            for x in range(4):
                rest_ref[at, x * 128 : (x + 1) * 128] = rest[x * 32 : (x + 1) * 32, lanes]
        return carry

    lax.fori_loop(0, 8, strips, 0, unroll=UNROLL)

    for part_ref, turn_back_ref, lanes in (
        (whole_ref, once_ref, slice(0, 1024)),
        (rest_ref, pair_ref, slice(1024, 1536)),
    ):
        picked = dot(pick_ref[...], part_ref[...]).astype(BF16)
        picked = dot(picked, turn_back_ref[...]).astype(BF16)
        out_ref[:, lanes] = dot(slot_ref[...], picked).astype(BF16)


CUT_SCRATCH = [
    pltpu.VMEM((1024, 1024), BF16),
    pltpu.VMEM((512, 512), BF16),
    pltpu.VMEM((256, 256), BF16),
    pltpu.VMEM((512, 1024), BF16),
    pltpu.VMEM((512, 512), BF16),
]


def old_kernel(field_hbm, anchor_ref, dest_ref, out_ref, pick_ref, slot_ref, field_ref, sem, *scratch):
    fetch = pltpu.make_async_copy(field_hbm, field_ref, sem)
    fetch.start()
    selections(*scratch[:3])
    target = dest_ref[...].astype(F32)
    row, col = iota((256, 256), 0), iota((256, 256), 1)

    def upright(line):
        return jnp.sum(jnp.where(row == col, jnp.broadcast_to(line, (256, 256)), 0.0), axis=1, keepdims=True)

    ahead = jnp.where((upright(target) == target) & (row < col), 1.0, 0.0)
    slot = target * 16.0 + jnp.sum(ahead, axis=0, keepdims=True)
    patch = ((anchor_ref[1] >> 3) & 15) * 32 + ((anchor_ref[2] >> 3) & 31)
    patch = upright(patch.astype(F32)).astype(jnp.int32)
    pick_ref[...] = jnp.where(iota((256, 512), 1) == patch, 1.0, 0.0).astype(BF16)
    sent = jnp.where(iota((512, 256), 0) == slot.astype(jnp.int32), 1.0, 0.0)
    slot_ref[...] = sent.astype(BF16)
    tag = jnp.sum(sent, axis=1, keepdims=True)
    out_ref[:, 1536:1664] = jnp.broadcast_to(tag, (512, 128)).astype(BF16)
    fetch.wait()

    def load(by):
        at = pl.ds(pl.multiple_of(by * 8, 8), 8)
        return field_ref[:, :, at, :].reshape(192, 256)

    cut_patches(load, pick_ref, slot_ref, out_ref, *scratch)


def new_kernel(
    field_hbm, z_prev_ref, z_next_ref, y_prev_ref, y_next_ref, pick_ref, slot_ref,
    new_hbm, out_ref, pad_ref, new_ref, sem, *scratch,
):
    fetch = pltpu.make_async_copy(field_hbm, pad_ref.at[:, 1:9, 8:136, :], sem.at[0])
    fetch.start()
    selections(*scratch[:3])
    pad_ref[:, 0:1, 8:136, :] = z_prev_ref[...].astype(F32)
    pad_ref[:, 9:10, 8:136, :] = z_next_ref[...].astype(F32)
    pad_ref[:, 1:9, 7:8, :] = y_prev_ref[...]
    pad_ref[:, 1:9, 136:137, :] = y_next_ref[...]
    fetch.wait()
    near = VISCOSITY * TIME_STEP

    def layer(z, carry):
        for y in range(0, 128, 16):
            along = [pad_ref[c, z + 1, 8 + y : 24 + y, :] for c in range(3)]
            drift = [(0.5 * TIME_STEP) * v for v in along]
            ahead = [near - v for v in drift]
            behind = [near + v for v in drift]
            for c in range(3):
                centre = along[c]
                z_next = pad_ref[c, z + 2, 8 + y : 24 + y, :]
                z_prev = pad_ref[c, z, 8 + y : 24 + y, :]
                y_next = pad_ref[c, z + 1, 9 + y : 25 + y, :]
                y_prev = pad_ref[c, z + 1, 7 + y : 23 + y, :]
                x_next = pltpu.roll(centre, 255, 1)
                x_prev = pltpu.roll(centre, 1, 1)
                new_ref[c, z, y : y + 16, :] = (
                    (1.0 - 6.0 * near) * centre
                    + (ahead[0] * x_next + behind[0] * x_prev)
                    + (ahead[1] * y_next + behind[1] * y_prev)
                    + (ahead[2] * z_next + behind[2] * z_prev)
                )
        return carry

    lax.fori_loop(0, 8, layer, 0)
    store = pltpu.make_async_copy(new_ref, new_hbm, sem.at[1])
    store.start()

    def load(by):
        at = pl.ds(pl.multiple_of(by * 8, 8), 8)
        return new_ref[:, :, at, :].reshape(192, 256)

    cut_patches(load, pick_ref, slot_ref, out_ref, *scratch)
    store.wait()


def pack(blocks):
    row, col = iota((128, 128), 0), iota((128, 128), 1)
    return jnp.where(row // 64 == col // 64, blocks[0], pltpu.roll(blocks[1], 64, 1))


def unpack(packed):
    row, col = iota((128, 128), 0), iota((128, 128), 1)
    own = row // 64 == col // 64
    return jnp.where(own, packed, 0.0), jnp.where(own, pltpu.roll(packed, 64, 1), 0.0)


def quartets(packed, high_ref, low_ref):
    blank = jnp.zeros((128, 128), F32)
    for p in range(2):
        one, two = unpack(packed[p * 128 : (p + 1) * 128])
        whole = jnp.concatenate(
            [jnp.concatenate([one, blank], axis=1), jnp.concatenate([blank, two], axis=1)], axis=0
        )
        high_ref[p], low_ref[p] = split(whole)


def absolute(m, j):
    return pl.multiple_of(((m - j) & 3) * 128, 128)


def forward_kernel(
    place_ref, old_ref, lift_w_ref, w0_ref, w1_ref, w2_ref, w3_ref,
    lifted_ref, query_ref, key_ref, key_spread_ref, value_ref, value_spread_ref,
    query_w_ref, key_w_ref, value_w_ref, out_w_ref, sums_ref, acc_ref,
):
    m = place_ref[0]
    for j, block in enumerate((w0_ref, w1_ref, w2_ref, w3_ref)):
        at = pl.ds(absolute(m, j), 128)
        query_w_ref[:, at] = block[0]
        key_w_ref[:, at] = block[1]
        value_w_ref[:, at] = block[2]
        for k in range(4):
            out_w_ref[at, k * 128 : (k + 1) * 128] = block[3, k * 128 : (k + 1) * 128, :]
    acc_ref[...] = jnp.zeros_like(acc_ref)
    mix = mean_matrix()

    def rows(i, carry):
        at = pl.ds(pl.multiple_of(i * CHUNK, CHUNK), CHUNK)
        lifted = dot(old_ref[at, 0:1536], lift_w_ref[...]).astype(BF16)
        lifted_ref[at, :] = lifted
        query_ref[at, :] = dot(lifted, query_w_ref[...]).astype(BF16)
        normed = []
        for w_ref, hat_ref, spread_ref in (
            (key_w_ref, key_ref, key_spread_ref),
            (value_w_ref, value_ref, value_spread_ref),
        ):
            heads = dot(lifted, w_ref[...])
            shifted = heads - head_mean(heads, mix)
            spread = jnp.sqrt(head_mean(shifted * shifted, mix, 1) + EPSILON)
            hat = shifted / spread
            normed.append(hat.astype(BF16))
            hat_ref[at, :] = normed[-1]
            spread_ref[at, :] = spread
        for p in range(4):
            part = slice(p * 128, (p + 1) * 128)
            acc_ref[p] += dot(normed[0][:, part], normed[1][:, part], (0, 0))
        return carry

    lax.fori_loop(0, 512 // CHUNK, rows, 0)
    sums_ref[0:128, :] = pack((acc_ref[0], acc_ref[1]))
    sums_ref[128:256, :] = pack((acc_ref[2], acc_ref[3]))
    count = jnp.sum(old_ref[:, 1536:1664].astype(F32), axis=0, keepdims=True)
    sums_ref[256:264, :] = jnp.broadcast_to(count, (8, 128))


def dealer(place_ref, mine_ref, theirs_ref):
    first = place_ref[1] == 0

    def deal(grad, rows, n, at):
        grad = grad.reshape(16, 2, rows, 128)
        even, odd = grad[:, 0], grad[:, 1]
        mine_ref[:, n, at : at + rows, :] = jnp.where(first, even, odd).astype(BF16)
        theirs_ref[:, n, at : at + rows, :] = jnp.where(first, odd, even).astype(BF16)

    return deal


def middle_kernel(
    place_ref, s0_ref, s1_ref, s2_ref, s3_ref, lifted_ref, query_ref, new_ref, out_w_ref, proj_w_ref,
    mine_ref, theirs_ref, d_query_ref, d_hidden_ref, sums_ref, count_ref,
    hidden_ref, d_guess_ref, attended_ref, d_tokens_ref, acc_ref, high_ref, low_ref, loss_ref,
):
    total = (s0_ref[...] + s1_ref[...]) + (s2_ref[...] + s3_ref[...])
    count = total[256:264, :]
    count_ref[...] = count
    quartets(total[0:256] / count[0:1, :], high_ref, low_ref)
    acc_ref[...] = jnp.zeros_like(acc_ref)
    loss_ref[...] = jnp.zeros_like(loss_ref)

    def rows(i, carry):
        at = pl.ds(pl.multiple_of(i * CHUNK, CHUNK), CHUNK)
        query = query_ref[at, :]
        parts = []
        for p in range(2):
            part = query[:, p * 256 : (p + 1) * 256]
            parts.append(dot(part, high_ref[p]) + dot(part, low_ref[p]))
        attended = jnp.concatenate(parts, axis=1).astype(BF16)
        attended_ref[at, :] = attended
        mixed = dot(attended, out_w_ref[...])
        hidden = (lifted_ref[at, :].astype(F32) + mixed).astype(BF16)
        hidden_ref[at, :] = hidden
        error = dot(hidden, proj_w_ref[...]) - new_ref[at, :].astype(F32)
        loss_ref[...] += jnp.sum((error * error).reshape(CHUNK // 8, 8, 1536), axis=0)
        d_guess = (error * (1.0 / 32768)).astype(BF16)
        d_guess_ref[at, :] = d_guess
        d_hidden = dot(d_guess, proj_w_ref[...], (1, 1))
        d_hidden_ref[at, :] = d_hidden
        d_tokens = d_hidden.astype(BF16)
        d_tokens_ref[at, :] = d_tokens
        high, low = split(dot(d_tokens, out_w_ref[...], (1, 1)))
        for p in range(2):
            part = slice(p * 256, (p + 1) * 256)
            back = (
                dot(high[:, part], high_ref[p], (1, 1))
                + dot(high[:, part], low_ref[p], (1, 1))
                + dot(low[:, part], high_ref[p], (1, 1))
            )
            d_query_ref[at, part] = back.astype(BF16)
        for p in range(4):
            part = slice(p * 128, (p + 1) * 128)
            acc_ref[p] += dot(query[:, part], high[:, part], (0, 0)) + dot(
                query[:, part], low[:, part], (0, 0)
            )
        return carry

    lax.fori_loop(0, 512 // CHUNK, rows, 0)
    sums_ref[0:128, :] = pack((acc_ref[0], acc_ref[1])).astype(BF16)
    sums_ref[128:256, :] = pack((acc_ref[2], acc_ref[3])).astype(BF16)
    loss = jnp.sum(loss_ref[...], axis=(0, 1), keepdims=True) * (1.0 / 50331648)
    sums_ref[256:272, :], sums_ref[272:288, :] = split(jnp.broadcast_to(loss, (16, 128)))
    deal = dealer(place_ref, mine_ref, theirs_ref)
    grad = dot(hidden_ref[...], d_guess_ref[...], (0, 0))
    for n in range(4):
        for j in range(3):
            at = n * 384 + j * 128
            deal(grad[:, at : at + 128], 16, n, 16 * j)
    grad = dot(d_tokens_ref[...], attended_ref[...], (0, 0))
    for n in range(4):
        deal(grad[:, n * 128 : (n + 1) * 128], 16, n, 48)


def backward_kernel(
    place_ref, s0_ref, s1_ref, s2_ref, s3_ref, count_ref, old_hbm, lifted_ref, key_ref, key_spread_ref,
    value_ref, value_spread_ref, d_query_ref, d_hidden_ref, query_w_ref, key_w_ref, value_w_ref,
    mine_ref, theirs_ref, loss_ref, high_ref, low_ref, d_heads_ref, d_lifted_ref, old_ref, sem,
):
    fetch = pltpu.make_async_copy(old_hbm.at[:, 0:1536], old_ref, sem)
    fetch.start()
    s0, s1, s2, s3 = [ref[...].astype(F32) for ref in (s0_ref, s1_ref, s2_ref, s3_ref)]
    total = (s0 + s1) + (s2 + s3)
    loss_ref[...] = total[256:264, :] + total[272:280, :]
    quartets(total[0:256] / count_ref[0:1, :], high_ref, low_ref)
    mix = mean_matrix()

    def rows(i, carry):
        at = pl.ds(pl.multiple_of(i * CHUNK, CHUNK), CHUNK)
        d_query = d_query_ref[at, :]
        d_heads_ref[at, 0:512] = d_query
        d_lifted = d_hidden_ref[at, :] + dot(d_query, query_w_ref[...], (1, 1))
        for hat_ref, spread_ref, other_ref, across, lanes, w_ref in (
            (key_ref, key_spread_ref, value_ref, (1, 1), 512, key_w_ref),
            (value_ref, value_spread_ref, key_ref, (1, 0), 1024, value_w_ref),
        ):
            other = other_ref[at, :]
            parts = []
            for p in range(2):
                part = other[:, p * 256 : (p + 1) * 256]
                parts.append(dot(part, high_ref[p], across) + dot(part, low_ref[p], across))
            grad = jnp.concatenate(parts, axis=1)
            hat = hat_ref[at, :].astype(F32)
            inner = head_mean(grad, mix)
            cross = head_mean(grad * hat, mix)
            grad = ((grad - inner - hat * cross) / spread_ref[at, :]).astype(BF16)
            d_heads_ref[at, lanes : lanes + 512] = grad
            d_lifted = d_lifted + dot(grad, w_ref[...], (1, 1))
        d_lifted_ref[at, :] = d_lifted.astype(BF16)
        return carry

    lax.fori_loop(0, 512 // CHUNK, rows, 0)
    deal = dealer(place_ref, mine_ref, theirs_ref)
    grad = dot(lifted_ref[...], d_heads_ref[...], (0, 0))
    for n in range(4):
        for j in range(3):
            at = 512 * j + 128 * n
            deal(grad[:, at : at + 128], 16, n, 48 + 16 * j)
    fetch.wait()
    grad = dot(old_ref[...], d_lifted_ref[...], (0, 0))
    for n in range(4):
        deal(grad[:, n * 128 : (n + 1) * 128], 48, n, 0)


def last_kernel(
    place_ref, r0_ref, r1_ref, r2_ref, r3_ref, heads_ref,
    lift_ref, query_ref, key_ref, value_ref, out_ref, proj_ref, loss_ref,
):
    m = place_ref[0]
    for j, block in enumerate((r0_ref, r1_ref, r2_ref, r3_ref)):
        lift_ref[:, pl.ds(absolute(m, j), 128)] = block[0:48, :]
        for k in range(3):
            at = pl.multiple_of(((m - j) & 3) * 384 + k * 128, 128)
            proj_ref[:, pl.ds(at, 128)] = block[48 + 16 * k : 64 + 16 * k, :]
    query_ref[...] = heads_ref[:, 0:16, :].astype(F32).reshape(512, 128)
    key_ref[...] = heads_ref[:, 16:32, :].astype(F32).reshape(512, 128)
    value_ref[...] = heads_ref[:, 32:48, :].astype(F32).reshape(512, 128)
    out_ref[...] = heads_ref[:, 48:64, :].astype(F32).reshape(512, 128).T
    loss = jnp.sum(heads_ref[:, 64:80, :].astype(F32), axis=0)
    loss_ref[...] = loss[0:1, 0:1] + loss[1:2, 0:1]


def call(body, outs, scratch=(), ins="", results=None):
    spaces = {"s": pltpu.SMEM, "h": pl.ANY, "v": pltpu.VMEM}
    return pl.pallas_call(
        body,
        out_shape=[jax.ShapeDtypeStruct(shape, kind) for shape, kind in outs],
        in_specs=[pl.BlockSpec(memory_space=spaces[k]) for k in ins],
        out_specs=[pl.BlockSpec(memory_space=spaces[k]) for k in results or "v" * len(outs)],
        scratch_shapes=list(scratch),
        compiler_params=pltpu.CompilerParams(vmem_limit_bytes=60 << 20),
    )


def around(value):
    got = [value]
    for d in (1, 2, 3):
        got.append(lax.ppermute(value, "mp", [(i, (i + d) % 4) for i in range(4)]))
    return got


def exchange(value, axes):
    return lax.all_to_all(value, axes, split_axis=0, concat_axis=0, tiled=True)


def pair_sum(mine, theirs):
    got = lax.ppermute(theirs, "slab", [(i, i ^ 1) for i in range(32)])
    return (mine.astype(F32) + got.astype(F32)).astype(BF16)


def total(partial):
    groups = [[(2 * q + c) * 4 + n for q in range(16) for n in range(4)] for c in range(2)]
    got = lax.all_to_all(
        partial.reshape(64, -1, 128),
        ("slab", "mp"),
        split_axis=0,
        concat_axis=0,
        axis_index_groups=groups,
        tiled=True,
    )
    return jnp.sum(got.astype(F32), axis=0)


def step(velocity, anchors, dest, w_lift, w_query, w_key, w_value, w_out, w_proj):
    slabs = lax.axis_size("slab")
    place = jnp.stack([lax.axis_index("mp"), lax.axis_index("slab") & 1])
    up = [(i, (i + 1) % slabs) for i in range(slabs)]
    z_prev = lax.ppermute(velocity[:, 7:8].astype(BF16), "slab", up)
    z_next = lax.ppermute(velocity[:, 0:1].astype(BF16), "slab", [(j, i) for i, j in up])
    up = [(i, (i + 1) % 4) for i in range(4)]
    y_prev = lax.ppermute(velocity[:, :, 127:128], "mp", up)
    y_next = lax.ppermute(velocity[:, :, 0:1], "mp", [(j, i) for i, j in up])
    tall = jnp.concatenate([w_out[:, k * 128 : (k + 1) * 128] for k in range(4)], axis=0)
    heads_w = around(jnp.stack([w_query, w_key, w_value, tall]))

    send_old, pick, slot = call(
        old_kernel,
        [((512, 1664), BF16), ((256, 512), BF16), ((512, 256), BF16)],
        [pltpu.VMEM((3, 8, 128, 256), F32), pltpu.SemaphoreType.DMA] + CUT_SCRATCH,
        "hvv",
    )(velocity, anchors.reshape(3, 1, 256), dest.reshape(1, 256))
    old = exchange(send_old, "slab")
    new_velocity, send_new = call(
        new_kernel,
        [((3, 8, 128, 256), F32), ((512, 1536), BF16)],
        [
            pltpu.VMEM((3, 10, 144, 256), F32),
            pltpu.VMEM((3, 8, 128, 256), F32),
            pltpu.SemaphoreType.DMA((2,)),
        ]
        + CUT_SCRATCH,
        "hvvvvvv",
        "hv",
    )(velocity, z_prev, z_next, y_prev, y_next, pick, slot)
    new = exchange(send_new, "slab")

    wide, wide_f = ((512, 512), BF16), ((512, 512), F32)
    lifted, query, key, key_spread, value, value_spread, wq, wk, wv, wo, sums = call(
        forward_kernel,
        [wide, wide, wide, wide_f, wide, wide_f, wide, wide, wide, wide, ((264, 128), F32)],
        [pltpu.VMEM((4, 128, 128), F32)],
        "svvvvvv",
    )(place, old, w_lift, *heads_w)
    sums = around(sums)
    mine, theirs, d_query, d_hidden, d_sums, count = call(
        middle_kernel,
        [((16, 4, 64, 128), BF16), ((16, 4, 64, 128), BF16), wide, wide_f, ((288, 128), BF16), ((8, 128), F32)],
        [
            pltpu.VMEM((512, 512), BF16),
            pltpu.VMEM((512, 1536), BF16),
            pltpu.VMEM((512, 512), BF16),
            pltpu.VMEM((512, 512), BF16),
            pltpu.VMEM((4, 128, 128), F32),
            pltpu.VMEM((2, 256, 256), BF16),
            pltpu.VMEM((2, 256, 256), BF16),
            pltpu.VMEM((8, 1536), F32),
        ],
        "svvvvvvvvv",
    )(place, *sums, lifted, query, new, wo, w_proj)
    d_sums = around(d_sums)
    total_out = total(pair_sum(mine, theirs))
    mine, theirs, loss_part = call(
        backward_kernel,
        [((16, 4, 96, 128), BF16), ((16, 4, 96, 128), BF16), ((8, 128), F32)],
        [
            pltpu.VMEM((2, 256, 256), BF16),
            pltpu.VMEM((2, 256, 256), BF16),
            pltpu.VMEM((512, 1536), BF16),
            pltpu.VMEM((512, 512), BF16),
            pltpu.VMEM((512, 1536), BF16),
            pltpu.SemaphoreType.DMA,
        ],
        "svvvvvhvvvvvvvvvv",
    )(place, *d_sums, count, old, lifted, key, key_spread, value, value_spread, d_query, d_hidden, wq, wk, wv)
    total_in = total(pair_sum(mine, theirs))
    blocks = jnp.concatenate([total_in[0:48], total_out[0:48]], axis=0)
    loss_high = loss_part.astype(BF16)
    loss_low = (loss_part - loss_high.astype(F32)).astype(BF16)
    heads = jnp.concatenate([total_in[48:96], total_out[48:64]], axis=0).astype(BF16)
    heads = jnp.concatenate([heads, loss_high[0:1], loss_low[0:1], jnp.zeros((14, 128), BF16)], axis=0)
    heads = exchange(jnp.broadcast_to(heads[None], (32, 80, 128)), "slab")
    lift, g_query, g_key, g_value, g_out, proj, loss = call(
        last_kernel,
        [
            ((48, 512), F32),
            ((512, 128), F32),
            ((512, 128), F32),
            ((512, 128), F32),
            ((128, 512), F32),
            ((16, 1536), F32),
            ((1, 1), F32),
        ],
        (),
        "svvvvv",
    )(place, *around(blocks), heads)
    return (new_velocity, loss.reshape(()), lift, g_query, g_key, g_value, g_out, proj)


def solution(mesh):
    return jax.shard_map(
        step,
        mesh=mesh,
        in_specs=(
            P(None, "slab", "mp", None),
            P(None, "slab", "mp", None),
            P("slab", "mp", None, None),
            P(),
            P(None, "mp"),
            P(None, "mp"),
            P(None, "mp"),
            P("mp", None),
            P(),
        ),
        out_specs=(
            P(None, "slab", "mp", None),
            P(),
            P("slab", None),
            P(None, "mp"),
            P(None, "mp"),
            P(None, "mp"),
            P("mp", None),
            P("slab", None),
        ),
        check_vma=False,
    )
```

```python
import jax
import jax.numpy as jnp
from jax import lax
from jax.experimental import pallas as pl
from jax.experimental.pallas import tpu as pltpu
from jax.sharding import PartitionSpec as P


TIME_STEP = 0.1
VISCOSITY = 0.2
EPSILON = 1e-05
F32 = jnp.float32
BF16 = jnp.bfloat16
CHUNK = 512
UNROLL = 2


def iota(shape, dim):
    return lax.broadcasted_iota(jnp.int32, shape, dim)


def dot(a, b, contract=(1, 0)):
    dims = (((contract[0],), (contract[1],)), ((), ()))
    return lax.dot_general(a, b, dims, preferred_element_type=F32)


def split(a):
    high = a.astype(BF16)
    return high, (a - high.astype(F32)).astype(BF16)


def head_mean(a, mix, terms=2):
    halves = []
    for at in (0, 256):
        parts = split(a[:, at : at + 256])[:terms]
        halves.append(sum(dot(part, mix) for part in parts))
    return jnp.concatenate(halves, axis=1)


def mean_matrix():
    same = iota((256, 256), 0) // 64 == iota((256, 256), 1) // 64
    return jnp.where(same, 1.0 / 64, 0.0).astype(BF16)


def selections(once_ref, pair_ref, turn_ref):
    row, col = iota((256, 256), 0), iota((256, 256), 1)
    turn_ref[...] = jnp.where(col == (row & 31) * 8 + (row >> 5), 1.0, 0.0).astype(BF16)

    def spread(i, carry):
        at = pl.ds(pl.multiple_of(i * 128, 128), 128)
        row, col = iota((128, 1024), 0), iota((128, 1024), 1)
        once_ref[at, :] = jnp.where(col == 8 * row + i, 1.0, 0.0).astype(BF16)
        return carry

    lax.fori_loop(0, 8, spread, 0)
    row, col = iota((512, 512), 0), iota((512, 512), 1)
    pair_ref[...] = jnp.where(col == 8 * (row & 63) + (row >> 6), 1.0, 0.0).astype(BF16)


def cut_patches(load, pick_ref, slot_ref, out_ref, once_ref, pair_ref, turn_ref, whole_ref, rest_ref):
    row, col = iota((128, 256), 0), iota((128, 256), 1)
    turn_pair = jnp.where(col == (row & 31) * 8 + 2 * (row >> 5), 1.0, 0.0).astype(BF16)

    def strips(i, carry):
        cells = [load(2 * i), load(2 * i + 1)]
        first = jnp.concatenate([c[:128] for c in cells], axis=0).astype(BF16)
        last = [c[128:] for c in cells]
        last = [jnp.concatenate([c, pltpu.roll(c, 255, 1)], axis=0) for c in last]
        last = jnp.concatenate(last, axis=0).astype(BF16)
        whole = dot(turn_ref[...], first, (1, 1)).astype(BF16)
        rest = dot(turn_pair, last, (1, 1)).astype(BF16)
        for k in range(2):
            at = pl.ds(pl.multiple_of(i * 64 + k * 32, 32), 32)
            lanes = slice(k * 128, (k + 1) * 128)
            for x in range(8):
                whole_ref[at, x * 128 : (x + 1) * 128] = whole[x * 32 : (x + 1) * 32, lanes]
            for x in range(4):
                rest_ref[at, x * 128 : (x + 1) * 128] = rest[x * 32 : (x + 1) * 32, lanes]
        return carry

    lax.fori_loop(0, 8, strips, 0, unroll=UNROLL)

    for part_ref, turn_back_ref, lanes in (
        (whole_ref, once_ref, slice(0, 1024)),
        (rest_ref, pair_ref, slice(1024, 1536)),
    ):
        picked = dot(pick_ref[...], part_ref[...]).astype(BF16)
        picked = dot(picked, turn_back_ref[...]).astype(BF16)
        out_ref[:, lanes] = dot(slot_ref[...], picked).astype(BF16)


CUT_SCRATCH = [
    pltpu.VMEM((1024, 1024), BF16),
    pltpu.VMEM((512, 512), BF16),
    pltpu.VMEM((256, 256), BF16),
    pltpu.VMEM((512, 1024), BF16),
    pltpu.VMEM((512, 512), BF16),
]


def old_kernel(field_hbm, anchor_ref, dest_ref, out_ref, pick_ref, slot_ref, field_ref, sem, *scratch):
    fetch = pltpu.make_async_copy(field_hbm, field_ref, sem)
    fetch.start()
    selections(*scratch[:3])
    target = dest_ref[...].astype(F32)
    row, col = iota((256, 256), 0), iota((256, 256), 1)

    def upright(line):
        return jnp.sum(jnp.where(row == col, jnp.broadcast_to(line, (256, 256)), 0.0), axis=1, keepdims=True)

    ahead = jnp.where((upright(target) == target) & (row < col), 1.0, 0.0)
    slot = target * 16.0 + jnp.sum(ahead, axis=0, keepdims=True)
    patch = ((anchor_ref[1] >> 3) & 15) * 32 + ((anchor_ref[2] >> 3) & 31)
    patch = upright(patch.astype(F32)).astype(jnp.int32)
    pick_ref[...] = jnp.where(iota((256, 512), 1) == patch, 1.0, 0.0).astype(BF16)
    sent = jnp.where(iota((512, 256), 0) == slot.astype(jnp.int32), 1.0, 0.0)
    slot_ref[...] = sent.astype(BF16)
    tag = jnp.sum(sent, axis=1, keepdims=True)
    out_ref[:, 1536:1664] = jnp.broadcast_to(tag, (512, 128)).astype(BF16)
    fetch.wait()

    def load(by):
        at = pl.ds(pl.multiple_of(by * 8, 8), 8)
        return field_ref[:, :, at, :].reshape(192, 256)

    cut_patches(load, pick_ref, slot_ref, out_ref, *scratch)


def new_kernel(
    field_hbm, z_prev_ref, z_next_ref, y_prev_ref, y_next_ref, pick_ref, slot_ref,
    new_hbm, out_ref, pad_ref, new_ref, sem, *scratch,
):
    fetch = pltpu.make_async_copy(field_hbm, pad_ref.at[:, 1:9, 8:136, :], sem.at[0])
    fetch.start()
    selections(*scratch[:3])
    pad_ref[:, 0:1, 8:136, :] = z_prev_ref[...]
    pad_ref[:, 9:10, 8:136, :] = z_next_ref[...]
    pad_ref[:, 1:9, 7:8, :] = y_prev_ref[...]
    pad_ref[:, 1:9, 136:137, :] = y_next_ref[...]
    fetch.wait()
    near = VISCOSITY * TIME_STEP

    def layer(z, carry):
        for y in range(0, 128, 16):
            along = [pad_ref[c, z + 1, 8 + y : 24 + y, :] for c in range(3)]
            drift = [(0.5 * TIME_STEP) * v for v in along]
            ahead = [near - v for v in drift]
            behind = [near + v for v in drift]
            for c in range(3):
                centre = along[c]
                z_next = pad_ref[c, z + 2, 8 + y : 24 + y, :]
                z_prev = pad_ref[c, z, 8 + y : 24 + y, :]
                y_next = pad_ref[c, z + 1, 9 + y : 25 + y, :]
                y_prev = pad_ref[c, z + 1, 7 + y : 23 + y, :]
                x_next = pltpu.roll(centre, 255, 1)
                x_prev = pltpu.roll(centre, 1, 1)
                new_ref[c, z, y : y + 16, :] = (
                    (1.0 - 6.0 * near) * centre
                    + (ahead[0] * x_next + behind[0] * x_prev)
                    + (ahead[1] * y_next + behind[1] * y_prev)
                    + (ahead[2] * z_next + behind[2] * z_prev)
                )
        return carry

    lax.fori_loop(0, 8, layer, 0)
    store = pltpu.make_async_copy(new_ref, new_hbm, sem.at[1])
    store.start()

    def load(by):
        at = pl.ds(pl.multiple_of(by * 8, 8), 8)
        return new_ref[:, :, at, :].reshape(192, 256)

    cut_patches(load, pick_ref, slot_ref, out_ref, *scratch)
    store.wait()


def pack(blocks):
    row, col = iota((128, 128), 0), iota((128, 128), 1)
    return jnp.where(row // 64 == col // 64, blocks[0], pltpu.roll(blocks[1], 64, 1))


def unpack(packed):
    row, col = iota((128, 128), 0), iota((128, 128), 1)
    own = row // 64 == col // 64
    return jnp.where(own, packed, 0.0), jnp.where(own, pltpu.roll(packed, 64, 1), 0.0)


def quartets(packed, high_ref, low_ref):
    blank = jnp.zeros((128, 128), F32)
    for p in range(2):
        one, two = unpack(packed[p * 128 : (p + 1) * 128])
        whole = jnp.concatenate(
            [jnp.concatenate([one, blank], axis=1), jnp.concatenate([blank, two], axis=1)], axis=0
        )
        high_ref[p], low_ref[p] = split(whole)


def absolute(m, j):
    return pl.multiple_of(((m - j) & 3) * 128, 128)


def forward_kernel(
    place_ref, old_ref, lift_w_ref, w0_ref, w1_ref, w2_ref, w3_ref,
    lifted_ref, query_ref, key_ref, key_spread_ref, value_ref, value_spread_ref,
    query_w_ref, key_w_ref, value_w_ref, out_w_ref, sums_ref, acc_ref,
):
    m = place_ref[0]
    for j, block in enumerate((w0_ref, w1_ref, w2_ref, w3_ref)):
        at = pl.ds(absolute(m, j), 128)
        query_w_ref[:, at] = block[0]
        key_w_ref[:, at] = block[1]
        value_w_ref[:, at] = block[2]
        for k in range(4):
            out_w_ref[at, k * 128 : (k + 1) * 128] = block[3, k * 128 : (k + 1) * 128, :]
    acc_ref[...] = jnp.zeros_like(acc_ref)
    mix = mean_matrix()

    def rows(i, carry):
        at = pl.ds(pl.multiple_of(i * CHUNK, CHUNK), CHUNK)
        lifted = dot(old_ref[at, 0:1536], lift_w_ref[...]).astype(BF16)
        lifted_ref[at, :] = lifted
        query_ref[at, :] = dot(lifted, query_w_ref[...]).astype(BF16)
        normed = []
        for w_ref, hat_ref, spread_ref in (
            (key_w_ref, key_ref, key_spread_ref),
            (value_w_ref, value_ref, value_spread_ref),
        ):
            heads = dot(lifted, w_ref[...])
            shifted = heads - head_mean(heads, mix)
            spread = jnp.sqrt(head_mean(shifted * shifted, mix, 1) + EPSILON)
            hat = shifted / spread
            normed.append(hat.astype(BF16))
            hat_ref[at, :] = normed[-1]
            spread_ref[at, :] = spread
        for p in range(4):
            part = slice(p * 128, (p + 1) * 128)
            acc_ref[p] += dot(normed[0][:, part], normed[1][:, part], (0, 0))
        return carry

    lax.fori_loop(0, 512 // CHUNK, rows, 0)
    sums_ref[0:128, :] = pack((acc_ref[0], acc_ref[1]))
    sums_ref[128:256, :] = pack((acc_ref[2], acc_ref[3]))
    count = jnp.sum(old_ref[:, 1536:1664].astype(F32), axis=0, keepdims=True)
    sums_ref[256:264, :] = jnp.broadcast_to(count, (8, 128))


def dealer(place_ref, mine_ref, theirs_ref):
    first = place_ref[1] == 0

    def deal(grad, rows, n, at):
        grad = grad.reshape(16, 2, rows, 128)
        even, odd = grad[:, 0], grad[:, 1]
        mine_ref[:, n, at : at + rows, :] = jnp.where(first, even, odd).astype(BF16)
        theirs_ref[:, n, at : at + rows, :] = jnp.where(first, odd, even).astype(BF16)

    return deal


def middle_kernel(
    place_ref, s0_ref, s1_ref, s2_ref, s3_ref, lifted_ref, query_ref, new_ref, out_w_ref, proj_w_ref,
    mine_ref, theirs_ref, d_query_ref, d_hidden_ref, sums_ref, count_ref,
    hidden_ref, d_guess_ref, attended_ref, d_tokens_ref, acc_ref, high_ref, low_ref, loss_ref,
):
    total = (s0_ref[...] + s1_ref[...]) + (s2_ref[...] + s3_ref[...])
    count = total[256:264, :]
    count_ref[...] = count
    quartets(total[0:256] / count[0:1, :], high_ref, low_ref)
    acc_ref[...] = jnp.zeros_like(acc_ref)
    loss_ref[...] = jnp.zeros_like(loss_ref)

    def rows(i, carry):
        at = pl.ds(pl.multiple_of(i * CHUNK, CHUNK), CHUNK)
        query = query_ref[at, :]
        parts = []
        for p in range(2):
            part = query[:, p * 256 : (p + 1) * 256]
            parts.append(dot(part, high_ref[p]) + dot(part, low_ref[p]))
        attended = jnp.concatenate(parts, axis=1).astype(BF16)
        attended_ref[at, :] = attended
        mixed = dot(attended, out_w_ref[...])
        hidden = (lifted_ref[at, :].astype(F32) + mixed).astype(BF16)
        hidden_ref[at, :] = hidden
        error = dot(hidden, proj_w_ref[...]) - new_ref[at, :].astype(F32)
        loss_ref[...] += jnp.sum((error * error).reshape(CHUNK // 8, 8, 1536), axis=0)
        d_guess = (error * (1.0 / 32768)).astype(BF16)
        d_guess_ref[at, :] = d_guess
        d_hidden = dot(d_guess, proj_w_ref[...], (1, 1))
        d_hidden_ref[at, :] = d_hidden
        d_tokens = d_hidden.astype(BF16)
        d_tokens_ref[at, :] = d_tokens
        high, low = split(dot(d_tokens, out_w_ref[...], (1, 1)))
        for p in range(2):
            part = slice(p * 256, (p + 1) * 256)
            back = (
                dot(high[:, part], high_ref[p], (1, 1))
                + dot(high[:, part], low_ref[p], (1, 1))
                + dot(low[:, part], high_ref[p], (1, 1))
            )
            d_query_ref[at, part] = back.astype(BF16)
        for p in range(4):
            part = slice(p * 128, (p + 1) * 128)
            acc_ref[p] += dot(query[:, part], high[:, part], (0, 0)) + dot(
                query[:, part], low[:, part], (0, 0)
            )
        return carry

    lax.fori_loop(0, 512 // CHUNK, rows, 0)
    sums_ref[0:128, :] = pack((acc_ref[0], acc_ref[1]))
    sums_ref[128:256, :] = pack((acc_ref[2], acc_ref[3]))
    loss = jnp.sum(loss_ref[...], axis=(0, 1), keepdims=True) * (1.0 / 50331648)
    sums_ref[256:264, :] = jnp.broadcast_to(loss, (8, 128))
    deal = dealer(place_ref, mine_ref, theirs_ref)
    grad = dot(hidden_ref[...], d_guess_ref[...], (0, 0))
    for n in range(4):
        for j in range(3):
            at = n * 384 + j * 128
            deal(grad[:, at : at + 128], 16, n, 16 * j)
    grad = dot(d_tokens_ref[...], attended_ref[...], (0, 0))
    for n in range(4):
        deal(grad[:, n * 128 : (n + 1) * 128], 16, n, 48)


def backward_kernel(
    place_ref, s0_ref, s1_ref, s2_ref, s3_ref, count_ref, old_hbm, lifted_ref, key_ref, key_spread_ref,
    value_ref, value_spread_ref, d_query_ref, d_hidden_ref, query_w_ref, key_w_ref, value_w_ref,
    mine_ref, theirs_ref, loss_ref, high_ref, low_ref, d_heads_ref, d_lifted_ref, old_ref, sem,
):
    fetch = pltpu.make_async_copy(old_hbm.at[:, 0:1536], old_ref, sem)
    fetch.start()
    total = (s0_ref[...] + s1_ref[...]) + (s2_ref[...] + s3_ref[...])
    loss_ref[...] = total[256:264, :]
    quartets(total[0:256] / count_ref[0:1, :], high_ref, low_ref)
    mix = mean_matrix()

    def rows(i, carry):
        at = pl.ds(pl.multiple_of(i * CHUNK, CHUNK), CHUNK)
        d_query = d_query_ref[at, :]
        d_heads_ref[at, 0:512] = d_query
        d_lifted = d_hidden_ref[at, :] + dot(d_query, query_w_ref[...], (1, 1))
        for hat_ref, spread_ref, other_ref, across, lanes, w_ref in (
            (key_ref, key_spread_ref, value_ref, (1, 1), 512, key_w_ref),
            (value_ref, value_spread_ref, key_ref, (1, 0), 1024, value_w_ref),
        ):
            other = other_ref[at, :]
            parts = []
            for p in range(2):
                part = other[:, p * 256 : (p + 1) * 256]
                parts.append(dot(part, high_ref[p], across) + dot(part, low_ref[p], across))
            grad = jnp.concatenate(parts, axis=1)
            hat = hat_ref[at, :].astype(F32)
            inner = head_mean(grad, mix)
            cross = head_mean(grad * hat, mix)
            grad = ((grad - inner - hat * cross) / spread_ref[at, :]).astype(BF16)
            d_heads_ref[at, lanes : lanes + 512] = grad
            d_lifted = d_lifted + dot(grad, w_ref[...], (1, 1))
        d_lifted_ref[at, :] = d_lifted.astype(BF16)
        return carry

    lax.fori_loop(0, 512 // CHUNK, rows, 0)
    deal = dealer(place_ref, mine_ref, theirs_ref)
    grad = dot(lifted_ref[...], d_heads_ref[...], (0, 0))
    for n in range(4):
        for j in range(3):
            at = 512 * j + 128 * n
            deal(grad[:, at : at + 128], 16, n, 48 + 16 * j)
    fetch.wait()
    grad = dot(old_ref[...], d_lifted_ref[...], (0, 0))
    for n in range(4):
        deal(grad[:, n * 128 : (n + 1) * 128], 48, n, 0)


def last_kernel(
    place_ref, r0_ref, r1_ref, r2_ref, r3_ref, heads_ref,
    lift_ref, query_ref, key_ref, value_ref, out_ref, proj_ref, loss_ref,
):
    m = place_ref[0]
    for j, block in enumerate((r0_ref, r1_ref, r2_ref, r3_ref)):
        lift_ref[:, pl.ds(absolute(m, j), 128)] = block[0:48, :]
        for k in range(3):
            at = pl.multiple_of(((m - j) & 3) * 384 + k * 128, 128)
            proj_ref[:, pl.ds(at, 128)] = block[48 + 16 * k : 64 + 16 * k, :]
    query_ref[...] = heads_ref[:, 0:16, :].astype(F32).reshape(512, 128)
    key_ref[...] = heads_ref[:, 16:32, :].astype(F32).reshape(512, 128)
    value_ref[...] = heads_ref[:, 32:48, :].astype(F32).reshape(512, 128)
    out_ref[...] = heads_ref[:, 48:64, :].astype(F32).reshape(512, 128).T
    loss = jnp.sum(heads_ref[:, 64:80, :].astype(F32), axis=0)
    loss_ref[...] = loss[0:1, 0:1] + loss[1:2, 0:1]


def call(body, outs, scratch=(), ins="", results=None):
    spaces = {"s": pltpu.SMEM, "h": pl.ANY, "v": pltpu.VMEM}
    return pl.pallas_call(
        body,
        out_shape=[jax.ShapeDtypeStruct(shape, kind) for shape, kind in outs],
        in_specs=[pl.BlockSpec(memory_space=spaces[k]) for k in ins],
        out_specs=[pl.BlockSpec(memory_space=spaces[k]) for k in results or "v" * len(outs)],
        scratch_shapes=list(scratch),
        compiler_params=pltpu.CompilerParams(vmem_limit_bytes=60 << 20),
    )


def around(value):
    got = [value]
    for d in (1, 2, 3):
        got.append(lax.ppermute(value, "mp", [(i, (i + d) % 4) for i in range(4)]))
    return got


def exchange(value, axes):
    return lax.all_to_all(value, axes, split_axis=0, concat_axis=0, tiled=True)


def pair_sum(mine, theirs):
    got = lax.ppermute(theirs, "slab", [(i, i ^ 1) for i in range(32)])
    return (mine.astype(F32) + got.astype(F32)).astype(BF16)


def total(partial):
    groups = [[(2 * q + c) * 4 + n for q in range(16) for n in range(4)] for c in range(2)]
    got = lax.all_to_all(
        partial.reshape(64, -1, 128),
        ("slab", "mp"),
        split_axis=0,
        concat_axis=0,
        axis_index_groups=groups,
        tiled=True,
    )
    return jnp.sum(got.astype(F32), axis=0)


def step(velocity, anchors, dest, w_lift, w_query, w_key, w_value, w_out, w_proj):
    slabs = lax.axis_size("slab")
    place = jnp.stack([lax.axis_index("mp"), lax.axis_index("slab") & 1])
    up = [(i, (i + 1) % slabs) for i in range(slabs)]
    z_prev = lax.ppermute(velocity[:, 7:8], "slab", up)
    z_next = lax.ppermute(velocity[:, 0:1], "slab", [(j, i) for i, j in up])
    up = [(i, (i + 1) % 4) for i in range(4)]
    y_prev = lax.ppermute(velocity[:, :, 127:128], "mp", up)
    y_next = lax.ppermute(velocity[:, :, 0:1], "mp", [(j, i) for i, j in up])
    tall = jnp.concatenate([w_out[:, k * 128 : (k + 1) * 128] for k in range(4)], axis=0)
    heads_w = around(jnp.stack([w_query, w_key, w_value, tall]))

    send_old, pick, slot = call(
        old_kernel,
        [((512, 1664), BF16), ((256, 512), BF16), ((512, 256), BF16)],
        [pltpu.VMEM((3, 8, 128, 256), F32), pltpu.SemaphoreType.DMA] + CUT_SCRATCH,
        "hvv",
    )(velocity, anchors.reshape(3, 1, 256), dest.reshape(1, 256))
    old = exchange(send_old, "slab")
    new_velocity, send_new = call(
        new_kernel,
        [((3, 8, 128, 256), F32), ((512, 1536), BF16)],
        [
            pltpu.VMEM((3, 10, 144, 256), F32),
            pltpu.VMEM((3, 8, 128, 256), F32),
            pltpu.SemaphoreType.DMA((2,)),
        ]
        + CUT_SCRATCH,
        "hvvvvvv",
        "hv",
    )(velocity, z_prev, z_next, y_prev, y_next, pick, slot)
    new = exchange(send_new, "slab")

    wide, wide_f = ((512, 512), BF16), ((512, 512), F32)
    lifted, query, key, key_spread, value, value_spread, wq, wk, wv, wo, sums = call(
        forward_kernel,
        [wide, wide, wide, wide_f, wide, wide_f, wide, wide, wide, wide, ((264, 128), F32)],
        [pltpu.VMEM((4, 128, 128), F32)],
        "svvvvvv",
    )(place, old, w_lift, *heads_w)
    sums = around(sums)
    mine, theirs, d_query, d_hidden, d_sums, count = call(
        middle_kernel,
        [((16, 4, 64, 128), BF16), ((16, 4, 64, 128), BF16), wide, wide_f, ((264, 128), F32), ((8, 128), F32)],
        [
            pltpu.VMEM((512, 512), BF16),
            pltpu.VMEM((512, 1536), BF16),
            pltpu.VMEM((512, 512), BF16),
            pltpu.VMEM((512, 512), BF16),
            pltpu.VMEM((4, 128, 128), F32),
            pltpu.VMEM((2, 256, 256), BF16),
            pltpu.VMEM((2, 256, 256), BF16),
            pltpu.VMEM((8, 1536), F32),
        ],
        "svvvvvvvvv",
    )(place, *sums, lifted, query, new, wo, w_proj)
    d_sums = around(d_sums)
    total_out = total(pair_sum(mine, theirs))
    mine, theirs, loss_part = call(
        backward_kernel,
        [((16, 4, 96, 128), BF16), ((16, 4, 96, 128), BF16), ((8, 128), F32)],
        [
            pltpu.VMEM((2, 256, 256), BF16),
            pltpu.VMEM((2, 256, 256), BF16),
            pltpu.VMEM((512, 1536), BF16),
            pltpu.VMEM((512, 512), BF16),
            pltpu.VMEM((512, 1536), BF16),
            pltpu.SemaphoreType.DMA,
        ],
        "svvvvvhvvvvvvvvvv",
    )(place, *d_sums, count, old, lifted, key, key_spread, value, value_spread, d_query, d_hidden, wq, wk, wv)
    total_in = total(pair_sum(mine, theirs))
    blocks = jnp.concatenate([total_in[0:48], total_out[0:48]], axis=0)
    loss_high = loss_part.astype(BF16)
    loss_low = (loss_part - loss_high.astype(F32)).astype(BF16)
    heads = jnp.concatenate([total_in[48:96], total_out[48:64]], axis=0).astype(BF16)
    heads = jnp.concatenate([heads, loss_high[0:1], loss_low[0:1], jnp.zeros((14, 128), BF16)], axis=0)
    heads = exchange(jnp.broadcast_to(heads[None], (32, 80, 128)), "slab")
    lift, g_query, g_key, g_value, g_out, proj, loss = call(
        last_kernel,
        [
            ((48, 512), F32),
            ((512, 128), F32),
            ((512, 128), F32),
            ((512, 128), F32),
            ((128, 512), F32),
            ((16, 1536), F32),
            ((1, 1), F32),
        ],
        (),
        "svvvvv",
    )(place, *around(blocks), heads)
    return (new_velocity, loss.reshape(()), lift, g_query, g_key, g_value, g_out, proj)


def solution(mesh):
    return jax.shard_map(
        step,
        mesh=mesh,
        in_specs=(
            P(None, "slab", "mp", None),
            P(None, "slab", "mp", None),
            P("slab", "mp", None, None),
            P(),
            P(None, "mp"),
            P(None, "mp"),
            P(None, "mp"),
            P("mp", None),
            P(),
        ),
        out_specs=(
            P(None, "slab", "mp", None),
            P(),
            P("slab", None),
            P(None, "mp"),
            P(None, "mp"),
            P(None, "mp"),
            P("mp", None),
            P("slab", None),
        ),
        check_vma=False,
    )
```

```python
import jax
import jax.numpy as jnp
from jax import lax
from jax.experimental import pallas as pl
from jax.experimental.pallas import tpu as pltpu
from jax.sharding import PartitionSpec as P


TIME_STEP = 0.1
VISCOSITY = 0.2
EPSILON = 1e-05
F32 = jnp.float32
BF16 = jnp.bfloat16
CHUNK = 512
UNROLL = 2


def iota(shape, dim):
    return lax.broadcasted_iota(jnp.int32, shape, dim)


def dot(a, b, contract=(1, 0)):
    dims = (((contract[0],), (contract[1],)), ((), ()))
    return lax.dot_general(a, b, dims, preferred_element_type=F32)


def split(a):
    high = a.astype(BF16)
    return high, (a - high.astype(F32)).astype(BF16)


def head_mean(a, mix, terms=2):
    halves = []
    for at in (0, 256):
        parts = split(a[:, at : at + 256])[:terms]
        halves.append(sum(dot(part, mix) for part in parts))
    return jnp.concatenate(halves, axis=1)


def mean_matrix():
    same = iota((256, 256), 0) // 64 == iota((256, 256), 1) // 64
    return jnp.where(same, 1.0 / 64, 0.0).astype(BF16)


def selections(once_ref, pair_ref, turn_ref):
    row, col = iota((256, 256), 0), iota((256, 256), 1)
    turn_ref[...] = jnp.where(col == (row & 31) * 8 + (row >> 5), 1.0, 0.0).astype(BF16)

    def spread(i, carry):
        at = pl.ds(pl.multiple_of(i * 128, 128), 128)
        row, col = iota((128, 1024), 0), iota((128, 1024), 1)
        once_ref[at, :] = jnp.where(col == 8 * row + i, 1.0, 0.0).astype(BF16)
        return carry

    lax.fori_loop(0, 8, spread, 0)
    row, col = iota((512, 512), 0), iota((512, 512), 1)
    pair_ref[...] = jnp.where(col == 8 * (row & 63) + (row >> 6), 1.0, 0.0).astype(BF16)


def cut_patches(load, pick_ref, slot_ref, out_ref, once_ref, pair_ref, turn_ref, whole_ref, rest_ref):
    row, col = iota((128, 256), 0), iota((128, 256), 1)
    turn_pair = jnp.where(col == (row & 31) * 8 + 2 * (row >> 5), 1.0, 0.0).astype(BF16)

    def strips(i, carry):
        cells = [load(2 * i), load(2 * i + 1)]
        first = jnp.concatenate([c[:128] for c in cells], axis=0).astype(BF16)
        last = [c[128:] for c in cells]
        last = [jnp.concatenate([c, pltpu.roll(c, 255, 1)], axis=0) for c in last]
        last = jnp.concatenate(last, axis=0).astype(BF16)
        whole = dot(turn_ref[...], first, (1, 1)).astype(BF16)
        rest = dot(turn_pair, last, (1, 1)).astype(BF16)
        for k in range(2):
            at = pl.ds(pl.multiple_of(i * 64 + k * 32, 32), 32)
            lanes = slice(k * 128, (k + 1) * 128)
            for x in range(8):
                whole_ref[at, x * 128 : (x + 1) * 128] = whole[x * 32 : (x + 1) * 32, lanes]
            for x in range(4):
                rest_ref[at, x * 128 : (x + 1) * 128] = rest[x * 32 : (x + 1) * 32, lanes]
        return carry

    lax.fori_loop(0, 8, strips, 0, unroll=UNROLL)

    for part_ref, turn_back_ref, lanes in (
        (whole_ref, once_ref, slice(0, 1024)),
        (rest_ref, pair_ref, slice(1024, 1536)),
    ):
        picked = dot(pick_ref[...], part_ref[...]).astype(BF16)
        picked = dot(picked, turn_back_ref[...]).astype(BF16)
        out_ref[:, lanes] = dot(slot_ref[...], picked).astype(BF16)


CUT_SCRATCH = [
    pltpu.VMEM((1024, 1024), BF16),
    pltpu.VMEM((512, 512), BF16),
    pltpu.VMEM((256, 256), BF16),
    pltpu.VMEM((512, 1024), BF16),
    pltpu.VMEM((512, 512), BF16),
]


def old_kernel(field_hbm, anchor_ref, dest_ref, out_ref, pick_ref, slot_ref, field_ref, sem, *scratch):
    fetch = pltpu.make_async_copy(field_hbm, field_ref, sem)
    fetch.start()
    selections(*scratch[:3])
    target = dest_ref[...].astype(F32)
    row, col = iota((256, 256), 0), iota((256, 256), 1)

    def upright(line):
        return jnp.sum(jnp.where(row == col, jnp.broadcast_to(line, (256, 256)), 0.0), axis=1, keepdims=True)

    ahead = jnp.where((upright(target) == target) & (row < col), 1.0, 0.0)
    slot = target * 16.0 + jnp.sum(ahead, axis=0, keepdims=True)
    patch = ((anchor_ref[1] >> 3) & 15) * 32 + ((anchor_ref[2] >> 3) & 31)
    patch = upright(patch.astype(F32)).astype(jnp.int32)
    pick_ref[...] = jnp.where(iota((256, 512), 1) == patch, 1.0, 0.0).astype(BF16)
    sent = jnp.where(iota((512, 256), 0) == slot.astype(jnp.int32), 1.0, 0.0)
    slot_ref[...] = sent.astype(BF16)
    tag = jnp.sum(sent, axis=1, keepdims=True)
    out_ref[:, 1536:1664] = jnp.broadcast_to(tag, (512, 128)).astype(BF16)
    fetch.wait()

    def load(by):
        at = pl.ds(pl.multiple_of(by * 8, 8), 8)
        return field_ref[:, :, at, :].reshape(192, 256)

    cut_patches(load, pick_ref, slot_ref, out_ref, *scratch)


def new_kernel(
    field_hbm, z_prev_ref, z_next_ref, y_prev_ref, y_next_ref, pick_ref, slot_ref,
    new_hbm, out_ref, pad_ref, new_ref, sem, *scratch,
):
    fetch = pltpu.make_async_copy(field_hbm, pad_ref.at[:, 1:9, 8:136, :], sem.at[0])
    fetch.start()
    selections(*scratch[:3])
    pad_ref[:, 0:1, 8:136, :] = z_prev_ref[...]
    pad_ref[:, 9:10, 8:136, :] = z_next_ref[...]
    pad_ref[:, 1:9, 7:8, :] = y_prev_ref[...]
    pad_ref[:, 1:9, 136:137, :] = y_next_ref[...]
    fetch.wait()
    near = VISCOSITY * TIME_STEP

    def layer(z, carry):
        for y in range(0, 128, 16):
            along = [pad_ref[c, z + 1, 8 + y : 24 + y, :] for c in range(3)]
            drift = [(0.5 * TIME_STEP) * v for v in along]
            ahead = [near - v for v in drift]
            behind = [near + v for v in drift]
            for c in range(3):
                centre = along[c]
                z_next = pad_ref[c, z + 2, 8 + y : 24 + y, :]
                z_prev = pad_ref[c, z, 8 + y : 24 + y, :]
                y_next = pad_ref[c, z + 1, 9 + y : 25 + y, :]
                y_prev = pad_ref[c, z + 1, 7 + y : 23 + y, :]
                x_next = pltpu.roll(centre, 255, 1)
                x_prev = pltpu.roll(centre, 1, 1)
                new_ref[c, z, y : y + 16, :] = (
                    (1.0 - 6.0 * near) * centre
                    + (ahead[0] * x_next + behind[0] * x_prev)
                    + (ahead[1] * y_next + behind[1] * y_prev)
                    + (ahead[2] * z_next + behind[2] * z_prev)
                )
        return carry

    lax.fori_loop(0, 8, layer, 0)
    store = pltpu.make_async_copy(new_ref, new_hbm, sem.at[1])
    store.start()

    def load(by):
        at = pl.ds(pl.multiple_of(by * 8, 8), 8)
        return new_ref[:, :, at, :].reshape(192, 256)

    cut_patches(load, pick_ref, slot_ref, out_ref, *scratch)
    store.wait()


def pack(blocks):
    row, col = iota((128, 128), 0), iota((128, 128), 1)
    return jnp.where(row // 64 == col // 64, blocks[0], pltpu.roll(blocks[1], 64, 1))


def unpack(packed):
    row, col = iota((128, 128), 0), iota((128, 128), 1)
    own = row // 64 == col // 64
    return jnp.where(own, packed, 0.0), jnp.where(own, pltpu.roll(packed, 64, 1), 0.0)


def quartets(packed, high_ref, low_ref):
    blank = jnp.zeros((128, 128), F32)
    for p in range(2):
        one, two = unpack(packed[p * 128 : (p + 1) * 128])
        whole = jnp.concatenate(
            [jnp.concatenate([one, blank], axis=1), jnp.concatenate([blank, two], axis=1)], axis=0
        )
        high_ref[p], low_ref[p] = split(whole)


def absolute(m, j):
    return pl.multiple_of(((m - j) & 3) * 128, 128)


def forward_kernel(
    place_ref, old_ref, lift_w_ref, w0_ref, w1_ref, w2_ref, w3_ref,
    lifted_ref, query_ref, key_ref, key_spread_ref, value_ref, value_spread_ref,
    query_w_ref, key_w_ref, value_w_ref, out_w_ref, sums_ref, acc_ref,
):
    m = place_ref[0]
    for j, block in enumerate((w0_ref, w1_ref, w2_ref, w3_ref)):
        at = pl.ds(absolute(m, j), 128)
        query_w_ref[:, at] = block[0]
        key_w_ref[:, at] = block[1]
        value_w_ref[:, at] = block[2]
        for k in range(4):
            out_w_ref[at, k * 128 : (k + 1) * 128] = block[3, k * 128 : (k + 1) * 128, :]
    acc_ref[...] = jnp.zeros_like(acc_ref)
    mix = mean_matrix()

    def rows(i, carry):
        at = pl.ds(pl.multiple_of(i * CHUNK, CHUNK), CHUNK)
        lifted = dot(old_ref[at, 0:1536], lift_w_ref[...]).astype(BF16)
        lifted_ref[at, :] = lifted
        query_ref[at, :] = dot(lifted, query_w_ref[...]).astype(BF16)
        normed = []
        for w_ref, hat_ref, spread_ref in (
            (key_w_ref, key_ref, key_spread_ref),
            (value_w_ref, value_ref, value_spread_ref),
        ):
            heads = dot(lifted, w_ref[...])
            shifted = heads - head_mean(heads, mix)
            spread = jnp.sqrt(head_mean(shifted * shifted, mix, 1) + EPSILON)
            hat = shifted / spread
            normed.append(hat.astype(BF16))
            hat_ref[at, :] = normed[-1]
            spread_ref[at, :] = spread
        for p in range(4):
            part = slice(p * 128, (p + 1) * 128)
            acc_ref[p] += dot(normed[0][:, part], normed[1][:, part], (0, 0))
        return carry

    lax.fori_loop(0, 512 // CHUNK, rows, 0)
    sums_ref[0:128, :] = pack((acc_ref[0], acc_ref[1]))
    sums_ref[128:256, :] = pack((acc_ref[2], acc_ref[3]))
    count = jnp.sum(old_ref[:, 1536:1664].astype(F32), axis=0, keepdims=True)
    sums_ref[256:264, :] = jnp.broadcast_to(count, (8, 128))


def dealer(place_ref, mine_ref, theirs_ref):
    first = place_ref[1] == 0

    def deal(grad, rows, n, at):
        grad = grad.reshape(16, 2, rows, 128)
        even, odd = grad[:, 0], grad[:, 1]
        mine_ref[:, n, at : at + rows, :] = jnp.where(first, even, odd).astype(BF16)
        theirs_ref[:, n, at : at + rows, :] = jnp.where(first, odd, even).astype(BF16)

    return deal


def middle_kernel(
    place_ref, s0_ref, s1_ref, s2_ref, s3_ref, lifted_ref, query_ref, new_ref, out_w_ref, proj_w_ref,
    mine_ref, theirs_ref, d_query_ref, d_hidden_ref, sums_ref, count_ref,
    hidden_ref, d_guess_ref, attended_ref, d_tokens_ref, acc_ref, high_ref, low_ref, loss_ref,
):
    total = (s0_ref[...] + s1_ref[...]) + (s2_ref[...] + s3_ref[...])
    count = total[256:264, :]
    count_ref[...] = count
    quartets(total[0:256] / count[0:1, :], high_ref, low_ref)
    acc_ref[...] = jnp.zeros_like(acc_ref)
    loss_ref[...] = jnp.zeros_like(loss_ref)

    def rows(i, carry):
        at = pl.ds(pl.multiple_of(i * CHUNK, CHUNK), CHUNK)
        query = query_ref[at, :]
        parts = []
        for p in range(2):
            part = query[:, p * 256 : (p + 1) * 256]
            parts.append(dot(part, high_ref[p]) + dot(part, low_ref[p]))
        attended = jnp.concatenate(parts, axis=1).astype(BF16)
        attended_ref[at, :] = attended
        mixed = dot(attended, out_w_ref[...])
        hidden = (lifted_ref[at, :].astype(F32) + mixed).astype(BF16)
        hidden_ref[at, :] = hidden
        error = dot(hidden, proj_w_ref[...]) - new_ref[at, :].astype(F32)
        loss_ref[...] += jnp.sum((error * error).reshape(CHUNK // 8, 8, 1536), axis=0)
        d_guess = (error * (1.0 / 32768)).astype(BF16)
        d_guess_ref[at, :] = d_guess
        d_hidden = dot(d_guess, proj_w_ref[...], (1, 1))
        d_hidden_ref[at, :] = d_hidden
        d_tokens = d_hidden.astype(BF16)
        d_tokens_ref[at, :] = d_tokens
        high, low = split(dot(d_tokens, out_w_ref[...], (1, 1)))
        for p in range(2):
            part = slice(p * 256, (p + 1) * 256)
            back = (
                dot(high[:, part], high_ref[p], (1, 1))
                + dot(high[:, part], low_ref[p], (1, 1))
                + dot(low[:, part], high_ref[p], (1, 1))
            )
            d_query_ref[at, part] = back.astype(BF16)
        for p in range(4):
            part = slice(p * 128, (p + 1) * 128)
            acc_ref[p] += dot(query[:, part], high[:, part], (0, 0)) + dot(
                query[:, part], low[:, part], (0, 0)
            )
        return carry

    lax.fori_loop(0, 512 // CHUNK, rows, 0)
    sums_ref[0:128, :] = pack((acc_ref[0], acc_ref[1])).astype(BF16)
    sums_ref[128:256, :] = pack((acc_ref[2], acc_ref[3])).astype(BF16)
    loss = jnp.sum(loss_ref[...], axis=(0, 1), keepdims=True) * (1.0 / 50331648)
    sums_ref[256:272, :], sums_ref[272:288, :] = split(jnp.broadcast_to(loss, (16, 128)))
    deal = dealer(place_ref, mine_ref, theirs_ref)
    grad = dot(hidden_ref[...], d_guess_ref[...], (0, 0))
    for n in range(4):
        for j in range(3):
            at = n * 384 + j * 128
            deal(grad[:, at : at + 128], 16, n, 16 * j)
    grad = dot(d_tokens_ref[...], attended_ref[...], (0, 0))
    for n in range(4):
        deal(grad[:, n * 128 : (n + 1) * 128], 16, n, 48)


def backward_kernel(
    place_ref, s0_ref, s1_ref, s2_ref, s3_ref, count_ref, old_hbm, lifted_ref, key_ref, key_spread_ref,
    value_ref, value_spread_ref, d_query_ref, d_hidden_ref, query_w_ref, key_w_ref, value_w_ref,
    mine_ref, theirs_ref, loss_ref, high_ref, low_ref, d_heads_ref, d_lifted_ref, old_ref, sem,
):
    fetch = pltpu.make_async_copy(old_hbm.at[:, 0:1536], old_ref, sem)
    fetch.start()
    s0, s1, s2, s3 = [ref[...].astype(F32) for ref in (s0_ref, s1_ref, s2_ref, s3_ref)]
    total = (s0 + s1) + (s2 + s3)
    loss_ref[...] = total[256:264, :] + total[272:280, :]
    quartets(total[0:256] / count_ref[0:1, :], high_ref, low_ref)
    mix = mean_matrix()

    def rows(i, carry):
        at = pl.ds(pl.multiple_of(i * CHUNK, CHUNK), CHUNK)
        d_query = d_query_ref[at, :]
        d_heads_ref[at, 0:512] = d_query
        d_lifted = d_hidden_ref[at, :] + dot(d_query, query_w_ref[...], (1, 1))
        for hat_ref, spread_ref, other_ref, across, lanes, w_ref in (
            (key_ref, key_spread_ref, value_ref, (1, 1), 512, key_w_ref),
            (value_ref, value_spread_ref, key_ref, (1, 0), 1024, value_w_ref),
        ):
            other = other_ref[at, :]
            parts = []
            for p in range(2):
                part = other[:, p * 256 : (p + 1) * 256]
                parts.append(dot(part, high_ref[p], across) + dot(part, low_ref[p], across))
            grad = jnp.concatenate(parts, axis=1)
            hat = hat_ref[at, :].astype(F32)
            inner = head_mean(grad, mix)
            cross = head_mean(grad * hat, mix)
            grad = ((grad - inner - hat * cross) / spread_ref[at, :]).astype(BF16)
            d_heads_ref[at, lanes : lanes + 512] = grad
            d_lifted = d_lifted + dot(grad, w_ref[...], (1, 1))
        d_lifted_ref[at, :] = d_lifted.astype(BF16)
        return carry

    lax.fori_loop(0, 512 // CHUNK, rows, 0)
    deal = dealer(place_ref, mine_ref, theirs_ref)
    grad = dot(lifted_ref[...], d_heads_ref[...], (0, 0))
    for n in range(4):
        for j in range(3):
            at = 512 * j + 128 * n
            deal(grad[:, at : at + 128], 16, n, 48 + 16 * j)
    fetch.wait()
    grad = dot(old_ref[...], d_lifted_ref[...], (0, 0))
    for n in range(4):
        deal(grad[:, n * 128 : (n + 1) * 128], 48, n, 0)


def last_kernel(
    place_ref, r0_ref, r1_ref, r2_ref, r3_ref, heads_ref,
    lift_ref, query_ref, key_ref, value_ref, out_ref, proj_ref, loss_ref,
):
    m = place_ref[0]
    for j, block in enumerate((r0_ref, r1_ref, r2_ref, r3_ref)):
        lift_ref[:, pl.ds(absolute(m, j), 128)] = block[0:48, :]
        for k in range(3):
            at = pl.multiple_of(((m - j) & 3) * 384 + k * 128, 128)
            proj_ref[:, pl.ds(at, 128)] = block[48 + 16 * k : 64 + 16 * k, :]
    query_ref[...] = heads_ref[:, 0:16, :].astype(F32).reshape(512, 128)
    key_ref[...] = heads_ref[:, 16:32, :].astype(F32).reshape(512, 128)
    value_ref[...] = heads_ref[:, 32:48, :].astype(F32).reshape(512, 128)
    out_ref[...] = heads_ref[:, 48:64, :].astype(F32).reshape(512, 128).T
    loss = jnp.sum(heads_ref[:, 64:80, :].astype(F32), axis=0)
    loss_ref[...] = loss[0:1, 0:1] + loss[1:2, 0:1]


def call(body, outs, scratch=(), ins="", results=None):
    spaces = {"s": pltpu.SMEM, "h": pl.ANY, "v": pltpu.VMEM}
    return pl.pallas_call(
        body,
        out_shape=[jax.ShapeDtypeStruct(shape, kind) for shape, kind in outs],
        in_specs=[pl.BlockSpec(memory_space=spaces[k]) for k in ins],
        out_specs=[pl.BlockSpec(memory_space=spaces[k]) for k in results or "v" * len(outs)],
        scratch_shapes=list(scratch),
        compiler_params=pltpu.CompilerParams(vmem_limit_bytes=60 << 20),
    )


def around(value):
    got = [value]
    for d in (1, 2, 3):
        got.append(lax.ppermute(value, "mp", [(i, (i + d) % 4) for i in range(4)]))
    return got


def exchange(value, axes):
    return lax.all_to_all(value, axes, split_axis=0, concat_axis=0, tiled=True)


def pair_sum(mine, theirs):
    got = lax.ppermute(theirs, "slab", [(i, i ^ 1) for i in range(32)])
    return (mine.astype(F32) + got.astype(F32)).astype(BF16)


def total(partial):
    groups = [[(2 * q + c) * 4 + n for q in range(16) for n in range(4)] for c in range(2)]
    got = lax.all_to_all(
        partial.reshape(64, -1, 128),
        ("slab", "mp"),
        split_axis=0,
        concat_axis=0,
        axis_index_groups=groups,
        tiled=True,
    )
    return jnp.sum(got.astype(F32), axis=0)


def step(velocity, anchors, dest, w_lift, w_query, w_key, w_value, w_out, w_proj):
    slabs = lax.axis_size("slab")
    place = jnp.stack([lax.axis_index("mp"), lax.axis_index("slab") & 1])
    up = [(i, (i + 1) % slabs) for i in range(slabs)]
    z_prev = lax.ppermute(velocity[:, 7:8], "slab", up)
    z_next = lax.ppermute(velocity[:, 0:1], "slab", [(j, i) for i, j in up])
    up = [(i, (i + 1) % 4) for i in range(4)]
    y_prev = lax.ppermute(velocity[:, :, 127:128], "mp", up)
    y_next = lax.ppermute(velocity[:, :, 0:1], "mp", [(j, i) for i, j in up])
    tall = jnp.concatenate([w_out[:, k * 128 : (k + 1) * 128] for k in range(4)], axis=0)
    heads_w = around(jnp.stack([w_query, w_key, w_value, tall]))

    send_old, pick, slot = call(
        old_kernel,
        [((512, 1664), BF16), ((256, 512), BF16), ((512, 256), BF16)],
        [pltpu.VMEM((3, 8, 128, 256), F32), pltpu.SemaphoreType.DMA] + CUT_SCRATCH,
        "hvv",
    )(velocity, anchors.reshape(3, 1, 256), dest.reshape(1, 256))
    old = exchange(send_old, "slab")
    new_velocity, send_new = call(
        new_kernel,
        [((3, 8, 128, 256), F32), ((512, 1536), BF16)],
        [
            pltpu.VMEM((3, 10, 144, 256), F32),
            pltpu.VMEM((3, 8, 128, 256), F32),
            pltpu.SemaphoreType.DMA((2,)),
        ]
        + CUT_SCRATCH,
        "hvvvvvv",
        "hv",
    )(velocity, z_prev, z_next, y_prev, y_next, pick, slot)
    new = exchange(send_new, "slab")

    wide, wide_f = ((512, 512), BF16), ((512, 512), F32)
    lifted, query, key, key_spread, value, value_spread, wq, wk, wv, wo, sums = call(
        forward_kernel,
        [wide, wide, wide, wide_f, wide, wide_f, wide, wide, wide, wide, ((264, 128), F32)],
        [pltpu.VMEM((4, 128, 128), F32)],
        "svvvvvv",
    )(place, old, w_lift, *heads_w)
    sums = around(sums)
    mine, theirs, d_query, d_hidden, d_sums, count = call(
        middle_kernel,
        [((16, 4, 64, 128), BF16), ((16, 4, 64, 128), BF16), wide, wide_f, ((288, 128), BF16), ((8, 128), F32)],
        [
            pltpu.VMEM((512, 512), BF16),
            pltpu.VMEM((512, 1536), BF16),
            pltpu.VMEM((512, 512), BF16),
            pltpu.VMEM((512, 512), BF16),
            pltpu.VMEM((4, 128, 128), F32),
            pltpu.VMEM((2, 256, 256), BF16),
            pltpu.VMEM((2, 256, 256), BF16),
            pltpu.VMEM((8, 1536), F32),
        ],
        "svvvvvvvvv",
    )(place, *sums, lifted, query, new, wo, w_proj)
    d_sums = around(d_sums)
    total_out = total(pair_sum(mine, theirs))
    mine, theirs, loss_part = call(
        backward_kernel,
        [((16, 4, 96, 128), BF16), ((16, 4, 96, 128), BF16), ((8, 128), F32)],
        [
            pltpu.VMEM((2, 256, 256), BF16),
            pltpu.VMEM((2, 256, 256), BF16),
            pltpu.VMEM((512, 1536), BF16),
            pltpu.VMEM((512, 512), BF16),
            pltpu.VMEM((512, 1536), BF16),
            pltpu.SemaphoreType.DMA,
        ],
        "svvvvvhvvvvvvvvvv",
    )(place, *d_sums, count, old, lifted, key, key_spread, value, value_spread, d_query, d_hidden, wq, wk, wv)
    total_in = total(pair_sum(mine, theirs))
    blocks = jnp.concatenate([total_in[0:48], total_out[0:48]], axis=0)
    loss_high = loss_part.astype(BF16)
    loss_low = (loss_part - loss_high.astype(F32)).astype(BF16)
    heads = jnp.concatenate([total_in[48:96], total_out[48:64]], axis=0).astype(BF16)
    heads = jnp.concatenate([heads, loss_high[0:1], loss_low[0:1], jnp.zeros((14, 128), BF16)], axis=0)
    heads = exchange(jnp.broadcast_to(heads[None], (32, 80, 128)), "slab")
    lift, g_query, g_key, g_value, g_out, proj, loss = call(
        last_kernel,
        [
            ((48, 512), F32),
            ((512, 128), F32),
            ((512, 128), F32),
            ((512, 128), F32),
            ((128, 512), F32),
            ((16, 1536), F32),
            ((1, 1), F32),
        ],
        (),
        "svvvvv",
    )(place, *around(blocks), heads)
    return (new_velocity, loss.reshape(()), lift, g_query, g_key, g_value, g_out, proj)


def solution(mesh):
    return jax.shard_map(
        step,
        mesh=mesh,
        in_specs=(
            P(None, "slab", "mp", None),
            P(None, "slab", "mp", None),
            P("slab", "mp", None, None),
            P(),
            P(None, "mp"),
            P(None, "mp"),
            P(None, "mp"),
            P("mp", None),
            P(),
        ),
        out_specs=(
            P(None, "slab", "mp", None),
            P(),
            P("slab", None),
            P(None, "mp"),
            P(None, "mp"),
            P(None, "mp"),
            P("mp", None),
            P("slab", None),
        ),
        check_vma=False,
    )
```
